128 devices in a mesh: snp: 8 (over z, y_lo), tile: 16 (over y_hi, x, core).
Axes of the slice: x: 4, y: 4 (y_hi: 2, y_lo: 2; y = y_hi * 2 + y_lo), z: 4, core: 2. Of those that a mesh axis runs over, the one named last changes fastest.
Arguments:
- dosages: float32 [32768, 16384], P('tile', 'snp'), may hold values from 0 to 2
- phenotypes: float32 [32768, 512], P('tile', 'snp'), may hold values from -6 to 6
Outputs:
- factor: float32 [32768, 512], P('tile')
- whitened: float32 [32768, 512], P('tile', 'snp')
The draws below stay inside these ranges and needn't reach their ends.
All inputs are finite; a program needn't handle non-finite values.
Results may differ from the reference program's by a relative error of at most 0.00011.
Values sent between devices are 32-bit elements; how exact they have to be, the bound alone decides.
No kernel may reach another device: no remote copies, remote signals or barrier semaphores. Data moves between devices by JAX's collectives and lax.ppermute only.
A program may use at most 128 MiB of HBM per device.

```python
import jax
import jax.numpy as jnp
from jax import lax

ROWS_DEV = 2048
BLK = 256
PHENO = 512
NSAMP = 32768
NSNP = 16384


def draw_dosages(key, part):
    base = jax.random.randint(jax.random.fold_in(key, 1), (1, NSNP), 5, 331)
    sample_ids = jnp.arange(NSAMP, dtype=jnp.int32)[:, None]
    threshold = base * (NSAMP + 2 * sample_ids) // NSAMP
    first_allele = jax.random.randint(jax.random.fold_in(key, 2), (NSAMP, NSNP), 0, 1000) < threshold
    second_allele = jax.random.randint(jax.random.fold_in(key, 3), (NSAMP, NSNP), 0, 1000) < threshold
    top = 0.3
    ramp = (NSAMP + 2 * sample_ids).astype(jnp.float32) / (3.0 * NSAMP)
    first_error = jax.random.uniform(jax.random.fold_in(key, 4), (NSAMP, NSNP), jnp.float32, 0.0, top) * ramp
    second_error = jax.random.uniform(jax.random.fold_in(key, 5), (NSAMP, NSNP), jnp.float32, 0.0, top) * ramp
    first_value = jnp.where(first_allele, 1.0 - first_error, first_error)
    second_value = jnp.where(second_allele, 1.0 - second_error, second_error)
    return (first_value + second_value).astype(jnp.float32)


def levels(stream_key, dims, split, least, largest):
    level, own = 1.0, jax.random.fold_in(stream_key, 6)
    for dim, blocks in split:
        steps = jnp.exp(jax.random.uniform(jax.random.fold_in(own, dim), (blocks,), jnp.float32, least / len(split), largest / len(split)))
        level = level * jnp.repeat(steps, dims[dim] // blocks).reshape([-1 if axis == dim else 1 for axis in range(len(dims))])
    return level


def scatter_about(rng, dims, deviation, most, pieces=(), kind=jnp.bfloat16):
    array = deviation * jax.random.normal(rng, dims, jnp.float32)
    if pieces:
        array = array * levels(rng, dims, pieces, -0.22, 0.18)
    return jnp.clip(array, -most, most).astype(kind)


def setup_inputs(seed: int = 0) -> dict:
    splits = jax.random.split(jax.random.key(seed), 3)
    return {
        "dosages": draw_dosages(jax.random.fold_in(splits[2], 71), 0),
        "phenotypes": scatter_about(splits[1], (NSAMP, PHENO), 1.0, 6.0, ((0, 16), (1, 8)), jnp.float32),
    }


def right_solve(lower, values):
    return lax.linalg.triangular_solve(lower, values, left_side=False, lower=True, transpose_a=True)

def left_solve(lower, values):
    return lax.linalg.triangular_solve(lower, values, left_side=True, lower=True)

def reference(dosages, phenotypes):
    n_rows = dosages.shape[0]
    n_snps = dosages.shape[1]
    counts = lax.optimization_barrier(jnp.sum(dosages, axis=0))
    allele_freq = counts / (2.0 * n_rows)
    spread = jnp.maximum(2.0 * allele_freq * (1.0 - allele_freq), 0.05)
    standard = (dosages - 2.0 * allele_freq) * lax.rsqrt(spread)
    stacked = jnp.concatenate([standard[:BLK], standard[ROWS_DEV:ROWS_DEV + BLK]], 0)
    cross = lax.dot_general(standard.astype(jnp.float32), stacked.astype(jnp.float32), (((1,), (1,)), ((), ())), precision=lax.Precision.HIGHEST, preferred_element_type=jnp.float32) * (1.0 / n_snps)
    diag = jnp.concatenate([cross[:BLK], cross[ROWS_DEV:ROWS_DEV + BLK]], 0) + jnp.eye(2 * BLK, dtype=jnp.float32)
    first_diag = jnp.linalg.cholesky(diag[:BLK, :BLK])
    lower_left = right_solve(first_diag, diag[BLK:, :BLK])
    schur = diag[BLK:, BLK:] - jnp.dot(lower_left, lower_left.T, precision=lax.Precision.HIGHEST)
    second_diag = jnp.linalg.cholesky(schur)
    left = right_solve(first_diag, cross[:, :BLK])
    rest = cross[:, BLK:] - jnp.dot(left, lower_left.T, precision=lax.Precision.HIGHEST)
    right = right_solve(second_diag, rest)
    left = left.at[:BLK].set(first_diag).at[ROWS_DEV:ROWS_DEV + BLK].set(lower_left)
    right = right.at[:BLK].set(jnp.zeros((BLK, BLK), jnp.float32)).at[ROWS_DEV:ROWS_DEV + BLK].set(second_diag)
    first_solved = left_solve(first_diag, phenotypes[:BLK])
    updated = phenotypes - jnp.dot(left, first_solved, precision=lax.Precision.HIGHEST)
    updated = updated.at[:BLK].set(first_solved)
    second_solved = left_solve(second_diag, updated[ROWS_DEV:ROWS_DEV + BLK])
    whitened = updated - jnp.dot(right, second_solved, precision=lax.Precision.HIGHEST)
    whitened = whitened.at[ROWS_DEV:ROWS_DEV + BLK].set(second_solved)
    return (jnp.concatenate([left, right], 1), whitened)
```

```python
import jax
import jax.numpy as jnp
from jax import lax
from jax.experimental import pallas as pl
from jax.experimental.pallas import tpu as pltpu
from jax.sharding import PartitionSpec as P

BLK = 256
HIGHEST = lax.Precision.HIGHEST
HIGH = lax.Precision.HIGH
F32 = jnp.float32

TILES = [(y, x, c) for y in range(2) for x in range(4) for c in range(2)]
SNPS = [(z, y) for z in range(4) for y in range(2)]


def tile_id(y, x, c):
    return (y * 4 + x) * 2 + c


def tile_send(value, target, only=None):
    pairs = [
        (tile_id(*a), tile_id(*target(*a))) for a in TILES if only is None or only(*a)
    ]
    return lax.ppermute(value, "tile", pairs)


SNP_FLIPS = (
    lambda z, y: (z ^ 1, y),
    lambda z, y: (3 - z, y),
    lambda z, y: (z, 1 - y),
)


def snp_exchange(value, dim):
    flip = SNP_FLIPS[dim]
    pairs = []
    for z, y in SNPS:
        z2, y2 = flip(z, y)
        pairs.append((z * 2 + y, z2 * 2 + y2))
    return lax.ppermute(value, "snp", pairs)


def snp_bits():
    index = lax.axis_index("snp")
    z, y = index // 2, index % 2
    return (jnp.where((z == 1) | (z == 2), 1, 0), jnp.where(z >= 2, 1, 0), y)


ORDERS = ((0, 1, 2), (1, 2, 0), (2, 0, 1))


def part_rows(rows):
    base = rows // 3 // 64 * 64
    sizes = [base, base, base]
    extra = rows - 3 * base
    for i in range(extra // 64):
        sizes[i] += 64
    return sizes


def cut(value, start, size):
    return lax.dynamic_slice_in_dim(value, start, size, 0)


def join(mine, other, bit):
    rows = mine.shape[0]
    return cut(jnp.concatenate([mine, other, mine], 0), bit * rows, 2 * rows)


def reduce_scatter_snp(value):
    bits = snp_bits()
    sizes = part_rows(value.shape[0])
    parts, at = [], 0
    for size in sizes:
        parts.append(value[at : at + size])
        at += size
    for stage in range(3):
        sent = []
        for part, order in zip(parts, ORDERS):
            half = part.shape[0] // 2
            sent.append(snp_exchange(cut(part, (1 - bits[order[stage]]) * half, half), order[stage]))
        kept = []
        for part, order, got in zip(parts, ORDERS, sent):
            half = part.shape[0] // 2
            kept.append(cut(part, bits[order[stage]] * half, half) + got)
        parts = kept
    return parts


def all_gather_snp(parts):
    bits = snp_bits()
    for stage in (2, 1, 0):
        got = [snp_exchange(p, order[stage]) for p, order in zip(parts, ORDERS)]
        parts = [join(p, g, bits[order[stage]]) for p, g, order in zip(parts, got, ORDERS)]
    return jnp.concatenate(parts, 0)


def sum_tiles(value):
    value = value + tile_send(value, lambda y, x, c: (y, x, 1 - c))
    value = value + tile_send(value, lambda y, x, c: (y, x ^ 1, c))
    value = value + tile_send(value, lambda y, x, c: (y, 3 - x, c))
    return value + tile_send(value, lambda y, x, c: (1 - y, x, c))


def place_ring(parts, first):
    rows = parts[0].shape[0]
    return cut(jnp.concatenate(parts + parts, 0), ((4 - first) % 4) * rows, 4 * rows)


def spread_panels(rows):
    tile = lax.axis_index("tile")
    x = (tile // 2) % 4
    core = tile % 2
    below = tile >= 8
    q = rows.shape[0] // 4
    h = q // 2
    p = [rows[i * q : (i + 1) * q] for i in range(4)]
    root = lambda y, xx, c: (y, xx) == (0, 0)
    to1 = tile_send(jnp.concatenate([p[1], p[2][:h]], 0), lambda y, xx, c: (0, 1, c), root)
    to3 = tile_send(jnp.concatenate([p[3], p[2][h:]], 0), lambda y, xx, c: (0, 3, c), root)
    f2a = tile_send(to1[q:], lambda y, xx, c: (0, 2, c), lambda y, xx, c: (y, xx) == (0, 1))
    f2b = tile_send(to3[q:], lambda y, xx, c: (0, 2, c), lambda y, xx, c: (y, xx) == (0, 3))
    own = jnp.where(
        x == 0,
        p[0],
        jnp.where(x == 1, to1[:q], jnp.where(x == 3, to3[:q], jnp.concatenate([f2a, f2b], 0))),
    )
    down = tile_send(own, lambda y, xx, c: (1, xx, c), lambda y, xx, c: y == 0)
    own = jnp.where(below, down, own)
    left = tile_send(own, lambda y, xx, c: (y, (xx + 1) % 4, c))
    right = tile_send(own, lambda y, xx, c: (y, (xx + 3) % 4, c))
    far_a = tile_send(left[:h], lambda y, xx, c: (y, (xx + 1) % 4, c))
    far_b = tile_send(right[h:], lambda y, xx, c: (y, (xx + 3) % 4, c))
    mine = place_ring([own, right, jnp.concatenate([far_a, far_b], 0), left], x)
    other = tile_send(mine, lambda y, xx, c: (y, xx, 1 - c))
    return join(mine, other, core)


def spread_small(value):
    tile = lax.axis_index("tile")
    x = (tile // 2) % 4
    other = tile_send(value, lambda y, xx, c: (y, xx, 1 - c))
    both = join(value, other, tile % 2)
    got = tile_send(both, lambda y, xx, c: (0, 1, c), lambda y, xx, c: (y, xx) == (0, 0))
    both = jnp.where(x == 1, got, both)
    got = tile_send(both, lambda y, xx, c: (0, 3 - xx, c), lambda y, xx, c: y == 0 and xx < 2)
    both = jnp.where(x >= 2, got, both)
    got = tile_send(both, lambda y, xx, c: (1, xx, c), lambda y, xx, c: y == 0)
    return jnp.where(tile >= 8, got, both)


def factor_leaf(work):
    sub = lax.broadcasted_iota(jnp.int32, (8, 128), 0)
    for j in range(0, 128, 8):
        halves = (work[j : j + 8, 0:128], work[j : j + 8, 128:256])
        s = {}
        for k in range(8):
            column = jnp.broadcast_to(halves[0][:, j + k : j + k + 1], (8, 128))
            for m in range(k, 8):
                s[m, k] = jnp.broadcast_to(column[m : m + 1, :], (8, 128))
        scale, low = [], {}
        for k in range(8):
            scale.append(lax.rsqrt(s[k, k]))
            for m in range(k + 1, 8):
                low[m, k] = s[m, k] * scale[k]
            for n in range(k + 1, 8):
                for m in range(n, 8):
                    s[m, n] = s[m, n] - low[m, k] * low[n, k]
        solved = []
        for half in halves:
            rows = []
            for m in range(8):
                row = jnp.broadcast_to(half[m : m + 1, :], (8, 128))
                for k in range(m):
                    row = row - low[m, k] * rows[k]
                rows.append(row * scale[m])
            block = rows[0]
            for m in range(1, 8):
                block = jnp.where(sub == m, rows[m], block)
            solved.append(block)
        both = jnp.concatenate(solved, 1)
        work[j : j + 8, :] = both
        if j < 120:
            update = lax.dot_general(
                solved[0], both, (((0,), (0,)), ((), ())), precision=HIGHEST, preferred_element_type=F32
            )
            work[j + 8 : 128, :] = work[j + 8 : 128, :] - update[j + 8 :, :]


def factor_kernel(diag_ref, lower_ref, inverse_ref, aug, work):
    n = diag_ref.shape[0]
    row = lax.broadcasted_iota(jnp.int32, (n, n), 0)
    col = lax.broadcasted_iota(jnp.int32, (n, n), 1)
    eye = jnp.where(row == col, 1.0, 0.0).astype(F32)
    aug[:, 0:n] = diag_ref[...] + eye
    aug[:, n : 2 * n] = eye
    small = lax.broadcasted_iota(jnp.int32, (128, 128), 0) == lax.broadcasted_iota(
        jnp.int32, (128, 128), 1
    )

    def step(b, carry):
        rows = pl.ds(pl.multiple_of(b * 128, 128), 128)
        work[:, 0:128] = aug[rows, rows]
        work[:, 128:256] = jnp.where(small, 1.0, 0.0).astype(F32)
        factor_leaf(work)
        solved = lax.dot_general(
            work[:, 128:256],
            aug[rows, :],
            (((1,), (0,)), ((), ())),
            precision=HIGHEST,
            preferred_element_type=F32,
        )
        aug[rows, :] = solved
        aug[rows, rows] = work[:, 0:128]

        def trail(q, carry):
            below = pl.ds(pl.multiple_of(q * 128, 128), 128)
            aug[below, :] = aug[below, :] - lax.dot_general(
                aug[rows, below],
                solved,
                (((0,), (0,)), ((), ())),
                precision=HIGHEST,
                preferred_element_type=F32,
            )
            return carry

        return lax.fori_loop(b + 1, n // 128, trail, carry)

    lax.fori_loop(0, n // 128, step, 0)
    lower_ref[...] = jnp.where(row >= col, jnp.transpose(aug[:, 0:n]), 0.0)
    inverse_ref[...] = aug[:, n : 2 * n]


def factor_panels(diag):
    n = diag.shape[0]
    vmem = pl.BlockSpec(memory_space=pltpu.VMEM)
    return pl.pallas_call(
        factor_kernel,
        out_shape=(jax.ShapeDtypeStruct((n, n), F32), jax.ShapeDtypeStruct((n, n), F32)),
        in_specs=[vmem],
        out_specs=(vmem, vmem),
        scratch_shapes=[pltpu.VMEM((n, 2 * n), F32), pltpu.VMEM((128, 256), F32)],
        compiler_params=pltpu.CompilerParams(vmem_limit_bytes=24 << 20),
        cost_estimate=pl.CostEstimate(flops=20_000_000_000, bytes_accessed=3 << 20, transcendentals=512),
        name="factor_panels",
    )(diag)


def dot_t(a, b, precision):
    return lax.dot_general(
        a, b, (((1,), (1,)), ((), ())), precision=precision, preferred_element_type=F32
    )


def sum_snp_square(value):
    index = lax.axis_index("snp")
    z = index // 2
    rows = value.shape[0] // 4

    def hop(v, k):
        return lax.ppermute(v, "snp", [(a * 2 + b, ((a + k) % 4) * 2 + b) for a, b in SNPS])

    total = cut(value, z * rows, rows)
    for k in (2, 1, 3):
        total = total + hop(cut(value, ((z + k) % 4) * rows, rows), k)
    total = total + snp_exchange(total, 2)
    back = [total] + [None] * 3
    for k in (2, 1, 3):
        back[(4 - k) % 4] = hop(total, k)
    return place_ring(back, z)


def body(dosages, phenotypes):
    n_tile = lax.axis_size("tile")
    n_snp = lax.axis_size("snp")
    rows, snps = dosages.shape
    width = BLK
    tile_index = lax.axis_index("tile")

    panels = spread_panels(dosages[:width])
    panel_pheno = spread_small(phenotypes[:width])
    counts = sum_tiles(jnp.sum(dosages, axis=0))
    allele_freq = counts / (2.0 * rows * n_tile)
    spread = jnp.maximum(2.0 * allele_freq * (1.0 - allele_freq), 0.05)
    mean = 2.0 * allele_freq
    weight = (1.0 / (snps * n_snp)) / spread
    centered = panels - mean
    weighted = centered * weight
    diag = sum_snp_square(dot_t(centered, weighted, HIGH))
    cross = dot_t(dosages - mean, weighted, HIGH)
    cross = all_gather_snp(reduce_scatter_snp(cross))

    lower, inverse = factor_panels(diag)
    factor = dot_t(cross, inverse, HIGH)
    head = jnp.where(
        tile_index == 0, lower[:width], jnp.where(tile_index == 1, lower[width:], factor[:width])
    )
    solved = jnp.dot(inverse, panel_pheno, precision=HIGHEST)
    whitened = phenotypes - jnp.dot(factor, solved, precision=HIGH)
    white_head = jnp.where(
        tile_index == 0, solved[:width], jnp.where(tile_index == 1, solved[width:], whitened[:width])
    )
    return (
        lax.dynamic_update_slice(factor, head, (0, 0)),
        lax.dynamic_update_slice(whitened, white_head, (0, 0)),
    )


def solution(mesh):
    placed = (P("tile", "snp"), P("tile", "snp"))
    return jax.shard_map(
        body,
        mesh=mesh,
        in_specs=placed,
        out_specs=(P("tile", None), P("tile", "snp")),
        check_vma=False,
    )
```

```python
import jax
import jax.numpy as jnp
from jax import lax
from jax.experimental import pallas as pl
from jax.experimental.pallas import tpu as pltpu
from jax.sharding import PartitionSpec as P

BLK = 256
HIGHEST = lax.Precision.HIGHEST
HIGH = lax.Precision.HIGH
F32 = jnp.float32

TILES = [(y, x, c) for y in range(2) for x in range(4) for c in range(2)]
SNPS = [(z, y) for z in range(4) for y in range(2)]


def tile_id(y, x, c):
    return (y * 4 + x) * 2 + c


def tile_send(value, target, only=None):
    pairs = [
        (tile_id(*a), tile_id(*target(*a))) for a in TILES if only is None or only(*a)
    ]
    return lax.ppermute(value, "tile", pairs)


SNP_FLIPS = (
    lambda z, y: (z ^ 1, y),
    lambda z, y: (3 - z, y),
    lambda z, y: (z, 1 - y),
)


def snp_exchange(value, dim):
    flip = SNP_FLIPS[dim]
    pairs = []
    for z, y in SNPS:
        z2, y2 = flip(z, y)
        pairs.append((z * 2 + y, z2 * 2 + y2))
    return lax.ppermute(value, "snp", pairs)


def snp_bits():
    index = lax.axis_index("snp")
    z, y = index // 2, index % 2
    return (jnp.where((z == 1) | (z == 2), 1, 0), jnp.where(z >= 2, 1, 0), y)


ORDERS = ((0, 1, 2), (1, 2, 0), (2, 0, 1))


def cut(value, start, size):
    return lax.dynamic_slice_in_dim(value, start, size, 0)


def join(mine, other, bit):
    rows = mine.shape[0]
    return cut(jnp.concatenate([mine, other, mine], 0), bit * rows, 2 * rows)


PART_ROWS = (768, 640, 640)


def reduce_scatter_snp(product):
    bits = snp_bits()
    at, starts = 0, []
    for size in PART_ROWS:
        starts.append(at)
        at += size
    got = []
    for start, size, order in zip(starts, PART_ROWS, ORDERS):
        half = size // 2
        sent = product(start + (1 - bits[order[0]]) * half, half)
        got.append(snp_exchange(sent, order[0]))
    parts = []
    for start, size, order, term in zip(starts, PART_ROWS, ORDERS, got):
        half = size // 2
        parts.append(product(start + bits[order[0]] * half, half) + term)
    for stage in (1, 2):
        got = []
        for part, order in zip(parts, ORDERS):
            half = part.shape[0] // 2
            got.append(snp_exchange(cut(part, (1 - bits[order[stage]]) * half, half), order[stage]))
        kept = []
        for part, order, term in zip(parts, ORDERS, got):
            half = part.shape[0] // 2
            kept.append(cut(part, bits[order[stage]] * half, half) + term)
        parts = kept
    return parts


def all_gather_snp(parts):
    bits = snp_bits()
    for stage in (2, 1, 0):
        got = [snp_exchange(p, order[stage]) for p, order in zip(parts, ORDERS)]
        parts = [join(p, g, bits[order[stage]]) for p, g, order in zip(parts, got, ORDERS)]
    return jnp.concatenate(parts, 0)


def sum_tiles(value):
    value = value + tile_send(value, lambda y, x, c: (y, x, 1 - c))
    value = value + tile_send(value, lambda y, x, c: (y, x ^ 1, c))
    return value + tile_send(value, lambda y, x, c: (y, 3 - x, c))


def swap_cores(value):
    return tile_send(value, lambda y, x, c: (y, x, 1 - c))


def place_ring(parts, first):
    rows = parts[0].shape[0]
    return cut(jnp.concatenate(parts + parts, 0), ((4 - first) % 4) * rows, 4 * rows)


def scatter_panels(rows):
    root = lambda y, x, c: (y, x) == (0, 0)
    to1 = tile_send(rows[64:160], lambda y, x, c: (0, 1, c), root)
    to3 = tile_send(rows[160:256], lambda y, x, c: (0, 3, c), root)
    return to1, to3


def own_piece(rows, to1, to3):
    tile = lax.axis_index("tile")
    x = (tile // 2) % 4
    far_a = tile_send(to1[64:], lambda y, x, c: (0, 2, c), lambda y, x, c: (y, x) == (0, 1))
    far_b = tile_send(to3[:32], lambda y, x, c: (0, 2, c), lambda y, x, c: (y, x) == (0, 3))
    own = jnp.where(
        x == 0,
        rows[:64],
        jnp.where(x == 1, to1[:64], jnp.where(x == 3, to3[32:], jnp.concatenate([far_a, far_b], 0))),
    )
    below = tile_send(own, lambda y, x, c: (1, x, c), lambda y, x, c: y == 0)
    return jnp.where(tile >= 8, below, own)


def gather_panels(own):
    ahead = lambda y, x, c: (y, (x + 1) % 4, c)
    back = lambda y, x, c: (y, (x + 3) % 4, c)
    left = tile_send(own, ahead)
    right = tile_send(own, back)
    own2 = swap_cores(own)
    far_a = tile_send(left[:32], ahead)
    far_b = tile_send(right[32:], back)
    left2 = swap_cores(left)
    right2 = swap_cores(right)
    far_a2 = swap_cores(far_a)
    far_b2 = swap_cores(far_b)
    return (own, right, far_a, far_b, left), (own2, right2, far_a2, far_b2, left2)


PIECES = ((0, 0, 64), (1, 0, 64), (2, 0, 32), (2, 32, 32), (3, 0, 64))


def standardize_kernel(where_ref, mean_ref, weight_ref, *refs):
    mine, other = refs[:5], refs[5:10]
    centered_ref, weighted_ref = refs[10], refs[11]
    x = where_ref[0]
    core = where_ref[1]
    mean = mean_ref[...]
    weight = weight_ref[...]
    for (turn, offset, rows), a_ref, b_ref in zip(PIECES, mine, other):
        at = ((x + turn) % 4) * 64 + offset
        centered = a_ref[...] - mean
        centered_ref[pl.ds(pl.multiple_of(at, 32), rows), :] = centered
        weighted_ref[pl.ds(pl.multiple_of(core * BLK + at, 32), rows), :] = centered * weight
        weighted_ref[pl.ds(pl.multiple_of((1 - core) * BLK + at, 32), rows), :] = (
            b_ref[...] - mean
        ) * weight


def standardize_panels(mine, other, mean, weight):
    n = mean.shape[0]
    tile = lax.axis_index("tile")
    where = jnp.stack([(tile // 2) % 4, tile % 2]).astype(jnp.int32)
    vmem = pl.BlockSpec(memory_space=pltpu.VMEM)
    return pl.pallas_call(
        standardize_kernel,
        out_shape=(jax.ShapeDtypeStruct((BLK, n), F32), jax.ShapeDtypeStruct((2 * BLK, n), F32)),
        in_specs=[pl.BlockSpec(memory_space=pltpu.SMEM)] + [vmem] * 12,
        out_specs=(vmem, vmem),
        compiler_params=pltpu.CompilerParams(vmem_limit_bytes=32 << 20),
        cost_estimate=pl.CostEstimate(flops=4_000_000, bytes_accessed=10 << 20, transcendentals=0),
        name="standardize_panels",
    )(where, mean.reshape(1, n), weight.reshape(1, n), *mine, *other)


def lane_columns(rows, j):
    return [jnp.broadcast_to(rows[:, j + k : j + k + 1], (8, 128)) for k in range(8)]


def factor_leaf(work):
    sub = lax.broadcasted_iota(jnp.int32, (8, 128), 0)
    current = [work[0:8, 0:128], work[0:8, 128:256]]
    for j in range(0, 128, 8):
        last = j == 120
        columns = lane_columns(current[0], j)
        s = {}
        for k in range(8):
            for m in range(k, 8):
                s[m, k] = jnp.broadcast_to(columns[k][m : m + 1, :], (8, 128))
        if not last:
            following = [work[j + 8 : j + 16, 0:128], work[j + 8 : j + 16, 128:256]]
            below = lane_columns(following[0], j)
        scale, low, coefs = [], {}, []
        rows = ([], [])
        for k in range(8):
            scale.append(lax.rsqrt(s[k, k]))
            for m in range(k + 1, 8):
                low[m, k] = s[m, k] * scale[k]
            for n in range(k + 1, 8):
                for m in range(n, 8):
                    s[m, n] = s[m, n] - low[m, k] * low[n, k]
            for h in range(2):
                row = jnp.broadcast_to(current[h][k : k + 1, :], (8, 128))
                for i in range(k):
                    row = row - low[k, i] * rows[h][i]
                rows[h].append(row * scale[k])
            if not last:
                coef = below[k]
                for i in range(k):
                    coef = coef - coefs[i] * low[k, i]
                coefs.append(coef * scale[k])
                for h in range(2):
                    following[h] = following[h] - coefs[k] * rows[h][k]
        solved = []
        for h in range(2):
            block = rows[h][0]
            for m in range(1, 8):
                block = jnp.where(sub == m, rows[h][m], block)
            solved.append(block)
        both = jnp.concatenate(solved, 1)
        work[j : j + 8, :] = both
        if j < 112:
            update = lax.dot_general(
                solved[0], both, (((0,), (0,)), ((), ())), precision=HIGHEST, preferred_element_type=F32
            )
            work[j + 16 : 128, :] = work[j + 16 : 128, :] - update[j + 16 :, :]
        if not last:
            current = following


def factor_step(b, first_ref, aug, work):
    n = aug.shape[0]
    rows = slice(b * 128, b * 128 + 128)
    if b == 0:
        eye = lax.broadcasted_iota(jnp.int32, (n, n), 0) == lax.broadcasted_iota(jnp.int32, (n, n), 1)
        eye = jnp.where(eye, 1.0, 0.0).astype(F32)
        aug[:, 0:n] = first_ref[...] + eye
        aug[:, n : 2 * n] = eye
    else:
        aug[...] = first_ref[...]
    small = lax.broadcasted_iota(jnp.int32, (128, 128), 0) == lax.broadcasted_iota(
        jnp.int32, (128, 128), 1
    )
    work[:, 0:128] = aug[rows, rows]
    work[:, 128:256] = jnp.where(small, 1.0, 0.0).astype(F32)
    factor_leaf(work)
    right = slice(b * 128, n + b * 128 + 128)
    solved = lax.dot_general(
        work[:, 128:256],
        aug[rows, right],
        (((1,), (0,)), ((), ())),
        precision=HIGHEST,
        preferred_element_type=F32,
    )
    aug[rows, right] = solved
    aug[rows, rows] = work[:, 0:128]
    if b < 3:
        below = slice(b * 128 + 128, n)
        aug[below, right] = aug[below, right] - lax.dot_general(
            solved[:, 128 : n - b * 128],
            solved,
            (((0,), (0,)), ((), ())),
            precision=HIGHEST,
            preferred_element_type=F32,
        )


def first_step_kernel(diag_ref, aug_ref, work):
    factor_step(0, diag_ref, aug_ref, work)


def last_step_kernel(in_ref, lower_ref, inverse_ref, aug, work):
    factor_step(3, in_ref, aug, work)
    n = aug.shape[0]
    row = lax.broadcasted_iota(jnp.int32, (n, n), 0)
    col = lax.broadcasted_iota(jnp.int32, (n, n), 1)
    lower_ref[...] = jnp.where(row >= col, jnp.transpose(aug[:, 0:n]), 0.0)
    inverse_ref[...] = aug[:, n : 2 * n]


def factor_panels(diag):
    n = diag.shape[0]
    vmem = pl.BlockSpec(memory_space=pltpu.VMEM)
    work = pltpu.VMEM((128, 256), F32)
    wide = jax.ShapeDtypeStruct((n, 2 * n), F32)
    square = jax.ShapeDtypeStruct((n, n), F32)
    common = dict(
        in_specs=[vmem],
        compiler_params=pltpu.CompilerParams(vmem_limit_bytes=16 << 20),
        cost_estimate=pl.CostEstimate(flops=6_000_000_000, bytes_accessed=3 << 20, transcendentals=512),
    )
    state = pl.pallas_call(
        first_step_kernel, out_shape=wide, out_specs=vmem, scratch_shapes=[work], name="factor_0", **common
    )(diag)
    for b in (1, 2):
        state = pl.pallas_call(
            lambda i, o, w, b=b: factor_step(b, i, o, w),
            out_shape=wide,
            out_specs=vmem,
            scratch_shapes=[work],
            name="factor_%d" % b,
            **common,
        )(state)
    return pl.pallas_call(
        last_step_kernel,
        out_shape=(square, square),
        out_specs=(vmem, vmem),
        scratch_shapes=[pltpu.VMEM((n, 2 * n), F32), work],
        name="factor_3",
        **common,
    )(state)


def dot_t(a, b, precision):
    return lax.dot_general(
        a, b, (((1,), (1,)), ((), ())), precision=precision, preferred_element_type=F32
    )


def sum_snp_square(value):
    index = lax.axis_index("snp")
    z = index // 2
    rows = value.shape[0] // 4

    def hop(v, k):
        return lax.ppermute(v, "snp", [(a * 2 + b, ((a + k) % 4) * 2 + b) for a, b in SNPS])

    total = cut(value, z * rows, rows)
    for k in (2, 1, 3):
        total = total + hop(cut(value, ((z + k) % 4) * rows, rows), k)
    total = total + snp_exchange(total, 2)
    back = [total] + [None] * 3
    for k in (2, 1, 3):
        back[(4 - k) % 4] = hop(total, k)
    return place_ring(back, z)


def body(dosages, phenotypes):
    n_tile = lax.axis_size("tile")
    n_snp = lax.axis_size("snp")
    rows, snps = dosages.shape
    width = BLK
    tile_index = lax.axis_index("tile")

    core = tile_index % 2
    head = dosages[:width]
    to1, to3 = scatter_panels(head)
    nothing = jnp.zeros_like(phenotypes[:width])
    pheno = jnp.concatenate(
        [
            jnp.where(tile_index == 0, phenotypes[:width], nothing),
            jnp.where(tile_index == 1, phenotypes[:width], nothing),
        ],
        1,
    )
    counts = jnp.sum(dosages, axis=0)
    small = sum_tiles(jnp.concatenate([counts.reshape(16, 128), pheno], 0))
    to1, to3, small = lax.optimization_barrier((to1, to3, small))
    small = small + tile_send(small, lambda y, x, c: (1 - y, x, c))
    mine, other = gather_panels(own_piece(head, to1, to3))

    counts = small[:16].reshape(snps)
    panel_pheno = jnp.concatenate([small[16:, :64], small[16:, 64:]], 0)
    allele_freq = counts / (2.0 * rows * n_tile)
    spread = jnp.maximum(2.0 * allele_freq * (1.0 - allele_freq), 0.05)
    mean = 2.0 * allele_freq
    weight = (1.0 / (snps * n_snp)) / spread
    centered, weighted = standardize_panels(mine, other, mean, weight)
    half = sum_snp_square(dot_t(centered, weighted, HIGH))
    diag = join(half, swap_cores(half), core)

    def product(start, size):
        return dot_t(cut(dosages, start, size) - mean, weighted, HIGH)

    cross = all_gather_snp(reduce_scatter_snp(product))

    lower, inverse = factor_panels(diag)
    factor = dot_t(cross, inverse, HIGHEST)
    head = jnp.where(
        tile_index == 0, lower[:width], jnp.where(tile_index == 1, lower[width:], factor[:width])
    )
    solved = jnp.dot(inverse, panel_pheno, precision=HIGHEST)
    whitened = phenotypes - jnp.dot(factor, solved, precision=HIGH)
    white_head = jnp.where(
        tile_index == 0, solved[:width], jnp.where(tile_index == 1, solved[width:], whitened[:width])
    )
    return (
        lax.dynamic_update_slice(factor, head, (0, 0)),
        lax.dynamic_update_slice(whitened, white_head, (0, 0)),
    )


def solution(mesh):
    placed = (P("tile", "snp"), P("tile", "snp"))
    return jax.shard_map(
        body,
        mesh=mesh,
        in_specs=placed,
        out_specs=(P("tile", None), P("tile", "snp")),
        check_vma=False,
    )
```

```python
import jax
import jax.numpy as jnp
from jax import lax
from jax.experimental import pallas as pl
from jax.experimental.pallas import tpu as pltpu
from jax.sharding import PartitionSpec as P

BLK = 256
HIGHEST = lax.Precision.HIGHEST
HIGH = lax.Precision.HIGH
F32 = jnp.float32

TILES = [(y, x, c) for y in range(2) for x in range(4) for c in range(2)]
SNPS = [(z, y) for z in range(4) for y in range(2)]


def tile_id(y, x, c):
    return (y * 4 + x) * 2 + c


def tile_send(value, target, only=None):
    pairs = [
        (tile_id(*a), tile_id(*target(*a))) for a in TILES if only is None or only(*a)
    ]
    return lax.ppermute(value, "tile", pairs)


SNP_FLIPS = (
    lambda z, y: (z ^ 1, y),
    lambda z, y: (3 - z, y),
    lambda z, y: (z, 1 - y),
)


def snp_exchange(value, dim):
    flip = SNP_FLIPS[dim]
    pairs = []
    for z, y in SNPS:
        z2, y2 = flip(z, y)
        pairs.append((z * 2 + y, z2 * 2 + y2))
    return lax.ppermute(value, "snp", pairs)


def snp_bits():
    index = lax.axis_index("snp")
    z, y = index // 2, index % 2
    return (jnp.where((z == 1) | (z == 2), 1, 0), jnp.where(z >= 2, 1, 0), y)


ORDERS = ((0, 1, 2), (1, 2, 0), (2, 0, 1))


def cut(value, start, size):
    return lax.dynamic_slice_in_dim(value, start, size, 0)


def join(mine, other, bit):
    rows = mine.shape[0]
    return cut(jnp.concatenate([mine, other, mine], 0), bit * rows, 2 * rows)


PART_ROWS = (768, 640, 640)


def halves(parts, stage, bits):
    sent, kept = [], []
    for part, order in zip(parts, ORDERS):
        half = part.shape[0] // 2
        sent.append(cut(part, (1 - bits[order[stage]]) * half, half))
        kept.append(cut(part, bits[order[stage]] * half, half))
    return sent, kept


def exchange_all(values, stage):
    return [snp_exchange(v, order[stage]) for v, order in zip(values, ORDERS)]


def after(value, *others):
    return lax.optimization_barrier((value, *others))[0]


def sum_and_factor(product, diag):
    bits = snp_bits()
    at, starts = 0, []
    for size in PART_ROWS:
        starts.append(at)
        at += size
    got = []
    for start, size, order in zip(starts, PART_ROWS, ORDERS):
        half = size // 2
        term = snp_exchange(diag, order[0])
        sent = product(start + (1 - bits[order[0]]) * half, half)
        sent, term = tie(sent, term)
        diag = diag + term
        got.append(snp_exchange(sent, order[0]))
    state = factor_block(0, gather_diag(diag))
    parts = []
    for start, size, order, term in zip(starts, PART_ROWS, ORDERS, got):
        half = size // 2
        parts.append(product(start + bits[order[0]] * half, half) + term)

    sent, kept = halves(parts, 1, bits)
    got = exchange_all(sent, 1)
    state = factor_block(1, after(state, *sent))
    parts = [k + g for k, g in zip(kept, got)]

    sent, kept = halves(parts, 2, bits)
    got = exchange_all(sent, 2)
    state = factor_block(2, after(state, *sent))
    parts = [k + g for k, g in zip(kept, got)]

    got = exchange_all(parts, 2)
    lower, inverse = factor_block(3, after(state, *parts))
    parts = [join(p, g, bits[order[2]]) for p, g, order in zip(parts, got, ORDERS)]
    got = exchange_all(parts, 1)
    parts = [join(p, g, bits[order[1]]) for p, g, order in zip(parts, got, ORDERS)]
    parts = [dot_t(part, inverse, HIGHEST) for part in parts]
    got = exchange_all(parts, 0)
    pieces = []
    for start, size, order, part, other in zip(starts, PART_ROWS, ORDERS, parts, got):
        half = size // 2
        bit = bits[order[0]]
        pieces.append((start + bit * half, part))
        pieces.append((start + (1 - bit) * half, other))
    return lower, inverse, pieces


def gather_diag(rows):
    tile = lax.axis_index("tile")
    x = (tile // 2) % 4
    other = tile_send(rows, lambda y, xx, c: (y, xx ^ 1, c))
    rows = join(rows, other, x % 2)
    other = tile_send(rows, lambda y, xx, c: (y, 3 - xx, c))
    rows = join(rows, other, x // 2)
    return join(rows, swap_cores(rows), tile % 2)


def swap_cores(value):
    return tile_send(value, lambda y, x, c: (y, x, 1 - c))


def tie(*values):
    return lax.optimization_barrier(values)


def spread_panels(head, small):
    tile = lax.axis_index("tile")
    x = (tile // 2) % 4
    below = tile >= 8
    p = [head[i * 32 : (i + 1) * 32] for i in range(8)]
    at = lambda row, col: lambda y, xx, c: (y, xx) == (row, col)
    to = lambda row, col: lambda y, xx, c: (row, col, c)
    ahead = lambda y, xx, c: (y, (xx + 1) % 4, c)
    back = lambda y, xx, c: (y, (xx + 3) % 4, c)
    root = at(0, 0)

    far_a = tile_send(p[4], to(0, 1), root)
    far_b = tile_send(p[5], to(0, 3), root)
    far_a, far_b, p2, p6 = tie(far_a, far_b, p[2], p[6])
    near_a = tile_send(p2, to(0, 1), root)
    back_a = tile_send(p6, to(0, 3), root)
    far_a = tile_send(far_a, to(0, 2), at(0, 1))
    far_b = tile_send(far_b, to(0, 2), at(0, 3))
    small = small + swap_cores(small)
    near_a, back_a, far_a, p3, p7, small = tie(near_a, back_a, far_a, p[3], p[7], small)
    near_b = tile_send(p3, to(0, 1), root)
    back_b = tile_send(p7, to(0, 3), root)
    own_a = jnp.where(x == 0, p[0], jnp.where(x == 1, near_a, jnp.where(x == 3, back_a, far_a)))
    down = tile_send(own_a, lambda y, xx, c: (1, xx, c), lambda y, xx, c: y == 0)
    own_a = jnp.where(below, down, own_a)
    small = small + tile_send(small, lambda y, xx, c: (1 - y, xx, c))
    own_a, near_b, back_b, far_b, small = tie(own_a, near_b, back_b, far_b, small)
    own_b = jnp.where(x == 0, p[1], jnp.where(x == 1, near_b, jnp.where(x == 3, back_b, far_b)))
    down = tile_send(own_b, lambda y, xx, c: (1, xx, c), lambda y, xx, c: y == 0)
    left_a = tile_send(own_a, ahead)
    right_a = tile_send(own_a, back)
    own_b = jnp.where(below, down, own_b)
    other_own_a = swap_cores(own_a)
    own_b, left_a, right_a = tie(own_b, left_a, right_a)
    left_b = tile_send(own_b, ahead)
    right_b = tile_send(own_b, back)
    far_a = tile_send(left_a, ahead)
    small = small + tile_send(small, lambda y, xx, c: (y, xx ^ 1, c))
    others = [swap_cores(own_b), swap_cores(left_a), swap_cores(right_a)]
    left_b, right_b, small = tie(left_b, right_b, small)
    far_b = tile_send(right_b, back)
    small = small + tile_send(small, lambda y, xx, c: (y, 3 - xx, c))
    others += [swap_cores(left_b), swap_cores(right_b), swap_cores(far_a), swap_cores(far_b)]
    mine = (own_a, own_b, left_a, right_a, left_b, right_b, far_a, far_b)
    other = (other_own_a, *others)
    return mine, other, small


PIECES = ((0, 0), (0, 32), (3, 0), (1, 0), (3, 32), (1, 32), (2, 0), (2, 32))


def standardize_kernel(where_ref, mean_ref, weight_ref, *refs):
    mine, other = refs[:8], refs[8:16]
    centered_ref, weighted_ref = refs[16], refs[17]
    x = where_ref[0]
    core = where_ref[1]
    mean = mean_ref[...]
    weight = weight_ref[...]
    for i, (turn, offset) in enumerate(PIECES):
        at = ((x + turn) % 4) * 64 + offset
        centered = mine[i][...] - mean
        if turn == 0:
            centered_ref[offset : offset + 32, :] = centered
        weighted_ref[pl.ds(pl.multiple_of(core * BLK + at, 32), 32), :] = centered * weight
        weighted_ref[pl.ds(pl.multiple_of((1 - core) * BLK + at, 32), 32), :] = (
            other[i][...] - mean
        ) * weight


def standardize_panels(mine, other, mean, weight):
    n = mean.shape[0]
    tile = lax.axis_index("tile")
    where = jnp.stack([(tile // 2) % 4, tile % 2]).astype(jnp.int32)
    vmem = pl.BlockSpec(memory_space=pltpu.VMEM)
    return pl.pallas_call(
        standardize_kernel,
        out_shape=(jax.ShapeDtypeStruct((64, n), F32), jax.ShapeDtypeStruct((2 * BLK, n), F32)),
        in_specs=[pl.BlockSpec(memory_space=pltpu.SMEM)] + [vmem] * 18,
        out_specs=(vmem, vmem),
        compiler_params=pltpu.CompilerParams(vmem_limit_bytes=32 << 20),
        cost_estimate=pl.CostEstimate(flops=4_000_000, bytes_accessed=10 << 20, transcendentals=0),
        name="standardize_panels",
    )(where, mean.reshape(1, n), weight.reshape(1, n), *mine, *other)


def lane_columns(rows, j):
    return [jnp.broadcast_to(rows[:, j + k : j + k + 1], (8, 128)) for k in range(8)]


def factor_leaf(work):
    sub = lax.broadcasted_iota(jnp.int32, (8, 128), 0)
    current = [work[0:8, 0:128], work[0:8, 128:256]]
    for j in range(0, 128, 8):
        last = j == 120
        columns = lane_columns(current[0], j)
        s = {}
        for k in range(8):
            for m in range(k, 8):
                s[m, k] = jnp.broadcast_to(columns[k][m : m + 1, :], (8, 128))
        if not last:
            following = [work[j + 8 : j + 16, 0:128], work[j + 8 : j + 16, 128:256]]
            below = lane_columns(following[0], j)
        scale, low, coefs = [], {}, []
        rows = ([], [])
        for k in range(8):
            scale.append(lax.rsqrt(s[k, k]))
            for m in range(k + 1, 8):
                low[m, k] = s[m, k] * scale[k]
            for n in range(k + 1, 8):
                for m in range(n, 8):
                    s[m, n] = s[m, n] - low[m, k] * low[n, k]
            for h in range(2):
                row = jnp.broadcast_to(current[h][k : k + 1, :], (8, 128))
                for i in range(k):
                    row = row - low[k, i] * rows[h][i]
                rows[h].append(row * scale[k])
            if not last:
                coef = below[k]
                for i in range(k):
                    coef = coef - coefs[i] * low[k, i]
                coefs.append(coef * scale[k])
                for h in range(2):
                    following[h] = following[h] - coefs[k] * rows[h][k]
        solved = []
        for h in range(2):
            block = rows[h][0]
            for m in range(1, 8):
                block = jnp.where(sub == m, rows[h][m], block)
            solved.append(block)
        both = jnp.concatenate(solved, 1)
        work[j : j + 8, :] = both
        if j < 112:
            update = lax.dot_general(
                solved[0], both, (((0,), (0,)), ((), ())), precision=HIGHEST, preferred_element_type=F32
            )
            work[j + 16 : 128, :] = work[j + 16 : 128, :] - update[j + 16 :, :]
        if not last:
            current = following


def factor_step(b, first_ref, aug, work):
    n = aug.shape[0]
    rows = slice(b * 128, b * 128 + 128)
    if b == 0:
        eye = lax.broadcasted_iota(jnp.int32, (n, n), 0) == lax.broadcasted_iota(jnp.int32, (n, n), 1)
        eye = jnp.where(eye, 1.0, 0.0).astype(F32)
        aug[:, 0:n] = first_ref[...] + eye
        aug[:, n : 2 * n] = eye
    else:
        aug[...] = first_ref[...]
    small = lax.broadcasted_iota(jnp.int32, (128, 128), 0) == lax.broadcasted_iota(
        jnp.int32, (128, 128), 1
    )
    work[:, 0:128] = aug[rows, rows]
    work[:, 128:256] = jnp.where(small, 1.0, 0.0).astype(F32)
    factor_leaf(work)
    right = slice(b * 128, n + b * 128 + 128)
    solved = lax.dot_general(
        work[:, 128:256],
        aug[rows, right],
        (((1,), (0,)), ((), ())),
        precision=HIGHEST,
        preferred_element_type=F32,
    )
    aug[rows, right] = solved
    aug[rows, rows] = work[:, 0:128]
    if b < 3:
        below = slice(b * 128 + 128, n)
        aug[below, right] = aug[below, right] - lax.dot_general(
            solved[:, 128 : n - b * 128],
            solved,
            (((0,), (0,)), ((), ())),
            precision=HIGHEST,
            preferred_element_type=F32,
        )


def last_step_kernel(in_ref, lower_ref, inverse_ref, aug, work):
    factor_step(3, in_ref, aug, work)
    n = aug.shape[0]
    row = lax.broadcasted_iota(jnp.int32, (n, n), 0)
    col = lax.broadcasted_iota(jnp.int32, (n, n), 1)
    lower_ref[...] = jnp.where(row >= col, jnp.transpose(aug[:, 0:n]), 0.0)
    inverse_ref[...] = aug[:, n : 2 * n]


def factor_block(b, value):
    n = value.shape[0]
    vmem = pl.BlockSpec(memory_space=pltpu.VMEM)
    work = pltpu.VMEM((128, 256), F32)
    square = jax.ShapeDtypeStruct((n, n), F32)
    if b == 3:
        body, shape, specs = last_step_kernel, (square, square), (vmem, vmem)
        scratch = [pltpu.VMEM((n, 2 * n), F32), work]
    else:
        body = lambda i, o, w: factor_step(b, i, o, w)
        shape, specs, scratch = jax.ShapeDtypeStruct((n, 2 * n), F32), vmem, [work]
    return pl.pallas_call(
        body,
        out_shape=shape,
        in_specs=[vmem],
        out_specs=specs,
        scratch_shapes=scratch,
        compiler_params=pltpu.CompilerParams(vmem_limit_bytes=16 << 20),
        cost_estimate=pl.CostEstimate(flops=6_000_000_000, bytes_accessed=3 << 20, transcendentals=512),
        name="factor_%d" % b,
    )(value)


def dot_t(a, b, precision):
    return lax.dot_general(
        a, b, (((1,), (1,)), ((), ())), precision=precision, preferred_element_type=F32
    )


def split(value):
    high = value.astype(jnp.bfloat16)
    return high, (value - high.astype(F32)).astype(jnp.bfloat16)


def output_kernel(where_ref, *refs):
    n_pieces = len(refs) - 8
    pieces = refs[:n_pieces]
    lower_ref, solved_ref, pheno_ref, factor_ref, white_ref, product, sems, head_sem = refs[n_pieces:]
    tile = where_ref[n_pieces]
    copies = []
    for i, piece in enumerate(pieces):
        rows = piece.shape[0]
        at = pl.multiple_of(where_ref[i], 64)
        copy = pltpu.make_async_copy(piece, factor_ref.at[pl.ds(at, rows), :], sems.at[i])
        copy.start()
        copies.append(copy)
    solved_high, solved_low = split(solved_ref[...])
    for i, piece in enumerate(pieces):
        rows = piece.shape[0]
        at = pl.multiple_of(where_ref[i], 64)
        high, low = split(piece[...])
        total = jnp.dot(high, solved_high, preferred_element_type=F32)
        total = total + jnp.dot(high, solved_low, preferred_element_type=F32)
        product[pl.ds(at, rows), :] = total + jnp.dot(low, solved_high, preferred_element_type=F32)
    white_ref[...] = pheno_ref[...] - jnp.transpose(product[...])
    for copy in copies:
        copy.wait()
    for panel in range(2):

        @pl.when(tile == panel)
        def _():
            own = slice(panel * BLK, panel * BLK + BLK)
            head = pltpu.make_async_copy(lower_ref.at[own, :], factor_ref.at[0:BLK, :], head_sem)
            head.start()
            white_ref[:, 0:BLK] = jnp.transpose(solved_ref[own, :])
            head.wait()


def write_outputs(pieces, lower, solved, pheno):
    n_pheno, rows = pheno.shape
    where = jnp.stack([at for at, _ in pieces] + [lax.axis_index("tile")]).astype(jnp.int32)
    vmem = pl.BlockSpec(memory_space=pltpu.VMEM)
    return pl.pallas_call(
        output_kernel,
        out_shape=(
            jax.ShapeDtypeStruct((rows, 2 * BLK), F32),
            jax.ShapeDtypeStruct((n_pheno, rows), F32),
        ),
        in_specs=[pl.BlockSpec(memory_space=pltpu.SMEM)] + [vmem] * (len(pieces) + 3),
        out_specs=(pl.BlockSpec(memory_space=pl.ANY), vmem),
        scratch_shapes=[
            pltpu.VMEM((rows, n_pheno), F32),
            pltpu.SemaphoreType.DMA((len(pieces),)),
            pltpu.SemaphoreType.DMA,
        ],
        compiler_params=pltpu.CompilerParams(vmem_limit_bytes=32 << 20),
        cost_estimate=pl.CostEstimate(flops=500_000_000, bytes_accessed=10 << 20, transcendentals=0),
        name="write_outputs",
    )(where, *[p for _, p in pieces], lower, solved, pheno)


def body(dosages, phenotypes):
    n_tile = lax.axis_size("tile")
    n_snp = lax.axis_size("snp")
    rows, snps = dosages.shape
    width = BLK
    tile_index = lax.axis_index("tile")

    nothing = jnp.zeros_like(phenotypes[:width])
    pheno = jnp.concatenate(
        [
            jnp.where(tile_index == 0, phenotypes[:width], nothing),
            jnp.where(tile_index == 1, phenotypes[:width], nothing),
        ],
        1,
    )
    counts = jnp.sum(dosages, axis=0)
    small = jnp.concatenate([counts.reshape(16, 128), pheno], 0)
    mine, other, small = spread_panels(dosages[:width], small)

    counts = small[:16].reshape(snps)
    panel_pheno = jnp.concatenate([small[16:, :64], small[16:, 64:]], 0)
    allele_freq = counts / (2.0 * rows * n_tile)
    spread = jnp.maximum(2.0 * allele_freq * (1.0 - allele_freq), 0.05)
    mean = 2.0 * allele_freq
    weight = (1.0 / (snps * n_snp)) / spread
    centered, weighted = standardize_panels(mine, other, mean, weight)

    def product(start, size):
        return dot_t(cut(dosages, start, size) - mean, weighted, HIGH)

    lower, inverse, pieces = sum_and_factor(product, dot_t(centered, weighted, HIGH))
    solved = jnp.dot(inverse, panel_pheno, precision=HIGHEST)
    factor, whitened = write_outputs(pieces, lower, solved, phenotypes.T)
    return factor, whitened.T


def solution(mesh):
    placed = (P("tile", "snp"), P("tile", "snp"))
    return jax.shard_map(
        body,
        mesh=mesh,
        in_specs=placed,
        out_specs=(P("tile", None), P("tile", "snp")),
        check_vma=False,
    )
```

```python
import jax
import jax.numpy as jnp
from jax import lax
from jax.experimental import pallas as pl
from jax.experimental.pallas import tpu as pltpu
from jax.sharding import PartitionSpec as P

BLK = 256
HIGHEST = lax.Precision.HIGHEST
F32 = jnp.float32

TILES = [(y, x, c) for y in range(2) for x in range(4) for c in range(2)]
SNPS = [(z, y) for z in range(4) for y in range(2)]


def tile_id(y, x, c):
    return (y * 4 + x) * 2 + c


def tile_send(value, target, only=None):
    pairs = [
        (tile_id(*a), tile_id(*target(*a))) for a in TILES if only is None or only(*a)
    ]
    return lax.ppermute(value, "tile", pairs)


SNP_FLIPS = (
    lambda z, y: (z ^ 1, y),
    lambda z, y: (3 - z, y),
    lambda z, y: (z, 1 - y),
)


def snp_exchange(value, dim):
    flip = SNP_FLIPS[dim]
    pairs = []
    for z, y in SNPS:
        z2, y2 = flip(z, y)
        pairs.append((z * 2 + y, z2 * 2 + y2))
    return lax.ppermute(value, "snp", pairs)


def snp_bits():
    index = lax.axis_index("snp")
    z, y = index // 2, index % 2
    return (jnp.where((z == 1) | (z == 2), 1, 0), jnp.where(z >= 2, 1, 0), y)


ORDERS = ((0, 1, 2), (1, 2, 0), (2, 0, 1))


def cut(value, start, size):
    return lax.dynamic_slice_in_dim(value, start, size, 0)


def join(mine, other, bit):
    rows = mine.shape[0]
    return cut(jnp.concatenate([mine, other, mine], 0), bit * rows, 2 * rows)


PART_ROWS = (768, 640, 640)


def halves(parts, stage, bits):
    sent, kept = [], []
    for part, order in zip(parts, ORDERS):
        half = part.shape[0] // 2
        sent.append(cut(part, (1 - bits[order[stage]]) * half, half))
        kept.append(cut(part, bits[order[stage]] * half, half))
    return sent, kept


def exchange_all(values, stage):
    return [snp_exchange(v, order[stage]) for v, order in zip(values, ORDERS)]


def sum_and_factor(product, diag, pheno):
    bits = snp_bits()
    at, starts = 0, []
    for size in PART_ROWS:
        starts.append(at)
        at += size
    sent, kept = [], []
    for start, size, order in zip(starts, PART_ROWS, ORDERS):
        half = size // 2
        sent.append(product(start + (1 - bits[order[0]]) * half, half))
        kept.append(product(start + bits[order[0]] * half, half))
    for dim in range(3):
        term, sent[dim] = tie(snp_exchange(diag, dim), sent[dim])
        diag = diag + term
    diag, pheno, kept = gather_small(diag, pheno, kept)
    diag, *sent = tie(diag, *sent)
    got = exchange_all(sent, 0)
    state = factor_block(1, factor_block(0, diag))
    parts = [k + g for k, g in zip(kept, got)]

    sent, kept = halves(parts, 1, bits)
    state, *sent = tie(state, *sent)
    got = exchange_all(sent, 1)
    state = factor_block(2, state)
    parts = [k + g for k, g in zip(kept, got)]

    sent, kept = halves(parts, 2, bits)
    state, *sent = tie(state, *sent)
    got = exchange_all(sent, 2)
    lower, inverse = factor_block(3, state)
    parts = [dot_t(k + g, inverse, HIGHEST) for k, g in zip(kept, got)]

    for stage in (2, 1):
        got = exchange_all(parts, stage)
        parts = [join(p, g, bits[order[stage]]) for p, g, order in zip(parts, got, ORDERS)]
    got = exchange_all(parts, 0)
    pieces = []
    for start, size, order, part, other in zip(starts, PART_ROWS, ORDERS, parts, got):
        half = size // 2
        bit = bits[order[0]]
        pieces.append((start + bit * half, part))
        pieces.append((start + (1 - bit) * half, other))
    return lower, inverse, pheno, pieces


def gather_small(diag, pheno, beside):
    beside = list(beside)
    tile = lax.axis_index("tile")
    x = (tile // 2) % 4
    pheno = jnp.where(tile < 2, pheno, jnp.zeros_like(pheno))
    pheno = pheno + tile_send(pheno, lambda y, xx, c: (1 - y, xx, c))
    rows = diag.shape[0]
    for i, (bit, flip) in enumerate(
        (
            (x % 2, lambda y, xx, c: (y, xx ^ 1, c)),
            (x // 2, lambda y, xx, c: (y, 3 - xx, c)),
        )
    ):
        other = tile_send(jnp.concatenate([diag, pheno], 0), flip)
        other, beside[i] = tie(other, beside[i])
        diag = join(diag, other[:rows], bit)
        pheno = pheno + other[rows:]
        rows = 2 * rows
    other = swap_cores(jnp.concatenate([diag, pheno], 0))
    other, beside[2] = tie(other, beside[2])
    core = tile % 2
    return join(diag, other[:rows], core), join(pheno, other[rows:], core), beside


def swap_cores(value):
    return tile_send(value, lambda y, x, c: (y, x, 1 - c))


def tie(*values):
    return lax.optimization_barrier(values)


def spread_panels(head, counts):
    tile = lax.axis_index("tile")
    x = (tile // 2) % 4
    below = tile >= 8
    p = [head[i * 32 : (i + 1) * 32] for i in range(8)]
    at = lambda row, col: lambda y, xx, c: (y, xx) == (row, col)
    to = lambda row, col: lambda y, xx, c: (row, col, c)
    ahead = lambda y, xx, c: (y, (xx + 1) % 4, c)
    back = lambda y, xx, c: (y, (xx + 3) % 4, c)
    root = at(0, 0)

    def go_down(own):
        down = tile_send(own, lambda y, xx, c: (1, xx, c), lambda y, xx, c: y == 0)
        return jnp.where(below, down, own)

    far_a = tile_send(p[4], to(0, 1), root)
    far_b = tile_send(p[5], to(0, 3), root)
    near = tile_send(head[64:128], to(0, 1), root)
    behind = tile_send(head[192:256], to(0, 3), root)
    far_a, far_b, counts = tie(far_a, far_b, counts)
    far_a = tile_send(far_a, to(0, 2), at(0, 1))
    far_b = tile_send(far_b, to(0, 2), at(0, 3))
    counts = counts + swap_cores(counts)
    counts = counts + tile_send(counts, lambda y, xx, c: (1 - y, xx, c))
    near, behind, counts = tie(near, behind, counts)
    own_a = jnp.where(x == 0, p[0], jnp.where(x == 1, near[:32], jnp.where(x == 3, behind[:32], far_a)))
    own_b = jnp.where(x == 0, p[1], jnp.where(x == 1, near[32:], jnp.where(x == 3, behind[32:], far_b)))
    own_a = go_down(own_a)
    counts = counts + tile_send(counts, lambda y, xx, c: (y, xx ^ 1, c))
    counts = counts + tile_send(counts, lambda y, xx, c: (y, 3 - xx, c))
    own_b = go_down(own_b)
    own_a, counts = tie(own_a, counts)
    left_a = tile_send(own_a, ahead)
    right_a = tile_send(own_a, back)
    left_b = tile_send(own_b, ahead)
    right_b = tile_send(own_b, back)
    far_a = tile_send(left_a, ahead)
    far_b = tile_send(right_b, back)
    mine = (own_a, own_b, left_a, right_a, left_b, right_b, far_a, far_b)
    return mine, tuple(swap_cores(piece) for piece in mine), counts


PIECES = ((0, 0), (0, 32), (3, 0), (1, 0), (3, 32), (1, 32), (2, 0), (2, 32))


def split(value):
    high = value.astype(jnp.bfloat16)
    return high, (value - high.astype(F32)).astype(jnp.bfloat16)


NT = (((1,), (1,)), ((), ()))


def dot3(a, b):
    total = lax.dot_general(a[0], b[0], NT, preferred_element_type=F32)
    total = total + lax.dot_general(a[0], b[1], NT, preferred_element_type=F32)
    return total + lax.dot_general(a[1], b[0], NT, preferred_element_type=F32)


def standardize_kernel(where_ref, mean_ref, weight_ref, *refs):
    mine, other = refs[:8], refs[8:16]
    diag_ref, panels_ref, own = refs[16:]
    x = where_ref[0]
    core = where_ref[1]
    mean = mean_ref[...]
    weight = weight_ref[...]
    for i, (turn, offset) in enumerate(PIECES):
        at = ((x + turn) % 4) * 64 + offset
        centered = mine[i][...] - mean
        if turn == 0:
            own[offset : offset + 32, :] = centered
        for panel, value in ((core, centered), (1 - core, other[i][...] - mean)):
            high, low = split(value * weight)
            row = pl.multiple_of(panel * BLK + at, 32)
            panels_ref[pl.ds(row, 32), :] = high
            panels_ref[pl.ds(row + 2 * BLK, 32), :] = low
    diag_ref[...] = dot3(split(own[...]), (panels_ref[: 2 * BLK, :], panels_ref[2 * BLK :, :]))


def standardize_panels(mine, other, mean, weight):
    n = mean.shape[0]
    tile = lax.axis_index("tile")
    where = jnp.stack([(tile // 2) % 4, tile % 2]).astype(jnp.int32)
    vmem = pl.BlockSpec(memory_space=pltpu.VMEM)
    return pl.pallas_call(
        standardize_kernel,
        out_shape=(
            jax.ShapeDtypeStruct((64, 2 * BLK), F32),
            jax.ShapeDtypeStruct((4 * BLK, n), jnp.bfloat16),
        ),
        in_specs=[pl.BlockSpec(memory_space=pltpu.SMEM)] + [vmem] * 18,
        out_specs=(vmem, vmem),
        scratch_shapes=[pltpu.VMEM((64, n), F32)],
        compiler_params=pltpu.CompilerParams(vmem_limit_bytes=24 << 20),
        cost_estimate=pl.CostEstimate(flops=1000, bytes_accessed=1000, transcendentals=0),
        name="standardize_panels",
    )(where, mean.reshape(1, n), weight.reshape(1, n), *mine, *other)


CHUNK = 512


def cross_kernel(start_ref, dosages_ref, mean_ref, panels_ref, out_ref, rows_ref, sems):
    rows, n = rows_ref.shape
    first = pl.multiple_of(start_ref[0], 64)

    def fetch(k):
        columns = pl.ds(pl.multiple_of(k * CHUNK, CHUNK), CHUNK)
        return pltpu.make_async_copy(
            dosages_ref.at[pl.ds(first, rows), columns], rows_ref.at[:, columns], sems.at[k]
        )

    for k in range(n // CHUNK):
        fetch(k).start()
    out_ref[...] = jnp.zeros_like(out_ref)

    def step(k, carry):
        fetch(k).wait()
        columns = pl.ds(pl.multiple_of(k * CHUNK, CHUNK), CHUNK)
        a = split(rows_ref[:, columns] - mean_ref[:, columns])
        out_ref[...] += dot3(a, (panels_ref[: 2 * BLK, columns], panels_ref[2 * BLK :, columns]))
        return carry

    lax.fori_loop(0, n // CHUNK, step, 0)


def cross_rows(start, rows, dosages, mean, panels):
    n = mean.shape[0]
    vmem = pl.BlockSpec(memory_space=pltpu.VMEM)
    return pl.pallas_call(
        cross_kernel,
        out_shape=jax.ShapeDtypeStruct((rows, 2 * BLK), F32),
        in_specs=[pl.BlockSpec(memory_space=pltpu.SMEM), pl.BlockSpec(memory_space=pltpu.HBM), vmem, vmem],
        out_specs=vmem,
        scratch_shapes=[pltpu.VMEM((rows, n), F32), pltpu.SemaphoreType.DMA((n // CHUNK,))],
        compiler_params=pltpu.CompilerParams(vmem_limit_bytes=44 << 20),
        cost_estimate=pl.CostEstimate(flops=3_000_000_000, bytes_accessed=1000, transcendentals=0),
        name="cross_rows",
    )(jnp.reshape(start, (1,)).astype(jnp.int32), dosages, mean.reshape(1, n), panels)


def lane_columns(rows, j):
    return [jnp.broadcast_to(rows[:, j + k : j + k + 1], (8, 128)) for k in range(8)]


def factor_leaf(work):
    sub = lax.broadcasted_iota(jnp.int32, (8, 128), 0)
    current = [work[0:8, 0:128], work[0:8, 128:256]]
    for j in range(0, 128, 8):
        last = j == 120
        columns = lane_columns(current[0], j)
        s = {}
        for k in range(8):
            for m in range(k, 8):
                s[m, k] = jnp.broadcast_to(columns[k][m : m + 1, :], (8, 128))
        if not last:
            following = [work[j + 8 : j + 16, 0:128], work[j + 8 : j + 16, 128:256]]
            below = lane_columns(following[0], j)
        scale, low, coefs = [], {}, []
        rows = ([], [])
        for k in range(8):
            scale.append(lax.rsqrt(s[k, k]))
            for m in range(k + 1, 8):
                low[m, k] = s[m, k] * scale[k]
            for n in range(k + 1, 8):
                for m in range(n, 8):
                    s[m, n] = s[m, n] - low[m, k] * low[n, k]
            for h in range(2):
                row = jnp.broadcast_to(current[h][k : k + 1, :], (8, 128))
                for i in range(k):
                    row = row - low[k, i] * rows[h][i]
                rows[h].append(row * scale[k])
            if not last:
                coef = below[k]
                for i in range(k):
                    coef = coef - coefs[i] * low[k, i]
                coefs.append(coef * scale[k])
                for h in range(2):
                    following[h] = following[h] - coefs[k] * rows[h][k]
        solved = []
        for h in range(2):
            block = rows[h][0]
            for m in range(1, 8):
                block = jnp.where(sub == m, rows[h][m], block)
            solved.append(block)
        both = jnp.concatenate(solved, 1)
        work[j : j + 8, :] = both
        if j < 112:
            update = lax.dot_general(
                solved[0], both, (((0,), (0,)), ((), ())), precision=HIGHEST, preferred_element_type=F32
            )
            work[j + 16 : 128, :] = work[j + 16 : 128, :] - update[j + 16 :, :]
        if not last:
            current = following


def factor_step(b, first_ref, aug, work):
    n = aug.shape[0]
    rows = slice(b * 128, b * 128 + 128)
    if b == 0:
        eye = lax.broadcasted_iota(jnp.int32, (n, n), 0) == lax.broadcasted_iota(jnp.int32, (n, n), 1)
        eye = jnp.where(eye, 1.0, 0.0).astype(F32)
        aug[:, 0:n] = first_ref[...] + eye
        aug[:, n : 2 * n] = eye
    else:
        aug[...] = first_ref[...]
    small = lax.broadcasted_iota(jnp.int32, (128, 128), 0) == lax.broadcasted_iota(
        jnp.int32, (128, 128), 1
    )
    work[:, 0:128] = aug[rows, rows]
    work[:, 128:256] = jnp.where(small, 1.0, 0.0).astype(F32)
    factor_leaf(work)
    right = slice(b * 128, n + b * 128 + 128)
    solved = lax.dot_general(
        work[:, 128:256],
        aug[rows, right],
        (((1,), (0,)), ((), ())),
        precision=HIGHEST,
        preferred_element_type=F32,
    )
    aug[rows, right] = solved
    aug[rows, rows] = work[:, 0:128]
    if b < 3:
        below = slice(b * 128 + 128, n)
        aug[below, right] = aug[below, right] - lax.dot_general(
            solved[:, 128 : n - b * 128],
            solved,
            (((0,), (0,)), ((), ())),
            precision=HIGHEST,
            preferred_element_type=F32,
        )


def last_step_kernel(in_ref, lower_ref, inverse_ref, aug, work):
    factor_step(3, in_ref, aug, work)
    n = aug.shape[0]
    row = lax.broadcasted_iota(jnp.int32, (n, n), 0)
    col = lax.broadcasted_iota(jnp.int32, (n, n), 1)
    lower_ref[...] = jnp.where(row >= col, jnp.transpose(aug[:, 0:n]), 0.0)
    inverse_ref[...] = aug[:, n : 2 * n]


def factor_block(b, value):
    n = value.shape[0]
    vmem = pl.BlockSpec(memory_space=pltpu.VMEM)
    work = pltpu.VMEM((128, 256), F32)
    square = jax.ShapeDtypeStruct((n, n), F32)
    if b == 3:
        body, shape, specs = last_step_kernel, (square, square), (vmem, vmem)
        scratch = [pltpu.VMEM((n, 2 * n), F32), work]
    else:
        body = lambda i, o, w: factor_step(b, i, o, w)
        shape, specs, scratch = jax.ShapeDtypeStruct((n, 2 * n), F32), vmem, [work]
    return pl.pallas_call(
        body,
        out_shape=shape,
        in_specs=[vmem],
        out_specs=specs,
        scratch_shapes=scratch,
        compiler_params=pltpu.CompilerParams(vmem_limit_bytes=16 << 20),
        cost_estimate=pl.CostEstimate(flops=1_000_000_000, bytes_accessed=3 << 10, transcendentals=512),
        name="factor_%d" % b,
    )(value)


def dot_t(a, b, precision):
    return lax.dot_general(
        a, b, (((1,), (1,)), ((), ())), precision=precision, preferred_element_type=F32
    )


def output_kernel(where_ref, *refs):
    n_pieces = len(refs) - 8
    pieces = refs[:n_pieces]
    lower_ref, solved_ref, pheno_ref, factor_ref, white_ref, product, sems, head_sem = refs[n_pieces:]
    tile = where_ref[n_pieces]
    copies = []
    for i, piece in enumerate(pieces):
        rows = piece.shape[0]
        at = pl.multiple_of(where_ref[i], 64)
        copy = pltpu.make_async_copy(piece, factor_ref.at[pl.ds(at, rows), :], sems.at[i])
        copy.start()
        copies.append(copy)
    solved_high, solved_low = split(solved_ref[...])
    for i, piece in enumerate(pieces):
        rows = piece.shape[0]
        at = pl.multiple_of(where_ref[i], 64)
        high, low = split(piece[...])
        total = jnp.dot(high, solved_high, preferred_element_type=F32)
        total = total + jnp.dot(high, solved_low, preferred_element_type=F32)
        product[pl.ds(at, rows), :] = total + jnp.dot(low, solved_high, preferred_element_type=F32)
    white_ref[...] = pheno_ref[...] - jnp.transpose(product[...])
    for copy in copies:
        copy.wait()
    for panel in range(2):

        @pl.when(tile == panel)
        def _():
            own = slice(panel * BLK, panel * BLK + BLK)
            head = pltpu.make_async_copy(lower_ref.at[own, :], factor_ref.at[0:BLK, :], head_sem)
            head.start()
            white_ref[:, 0:BLK] = jnp.transpose(solved_ref[own, :])
            head.wait()


def write_outputs(pieces, lower, solved, pheno):
    n_pheno, rows = pheno.shape
    where = jnp.stack([at for at, _ in pieces] + [lax.axis_index("tile")]).astype(jnp.int32)
    vmem = pl.BlockSpec(memory_space=pltpu.VMEM)
    return pl.pallas_call(
        output_kernel,
        out_shape=(
            jax.ShapeDtypeStruct((rows, 2 * BLK), F32),
            jax.ShapeDtypeStruct((n_pheno, rows), F32),
        ),
        in_specs=[pl.BlockSpec(memory_space=pltpu.SMEM)] + [vmem] * (len(pieces) + 3),
        out_specs=(pl.BlockSpec(memory_space=pl.ANY), vmem),
        scratch_shapes=[
            pltpu.VMEM((rows, n_pheno), F32),
            pltpu.SemaphoreType.DMA((len(pieces),)),
            pltpu.SemaphoreType.DMA,
        ],
        compiler_params=pltpu.CompilerParams(vmem_limit_bytes=32 << 20),
        cost_estimate=pl.CostEstimate(flops=500_000_000, bytes_accessed=10 << 20, transcendentals=0),
        name="write_outputs",
    )(where, *[p for _, p in pieces], lower, solved, pheno)


def body(dosages, phenotypes):
    n_tile = lax.axis_size("tile")
    n_snp = lax.axis_size("snp")
    rows, snps = dosages.shape
    width = BLK
    tile_index = lax.axis_index("tile")

    counts = jnp.sum(dosages, axis=0)
    mine, other, counts = spread_panels(dosages[:width], counts.reshape(16, 128))
    flipped = phenotypes.T
    head = flipped[:, :width]
    head = jnp.concatenate([head[:32], head[32:]], 1)

    counts = counts.reshape(snps)
    allele_freq = counts / (2.0 * rows * n_tile)
    spread = jnp.maximum(2.0 * allele_freq * (1.0 - allele_freq), 0.05)
    mean = 2.0 * allele_freq
    weight = (1.0 / (snps * n_snp)) / spread
    diag, split_panels = standardize_panels(mine, other, mean, weight)

    def product(start, size):
        return cross_rows(start, size, dosages, mean, split_panels)

    lower, inverse, heads, pieces = sum_and_factor(product, diag, head)
    panel_pheno = jnp.concatenate(
        [
            jnp.concatenate([heads[:32, :width], heads[32:, :width]], 1),
            jnp.concatenate([heads[:32, width:], heads[32:, width:]], 1),
        ],
        0,
    )
    solved = dot_t(inverse, panel_pheno, HIGHEST)
    factor, whitened = write_outputs(pieces, lower, solved, flipped)
    return factor, whitened.T


def solution(mesh):
    placed = (P("tile", "snp"), P("tile", "snp"))
    return jax.shard_map(
        body,
        mesh=mesh,
        in_specs=placed,
        out_specs=(P("tile", None), P("tile", "snp")),
        check_vma=False,
    )
```

```python
import jax
import jax.numpy as jnp
from jax import lax
from jax.experimental import pallas as pl
from jax.experimental.pallas import tpu as pltpu
from jax.sharding import PartitionSpec as P

BLK = 256
HIGHEST = lax.Precision.HIGHEST
HIGH = lax.Precision.HIGH
F32 = jnp.float32

TILES = [(y, x, c) for y in range(2) for x in range(4) for c in range(2)]
SNPS = [(z, y) for z in range(4) for y in range(2)]


def tile_id(y, x, c):
    return (y * 4 + x) * 2 + c


def tile_send(value, target, only=None):
    pairs = [
        (tile_id(*a), tile_id(*target(*a))) for a in TILES if only is None or only(*a)
    ]
    return lax.ppermute(value, "tile", pairs)


SNP_FLIPS = (
    lambda z, y: (z ^ 1, y),
    lambda z, y: (3 - z, y),
    lambda z, y: (z, 1 - y),
)


def snp_exchange(value, dim):
    flip = SNP_FLIPS[dim]
    pairs = []
    for z, y in SNPS:
        z2, y2 = flip(z, y)
        pairs.append((z * 2 + y, z2 * 2 + y2))
    return lax.ppermute(value, "snp", pairs)


def snp_bits():
    index = lax.axis_index("snp")
    z, y = index // 2, index % 2
    return (jnp.where((z == 1) | (z == 2), 1, 0), jnp.where(z >= 2, 1, 0), y)


ORDERS = ((0, 1, 2), (1, 2, 0), (2, 0, 1))


def cut(value, start, size):
    return lax.dynamic_slice_in_dim(value, start, size, 0)


def join(mine, other, bit):
    rows = mine.shape[0]
    return cut(jnp.concatenate([mine, other, mine], 0), bit * rows, 2 * rows)


PART_ROWS = (768, 640, 640)


def halves(parts, stage, bits):
    sent, kept = [], []
    for part, order in zip(parts, ORDERS):
        half = part.shape[0] // 2
        sent.append(cut(part, (1 - bits[order[stage]]) * half, half))
        kept.append(cut(part, bits[order[stage]] * half, half))
    return sent, kept


def exchange_all(values, stage):
    return [snp_exchange(v, order[stage]) for v, order in zip(values, ORDERS)]


def sum_and_factor(product, diag, pheno):
    bits = snp_bits()
    at, starts, parts = 0, [], []
    for dim, size in enumerate(PART_ROWS):
        term, part = tie(snp_exchange(diag, dim), product(at, size))
        diag = diag + term
        starts.append(at)
        parts.append(part)
        at += size

    sent, kept = halves(parts, 0, bits)
    got = exchange_all(sent, 0)
    diag, pheno = gather_small(diag, pheno)
    state = factor_block(0, diag)
    parts = [k + g for k, g in zip(kept, got)]
    for stage in (1, 2):
        sent, kept = halves(parts, stage, bits)
        state, *sent = tie(state, *sent)
        got = exchange_all(sent, stage)
        state = factor_block(stage, state)
        parts = [k + g for k, g in zip(kept, got)]

    state, *parts = tie(state, *parts)
    got = exchange_all(parts, 2)
    lower, inverse = factor_block(3, state)
    parts = [join(p, g, bits[order[2]]) for p, g, order in zip(parts, got, ORDERS)]
    parts = [dot_t(part, inverse, HIGHEST) for part in parts]
    got = exchange_all(parts, 1)
    parts = [join(p, g, bits[order[1]]) for p, g, order in zip(parts, got, ORDERS)]
    got = exchange_all(parts, 0)
    pieces = []
    for start, size, order, part, other in zip(starts, PART_ROWS, ORDERS, parts, got):
        half = size // 2
        bit = bits[order[0]]
        pieces.append((start + bit * half, part))
        pieces.append((start + (1 - bit) * half, other))
    return lower, inverse, pheno, pieces


def gather_small(diag, pheno):
    tile = lax.axis_index("tile")
    x = (tile // 2) % 4
    pheno = jnp.where(tile < 2, pheno, jnp.zeros_like(pheno))
    pheno = pheno + tile_send(pheno, lambda y, xx, c: (1 - y, xx, c))
    rows = diag.shape[0]
    for bit, flip in (
        (x % 2, lambda y, xx, c: (y, xx ^ 1, c)),
        (x // 2, lambda y, xx, c: (y, 3 - xx, c)),
    ):
        other = tile_send(jnp.concatenate([diag, pheno], 0), flip)
        diag = join(diag, other[:rows], bit)
        pheno = pheno + other[rows:]
        rows = 2 * rows
    other = swap_cores(jnp.concatenate([diag, pheno], 0))
    core = tile % 2
    return join(diag, other[:rows], core), join(pheno, other[rows:], core)


def swap_cores(value):
    return tile_send(value, lambda y, x, c: (y, x, 1 - c))


def tie(*values):
    return lax.optimization_barrier(values)


def spread_panels(head, counts):
    tile = lax.axis_index("tile")
    x = (tile // 2) % 4
    below = tile >= 8
    p = [head[i * 32 : (i + 1) * 32] for i in range(8)]
    at = lambda row, col: lambda y, xx, c: (y, xx) == (row, col)
    to = lambda row, col: lambda y, xx, c: (row, col, c)
    ahead = lambda y, xx, c: (y, (xx + 1) % 4, c)
    back = lambda y, xx, c: (y, (xx + 3) % 4, c)
    root = at(0, 0)

    def go_down(own):
        down = tile_send(own, lambda y, xx, c: (1, xx, c), lambda y, xx, c: y == 0)
        return jnp.where(below, down, own)

    far_a = tile_send(p[4], to(0, 1), root)
    far_b = tile_send(p[5], to(0, 3), root)
    near = tile_send(head[64:128], to(0, 1), root)
    behind = tile_send(head[192:256], to(0, 3), root)
    far_a, far_b, counts = tie(far_a, far_b, counts)
    far_a = tile_send(far_a, to(0, 2), at(0, 1))
    far_b = tile_send(far_b, to(0, 2), at(0, 3))
    counts = counts + swap_cores(counts)
    counts = counts + tile_send(counts, lambda y, xx, c: (1 - y, xx, c))
    near, behind, counts = tie(near, behind, counts)
    own_a = jnp.where(x == 0, p[0], jnp.where(x == 1, near[:32], jnp.where(x == 3, behind[:32], far_a)))
    own_b = jnp.where(x == 0, p[1], jnp.where(x == 1, near[32:], jnp.where(x == 3, behind[32:], far_b)))
    own_a = go_down(own_a)
    counts = counts + tile_send(counts, lambda y, xx, c: (y, xx ^ 1, c))
    counts = counts + tile_send(counts, lambda y, xx, c: (y, 3 - xx, c))
    own_b = go_down(own_b)
    own_a, counts = tie(own_a, counts)
    left_a = tile_send(own_a, ahead)
    right_a = tile_send(own_a, back)
    left_b = tile_send(own_b, ahead)
    right_b = tile_send(own_b, back)
    far_a = tile_send(left_a, ahead)
    far_b = tile_send(right_b, back)
    mine = (own_a, own_b, left_a, right_a, left_b, right_b, far_a, far_b)
    return mine, tuple(swap_cores(piece) for piece in mine), counts


PIECES = ((0, 0), (0, 32), (3, 0), (1, 0), (3, 32), (1, 32), (2, 0), (2, 32))


def split(value):
    high = value.astype(jnp.bfloat16)
    return high, (value - high.astype(F32)).astype(jnp.bfloat16)


NT = (((1,), (1,)), ((), ()))


def dot3(a, b):
    total = lax.dot_general(a[0], b[0], NT, preferred_element_type=F32)
    total = total + lax.dot_general(a[0], b[1], NT, preferred_element_type=F32)
    return total + lax.dot_general(a[1], b[0], NT, preferred_element_type=F32)


def standardize_kernel(where_ref, mean_ref, weight_ref, *refs):
    mine, other = refs[:8], refs[8:16]
    diag_ref, panels_ref, own = refs[16:]
    x = where_ref[0]
    core = where_ref[1]
    mean = mean_ref[...]
    weight = weight_ref[...]
    for i, (turn, offset) in enumerate(PIECES):
        at = ((x + turn) % 4) * 64 + offset
        centered = mine[i][...] - mean
        if turn == 0:
            own[offset : offset + 32, :] = centered
        for panel, value in ((core, centered), (1 - core, other[i][...] - mean)):
            panels_ref[pl.ds(pl.multiple_of(panel * BLK + at, 32), 32), :] = value * weight
    diag_ref[...] = dot3(split(own[...]), split(panels_ref[...]))


def standardize_panels(mine, other, mean, weight):
    n = mean.shape[0]
    tile = lax.axis_index("tile")
    where = jnp.stack([(tile // 2) % 4, tile % 2]).astype(jnp.int32)
    vmem = pl.BlockSpec(memory_space=pltpu.VMEM)
    return pl.pallas_call(
        standardize_kernel,
        out_shape=(
            jax.ShapeDtypeStruct((64, 2 * BLK), F32),
            jax.ShapeDtypeStruct((2 * BLK, n), F32),
        ),
        in_specs=[pl.BlockSpec(memory_space=pltpu.SMEM)] + [vmem] * 18,
        out_specs=(vmem, vmem),
        scratch_shapes=[pltpu.VMEM((64, n), F32)],
        compiler_params=pltpu.CompilerParams(vmem_limit_bytes=16 << 20),
        cost_estimate=pl.CostEstimate(flops=1000, bytes_accessed=1000, transcendentals=0),
        name="standardize_panels",
    )(where, mean.reshape(1, n), weight.reshape(1, n), *mine, *other)


def lane_columns(rows, j):
    return [jnp.broadcast_to(rows[:, j + k : j + k + 1], (8, 128)) for k in range(8)]


def factor_leaf(work):
    sub = lax.broadcasted_iota(jnp.int32, (8, 128), 0)
    current = [work[0:8, 0:128], work[0:8, 128:256]]
    for j in range(0, 128, 8):
        last = j == 120
        columns = lane_columns(current[0], j)
        s = {}
        for k in range(8):
            for m in range(k, 8):
                s[m, k] = jnp.broadcast_to(columns[k][m : m + 1, :], (8, 128))
        if not last:
            following = [work[j + 8 : j + 16, 0:128], work[j + 8 : j + 16, 128:256]]
            below = lane_columns(following[0], j)
        scale, low, coefs = [], {}, []
        rows = ([], [])
        for k in range(8):
            scale.append(lax.rsqrt(s[k, k]))
            for m in range(k + 1, 8):
                low[m, k] = s[m, k] * scale[k]
            for n in range(k + 1, 8):
                for m in range(n, 8):
                    s[m, n] = s[m, n] - low[m, k] * low[n, k]
            for h in range(2):
                row = jnp.broadcast_to(current[h][k : k + 1, :], (8, 128))
                for i in range(k):
                    row = row - low[k, i] * rows[h][i]
                rows[h].append(row * scale[k])
            if not last:
                coef = below[k]
                for i in range(k):
                    coef = coef - coefs[i] * low[k, i]
                coefs.append(coef * scale[k])
                for h in range(2):
                    following[h] = following[h] - coefs[k] * rows[h][k]
        solved = []
        for h in range(2):
            block = rows[h][0]
            for m in range(1, 8):
                block = jnp.where(sub == m, rows[h][m], block)
            solved.append(block)
        both = jnp.concatenate(solved, 1)
        work[j : j + 8, :] = both
        if j < 112:
            update = lax.dot_general(
                solved[0], both, (((0,), (0,)), ((), ())), precision=HIGHEST, preferred_element_type=F32
            )
            work[j + 16 : 128, :] = work[j + 16 : 128, :] - update[j + 16 :, :]
        if not last:
            current = following


def factor_step(b, first_ref, aug, work):
    n = aug.shape[0]
    rows = slice(b * 128, b * 128 + 128)
    if b == 0:
        eye = lax.broadcasted_iota(jnp.int32, (n, n), 0) == lax.broadcasted_iota(jnp.int32, (n, n), 1)
        eye = jnp.where(eye, 1.0, 0.0).astype(F32)
        aug[:, 0:n] = first_ref[...] + eye
        aug[:, n : 2 * n] = eye
    else:
        aug[...] = first_ref[...]
    small = lax.broadcasted_iota(jnp.int32, (128, 128), 0) == lax.broadcasted_iota(
        jnp.int32, (128, 128), 1
    )
    work[:, 0:128] = aug[rows, rows]
    work[:, 128:256] = jnp.where(small, 1.0, 0.0).astype(F32)
    factor_leaf(work)
    right = slice(b * 128, n + b * 128 + 128)
    solved = lax.dot_general(
        work[:, 128:256],
        aug[rows, right],
        (((1,), (0,)), ((), ())),
        precision=HIGHEST,
        preferred_element_type=F32,
    )
    aug[rows, right] = solved
    aug[rows, rows] = work[:, 0:128]
    if b < 3:
        below = slice(b * 128 + 128, n)
        aug[below, right] = aug[below, right] - lax.dot_general(
            solved[:, 128 : n - b * 128],
            solved,
            (((0,), (0,)), ((), ())),
            precision=HIGHEST,
            preferred_element_type=F32,
        )


def last_step_kernel(in_ref, lower_ref, inverse_ref, aug, work):
    factor_step(3, in_ref, aug, work)
    n = aug.shape[0]
    row = lax.broadcasted_iota(jnp.int32, (n, n), 0)
    col = lax.broadcasted_iota(jnp.int32, (n, n), 1)
    lower_ref[...] = jnp.where(row >= col, jnp.transpose(aug[:, 0:n]), 0.0)
    inverse_ref[...] = aug[:, n : 2 * n]


def factor_block(b, value):
    n = value.shape[0]
    vmem = pl.BlockSpec(memory_space=pltpu.VMEM)
    work = pltpu.VMEM((128, 256), F32)
    square = jax.ShapeDtypeStruct((n, n), F32)
    if b == 3:
        body, shape, specs = last_step_kernel, (square, square), (vmem, vmem)
        scratch = [pltpu.VMEM((n, 2 * n), F32), work]
    else:
        body = lambda i, o, w: factor_step(b, i, o, w)
        shape, specs, scratch = jax.ShapeDtypeStruct((n, 2 * n), F32), vmem, [work]
    return pl.pallas_call(
        body,
        out_shape=shape,
        in_specs=[vmem],
        out_specs=specs,
        scratch_shapes=scratch,
        compiler_params=pltpu.CompilerParams(vmem_limit_bytes=16 << 20),
        cost_estimate=pl.CostEstimate(flops=1000, bytes_accessed=1000, transcendentals=0),
        name="factor_%d" % b,
    )(value)


def dot_t(a, b, precision):
    return lax.dot_general(
        a, b, (((1,), (1,)), ((), ())), precision=precision, preferred_element_type=F32
    )


def output_kernel(where_ref, *refs):
    n_pieces = len(refs) - 8
    pieces = refs[:n_pieces]
    lower_ref, solved_ref, pheno_ref, factor_ref, white_ref, product, sems, head_sem = refs[n_pieces:]
    tile = where_ref[n_pieces]
    copies = []
    for i, piece in enumerate(pieces):
        rows = piece.shape[0]
        at = pl.multiple_of(where_ref[i], 64)
        copy = pltpu.make_async_copy(piece, factor_ref.at[pl.ds(at, rows), :], sems.at[i])
        copy.start()
        copies.append(copy)
    solved_high, solved_low = split(solved_ref[...])
    for i, piece in enumerate(pieces):
        rows = piece.shape[0]
        at = pl.multiple_of(where_ref[i], 64)
        high, low = split(piece[...])
        total = jnp.dot(high, solved_high, preferred_element_type=F32)
        total = total + jnp.dot(high, solved_low, preferred_element_type=F32)
        product[pl.ds(at, rows), :] = total + jnp.dot(low, solved_high, preferred_element_type=F32)
    white_ref[...] = pheno_ref[...] - jnp.transpose(product[...])
    for copy in copies:
        copy.wait()
    for panel in range(2):

        @pl.when(tile == panel)
        def _():
            own = slice(panel * BLK, panel * BLK + BLK)
            head = pltpu.make_async_copy(lower_ref.at[own, :], factor_ref.at[0:BLK, :], head_sem)
            head.start()
            white_ref[:, 0:BLK] = jnp.transpose(solved_ref[own, :])
            head.wait()


def write_outputs(pieces, lower, solved, pheno):
    n_pheno, rows = pheno.shape
    where = jnp.stack([at for at, _ in pieces] + [lax.axis_index("tile")]).astype(jnp.int32)
    vmem = pl.BlockSpec(memory_space=pltpu.VMEM)
    return pl.pallas_call(
        output_kernel,
        out_shape=(
            jax.ShapeDtypeStruct((rows, 2 * BLK), F32),
            jax.ShapeDtypeStruct((n_pheno, rows), F32),
        ),
        in_specs=[pl.BlockSpec(memory_space=pltpu.SMEM)] + [vmem] * (len(pieces) + 3),
        out_specs=(pl.BlockSpec(memory_space=pl.ANY), vmem),
        scratch_shapes=[
            pltpu.VMEM((rows, n_pheno), F32),
            pltpu.SemaphoreType.DMA((len(pieces),)),
            pltpu.SemaphoreType.DMA,
        ],
        compiler_params=pltpu.CompilerParams(vmem_limit_bytes=32 << 20),
        cost_estimate=pl.CostEstimate(flops=500_000_000, bytes_accessed=10 << 20, transcendentals=0),
        name="write_outputs",
    )(where, *[p for _, p in pieces], lower, solved, pheno)


def body(dosages, phenotypes):
    n_tile = lax.axis_size("tile")
    n_snp = lax.axis_size("snp")
    rows, snps = dosages.shape
    width = BLK
    tile_index = lax.axis_index("tile")

    counts = jnp.sum(dosages, axis=0)
    mine, other, counts = spread_panels(dosages[:width], counts.reshape(16, 128))
    flipped = phenotypes.T
    head = flipped[:, :width]
    head = jnp.concatenate([head[:32], head[32:]], 1)

    counts = counts.reshape(snps)
    allele_freq = counts / (2.0 * rows * n_tile)
    spread = jnp.maximum(2.0 * allele_freq * (1.0 - allele_freq), 0.05)
    mean = 2.0 * allele_freq
    weight = (1.0 / (snps * n_snp)) / spread
    diag, panels = standardize_panels(mine, other, mean, weight)

    def product(start, size):
        return dot_t(dosages[start : start + size] - mean, panels, HIGH)

    lower, inverse, heads, pieces = sum_and_factor(product, diag, head)
    panel_pheno = jnp.concatenate(
        [
            jnp.concatenate([heads[:32, :width], heads[32:, :width]], 1),
            jnp.concatenate([heads[:32, width:], heads[32:, width:]], 1),
        ],
        0,
    )
    solved = dot_t(inverse, panel_pheno, HIGHEST)
    factor, whitened = write_outputs(pieces, lower, solved, flipped)
    return factor, whitened.T


def solution(mesh):
    placed = (P("tile", "snp"), P("tile", "snp"))
    return jax.shard_map(
        body,
        mesh=mesh,
        in_specs=placed,
        out_specs=(P("tile", None), P("tile", "snp")),
        check_vma=False,
    )
```

```python
import jax
import jax.numpy as jnp
from jax import lax
from jax.experimental import pallas as pl
from jax.experimental.pallas import tpu as pltpu
from jax.sharding import PartitionSpec as P

BLK = 256
HIGHEST = lax.Precision.HIGHEST
HIGH = lax.Precision.HIGH
F32 = jnp.float32

TILES = [(y, x, c) for y in range(2) for x in range(4) for c in range(2)]
SNPS = [(z, y) for z in range(4) for y in range(2)]


def tile_id(y, x, c):
    return (y * 4 + x) * 2 + c


def tile_send(value, target, only=None):
    pairs = [
        (tile_id(*a), tile_id(*target(*a))) for a in TILES if only is None or only(*a)
    ]
    return lax.ppermute(value, "tile", pairs)


SNP_FLIPS = (
    lambda z, y: (z ^ 1, y),
    lambda z, y: (3 - z, y),
    lambda z, y: (z, 1 - y),
)


def snp_exchange(value, dim):
    flip = SNP_FLIPS[dim]
    pairs = []
    for z, y in SNPS:
        z2, y2 = flip(z, y)
        pairs.append((z * 2 + y, z2 * 2 + y2))
    return lax.ppermute(value, "snp", pairs)


def snp_bits():
    index = lax.axis_index("snp")
    z, y = index // 2, index % 2
    return (jnp.where((z == 1) | (z == 2), 1, 0), jnp.where(z >= 2, 1, 0), y)


ORDERS = ((0, 1, 2), (1, 2, 0), (2, 0, 1))


def cut(value, start, size):
    return lax.dynamic_slice_in_dim(value, start, size, 0)


def join(mine, other, bit):
    rows = mine.shape[0]
    return cut(jnp.concatenate([mine, other, mine], 0), bit * rows, 2 * rows)


PART_ROWS = (768, 640, 640)


def halves(parts, stage, bits):
    sent, kept = [], []
    for part, order in zip(parts, ORDERS):
        half = part.shape[0] // 2
        sent.append(cut(part, (1 - bits[order[stage]]) * half, half))
        kept.append(cut(part, bits[order[stage]] * half, half))
    return sent, kept


def exchange_all(values, stage):
    return [snp_exchange(v, order[stage]) for v, order in zip(values, ORDERS)]


def sum_and_factor(product, diag, pheno):
    bits = snp_bits()
    at, starts, parts = 0, [], []
    for dim, size in enumerate(PART_ROWS):
        term, part = tie(snp_exchange(diag, dim), product(at, size))
        diag = diag + term
        starts.append(at)
        parts.append(part)
        at += size

    sent, kept = halves(parts, 0, bits)
    got = exchange_all(sent, 0)
    diag, pheno = gather_small(diag, pheno)
    state, *got = tie(factor_block(0, diag), *got)
    parts = [k + g for k, g in zip(kept, got)]
    for stage in (1, 2):
        sent, kept = halves(parts, stage, bits)
        got = exchange_all(sent, stage)
        state, *got = tie(factor_block(stage, state), *got)
        parts = [k + g for k, g in zip(kept, got)]

    got = exchange_all(parts, 2)
    lower, inverse = factor_block(3, state)
    lower, inverse, *got = tie(lower, inverse, *got)
    parts = [join(p, g, bits[order[2]]) for p, g, order in zip(parts, got, ORDERS)]
    parts = [dot_t(part, inverse, HIGHEST) for part in parts]
    got = exchange_all(parts, 1)
    parts = [join(p, g, bits[order[1]]) for p, g, order in zip(parts, got, ORDERS)]
    got = exchange_all(parts, 0)
    pieces = []
    for start, size, order, part, other in zip(starts, PART_ROWS, ORDERS, parts, got):
        half = size // 2
        bit = bits[order[0]]
        pieces.append((start + bit * half, part))
        pieces.append((start + (1 - bit) * half, other))
    return lower, inverse, pheno, pieces


def gather_small(diag, pheno):
    tile = lax.axis_index("tile")
    x = (tile // 2) % 4
    pheno = jnp.where(tile < 2, pheno, jnp.zeros_like(pheno))
    pheno = pheno + tile_send(pheno, lambda y, xx, c: (1 - y, xx, c))
    rows = diag.shape[0]
    for bit, flip in (
        (x % 2, lambda y, xx, c: (y, xx ^ 1, c)),
        (x // 2, lambda y, xx, c: (y, 3 - xx, c)),
    ):
        other = tile_send(jnp.concatenate([diag, pheno], 0), flip)
        diag = join(diag, other[:rows], bit)
        pheno = pheno + other[rows:]
        rows = 2 * rows
    other = swap_cores(jnp.concatenate([diag, pheno], 0))
    core = tile % 2
    return join(diag, other[:rows], core), join(pheno, other[rows:], core)


def swap_cores(value):
    return tile_send(value, lambda y, x, c: (y, x, 1 - c))


def tie(*values):
    return lax.optimization_barrier(values)


def spread_panels(head, counts):
    tile = lax.axis_index("tile")
    x = (tile // 2) % 4
    below = tile >= 8
    p = [head[i * 32 : (i + 1) * 32] for i in range(8)]
    at = lambda row, col: lambda y, xx, c: (y, xx) == (row, col)
    to = lambda row, col: lambda y, xx, c: (row, col, c)
    ahead = lambda y, xx, c: (y, (xx + 1) % 4, c)
    back = lambda y, xx, c: (y, (xx + 3) % 4, c)
    root = at(0, 0)

    def go_down(own):
        down = tile_send(own, lambda y, xx, c: (1, xx, c), lambda y, xx, c: y == 0)
        return jnp.where(below, down, own)

    far_a = tile_send(p[4], to(0, 1), root)
    far_b = tile_send(p[5], to(0, 3), root)
    near = tile_send(head[64:128], to(0, 1), root)
    behind = tile_send(head[192:256], to(0, 3), root)
    far_a, far_b, counts = tie(far_a, far_b, counts)
    far_a = tile_send(far_a, to(0, 2), at(0, 1))
    far_b = tile_send(far_b, to(0, 2), at(0, 3))
    counts = counts + swap_cores(counts)
    counts = counts + tile_send(counts, lambda y, xx, c: (1 - y, xx, c))
    near, behind, counts = tie(near, behind, counts)
    own_a = jnp.where(x == 0, p[0], jnp.where(x == 1, near[:32], jnp.where(x == 3, behind[:32], far_a)))
    own_b = jnp.where(x == 0, p[1], jnp.where(x == 1, near[32:], jnp.where(x == 3, behind[32:], far_b)))
    own_a = go_down(own_a)
    counts = counts + tile_send(counts, lambda y, xx, c: (y, xx ^ 1, c))
    counts = counts + tile_send(counts, lambda y, xx, c: (y, 3 - xx, c))
    own_b = go_down(own_b)
    own_a, counts = tie(own_a, counts)
    left_a = tile_send(own_a, ahead)
    right_a = tile_send(own_a, back)
    left_b = tile_send(own_b, ahead)
    right_b = tile_send(own_b, back)
    far_a = tile_send(left_a, ahead)
    far_b = tile_send(right_b, back)
    mine = (own_a, own_b, left_a, right_a, left_b, right_b, far_a, far_b)
    return mine, tuple(swap_cores(piece) for piece in mine), counts


PIECES = ((0, 0), (0, 32), (3, 0), (1, 0), (3, 32), (1, 32), (2, 0), (2, 32))


def split(value):
    high = value.astype(jnp.bfloat16)
    return high, (value - high.astype(F32)).astype(jnp.bfloat16)


NT = (((1,), (1,)), ((), ()))


def dot3(a, b):
    total = lax.dot_general(a[0], b[0], NT, preferred_element_type=F32)
    total = total + lax.dot_general(a[0], b[1], NT, preferred_element_type=F32)
    return total + lax.dot_general(a[1], b[0], NT, preferred_element_type=F32)


def standardize_kernel(where_ref, mean_ref, weight_ref, *refs):
    mine, other = refs[:8], refs[8:16]
    diag_ref, panels_ref, own = refs[16:]
    x = where_ref[0]
    core = where_ref[1]
    mean = mean_ref[...]
    weight = weight_ref[...]
    for i, (turn, offset) in enumerate(PIECES):
        at = ((x + turn) % 4) * 64 + offset
        centered = mine[i][...] - mean
        if turn == 0:
            own[offset : offset + 32, :] = centered
        for panel, value in ((core, centered), (1 - core, other[i][...] - mean)):
            panels_ref[pl.ds(pl.multiple_of(panel * BLK + at, 32), 32), :] = value * weight
    diag_ref[...] = dot3(split(own[...]), split(panels_ref[...]))


def standardize_panels(mine, other, mean, weight):
    n = mean.shape[0]
    tile = lax.axis_index("tile")
    where = jnp.stack([(tile // 2) % 4, tile % 2]).astype(jnp.int32)
    vmem = pl.BlockSpec(memory_space=pltpu.VMEM)
    return pl.pallas_call(
        standardize_kernel,
        out_shape=(
            jax.ShapeDtypeStruct((64, 2 * BLK), F32),
            jax.ShapeDtypeStruct((2 * BLK, n), F32),
        ),
        in_specs=[pl.BlockSpec(memory_space=pltpu.SMEM)] + [vmem] * 18,
        out_specs=(vmem, vmem),
        scratch_shapes=[pltpu.VMEM((64, n), F32)],
        compiler_params=pltpu.CompilerParams(vmem_limit_bytes=16 << 20),
        cost_estimate=pl.CostEstimate(flops=1000, bytes_accessed=1000, transcendentals=0),
        name="standardize_panels",
    )(where, mean.reshape(1, n), weight.reshape(1, n), *mine, *other)


def lane_columns(rows, j):
    return [jnp.broadcast_to(rows[:, j + k : j + k + 1], (8, 128)) for k in range(8)]


def factor_leaf(work):
    sub = lax.broadcasted_iota(jnp.int32, (8, 128), 0)
    current = [work[0:8, 0:128], work[0:8, 128:256]]
    for j in range(0, 128, 8):
        last = j == 120
        columns = lane_columns(current[0], j)
        s = {}
        for k in range(8):
            for m in range(k, 8):
                s[m, k] = jnp.broadcast_to(columns[k][m : m + 1, :], (8, 128))
        if not last:
            following = [work[j + 8 : j + 16, 0:128], work[j + 8 : j + 16, 128:256]]
            below = lane_columns(following[0], j)
        scale, low, coefs = [], {}, []
        rows = ([], [])
        for k in range(8):
            scale.append(lax.rsqrt(s[k, k]))
            for m in range(k + 1, 8):
                low[m, k] = s[m, k] * scale[k]
            for n in range(k + 1, 8):
                for m in range(n, 8):
                    s[m, n] = s[m, n] - low[m, k] * low[n, k]
            for h in range(2):
                row = jnp.broadcast_to(current[h][k : k + 1, :], (8, 128))
                for i in range(k):
                    row = row - low[k, i] * rows[h][i]
                rows[h].append(row * scale[k])
            if not last:
                coef = below[k]
                for i in range(k):
                    coef = coef - coefs[i] * low[k, i]
                coefs.append(coef * scale[k])
                for h in range(2):
                    following[h] = following[h] - coefs[k] * rows[h][k]
        solved = []
        for h in range(2):
            block = rows[h][0]
            for m in range(1, 8):
                block = jnp.where(sub == m, rows[h][m], block)
            solved.append(block)
        both = jnp.concatenate(solved, 1)
        work[j : j + 8, :] = both
        if j < 112:
            update = lax.dot_general(
                solved[0], both, (((0,), (0,)), ((), ())), precision=HIGHEST, preferred_element_type=F32
            )
            work[j + 16 : 128, :] = work[j + 16 : 128, :] - update[j + 16 :, :]
        if not last:
            current = following


def factor_step(b, first_ref, aug, work):
    n = aug.shape[0]
    rows = slice(b * 128, b * 128 + 128)
    if b == 0:
        eye = lax.broadcasted_iota(jnp.int32, (n, n), 0) == lax.broadcasted_iota(jnp.int32, (n, n), 1)
        eye = jnp.where(eye, 1.0, 0.0).astype(F32)
        aug[:, 0:n] = first_ref[...] + eye
        aug[:, n : 2 * n] = eye
    else:
        aug[...] = first_ref[...]
    small = lax.broadcasted_iota(jnp.int32, (128, 128), 0) == lax.broadcasted_iota(
        jnp.int32, (128, 128), 1
    )
    work[:, 0:128] = aug[rows, rows]
    work[:, 128:256] = jnp.where(small, 1.0, 0.0).astype(F32)
    factor_leaf(work)
    right = slice(b * 128, n + b * 128 + 128)
    solved = lax.dot_general(
        work[:, 128:256],
        aug[rows, right],
        (((1,), (0,)), ((), ())),
        precision=HIGHEST,
        preferred_element_type=F32,
    )
    aug[rows, right] = solved
    aug[rows, rows] = work[:, 0:128]
    if b < 3:
        below = slice(b * 128 + 128, n)
        aug[below, right] = aug[below, right] - lax.dot_general(
            solved[:, 128 : n - b * 128],
            solved,
            (((0,), (0,)), ((), ())),
            precision=HIGHEST,
            preferred_element_type=F32,
        )


def last_step_kernel(in_ref, lower_ref, inverse_ref, aug, work):
    factor_step(3, in_ref, aug, work)
    n = aug.shape[0]
    row = lax.broadcasted_iota(jnp.int32, (n, n), 0)
    col = lax.broadcasted_iota(jnp.int32, (n, n), 1)
    lower_ref[...] = jnp.where(row >= col, jnp.transpose(aug[:, 0:n]), 0.0)
    inverse_ref[...] = aug[:, n : 2 * n]


def factor_block(b, value):
    n = value.shape[0]
    vmem = pl.BlockSpec(memory_space=pltpu.VMEM)
    work = pltpu.VMEM((128, 256), F32)
    square = jax.ShapeDtypeStruct((n, n), F32)
    if b == 3:
        body, shape, specs = last_step_kernel, (square, square), (vmem, vmem)
        scratch = [pltpu.VMEM((n, 2 * n), F32), work]
    else:
        body = lambda i, o, w: factor_step(b, i, o, w)
        shape, specs, scratch = jax.ShapeDtypeStruct((n, 2 * n), F32), vmem, [work]
    return pl.pallas_call(
        body,
        out_shape=shape,
        in_specs=[vmem],
        out_specs=specs,
        scratch_shapes=scratch,
        compiler_params=pltpu.CompilerParams(vmem_limit_bytes=16 << 20),
        cost_estimate=pl.CostEstimate(flops=7_000_000_000 if b else 1000, bytes_accessed=1000, transcendentals=0),
        name="factor_%d" % b,
    )(value)


def dot_t(a, b, precision):
    return lax.dot_general(
        a, b, (((1,), (1,)), ((), ())), precision=precision, preferred_element_type=F32
    )


def output_kernel(where_ref, *refs):
    n_pieces = len(refs) - 8
    pieces = refs[:n_pieces]
    lower_ref, solved_ref, pheno_ref, factor_ref, white_ref, product, sems, head_sem = refs[n_pieces:]
    tile = where_ref[n_pieces]
    copies = []
    for i, piece in enumerate(pieces):
        rows = piece.shape[0]
        at = pl.multiple_of(where_ref[i], 64)
        copy = pltpu.make_async_copy(piece, factor_ref.at[pl.ds(at, rows), :], sems.at[i])
        copy.start()
        copies.append(copy)
    solved_high, solved_low = split(solved_ref[...])
    for i, piece in enumerate(pieces):
        rows = piece.shape[0]
        at = pl.multiple_of(where_ref[i], 64)
        high, low = split(piece[...])
        total = jnp.dot(high, solved_high, preferred_element_type=F32)
        total = total + jnp.dot(high, solved_low, preferred_element_type=F32)
        product[pl.ds(at, rows), :] = total + jnp.dot(low, solved_high, preferred_element_type=F32)
    white_ref[...] = pheno_ref[...] - jnp.transpose(product[...])
    for copy in copies:
        copy.wait()
    for panel in range(2):

        @pl.when(tile == panel)
        def _():
            own = slice(panel * BLK, panel * BLK + BLK)
            head = pltpu.make_async_copy(lower_ref.at[own, :], factor_ref.at[0:BLK, :], head_sem)
            head.start()
            white_ref[:, 0:BLK] = jnp.transpose(solved_ref[own, :])
            head.wait()


def write_outputs(pieces, lower, solved, pheno):
    n_pheno, rows = pheno.shape
    where = jnp.stack([at for at, _ in pieces] + [lax.axis_index("tile")]).astype(jnp.int32)
    vmem = pl.BlockSpec(memory_space=pltpu.VMEM)
    return pl.pallas_call(
        output_kernel,
        out_shape=(
            jax.ShapeDtypeStruct((rows, 2 * BLK), F32),
            jax.ShapeDtypeStruct((n_pheno, rows), F32),
        ),
        in_specs=[pl.BlockSpec(memory_space=pltpu.SMEM)] + [vmem] * (len(pieces) + 3),
        out_specs=(pl.BlockSpec(memory_space=pl.ANY), vmem),
        scratch_shapes=[
            pltpu.VMEM((rows, n_pheno), F32),
            pltpu.SemaphoreType.DMA((len(pieces),)),
            pltpu.SemaphoreType.DMA,
        ],
        compiler_params=pltpu.CompilerParams(vmem_limit_bytes=32 << 20),
        cost_estimate=pl.CostEstimate(flops=500_000_000, bytes_accessed=10 << 20, transcendentals=0),
        name="write_outputs",
    )(where, *[p for _, p in pieces], lower, solved, pheno)


def body(dosages, phenotypes):
    n_tile = lax.axis_size("tile")
    n_snp = lax.axis_size("snp")
    rows, snps = dosages.shape
    width = BLK
    tile_index = lax.axis_index("tile")

    counts = jnp.sum(dosages, axis=0)
    mine, other, counts = spread_panels(dosages[:width], counts.reshape(16, 128))
    flipped = phenotypes.T
    head = flipped[:, :width]
    head = jnp.concatenate([head[:32], head[32:]], 1)

    counts = counts.reshape(snps)
    allele_freq = counts / (2.0 * rows * n_tile)
    spread = jnp.maximum(2.0 * allele_freq * (1.0 - allele_freq), 0.05)
    mean = 2.0 * allele_freq
    weight = (1.0 / (snps * n_snp)) / spread
    diag, panels = standardize_panels(mine, other, mean, weight)

    def product(start, size):
        return dot_t(dosages[start : start + size] - mean, panels, HIGH)

    lower, inverse, heads, pieces = sum_and_factor(product, diag, head)
    panel_pheno = jnp.concatenate(
        [
            jnp.concatenate([heads[:32, :width], heads[32:, :width]], 1),
            jnp.concatenate([heads[:32, width:], heads[32:, width:]], 1),
        ],
        0,
    )
    solved = dot_t(inverse, panel_pheno, HIGHEST)
    factor, whitened = write_outputs(pieces, lower, solved, flipped)
    return factor, whitened.T


def solution(mesh):
    placed = (P("tile", "snp"), P("tile", "snp"))
    return jax.shard_map(
        body,
        mesh=mesh,
        in_specs=placed,
        out_specs=(P("tile", None), P("tile", "snp")),
        check_vma=False,
    )
```

```python
import jax
import jax.numpy as jnp
from jax import lax
from jax.experimental import pallas as pl
from jax.experimental.pallas import tpu as pltpu
from jax.sharding import PartitionSpec as P

BLK = 256
HIGHEST = lax.Precision.HIGHEST
HIGH = lax.Precision.HIGH
F32 = jnp.float32

TILES = [(y, x, c) for y in range(2) for x in range(4) for c in range(2)]
SNPS = [(z, y) for z in range(4) for y in range(2)]


def tile_id(y, x, c):
    return (y * 4 + x) * 2 + c


def tile_send(value, target, only=None):
    pairs = [
        (tile_id(*a), tile_id(*target(*a))) for a in TILES if only is None or only(*a)
    ]
    return lax.ppermute(value, "tile", pairs)


SNP_FLIPS = (
    lambda z, y: (z ^ 1, y),
    lambda z, y: (3 - z, y),
    lambda z, y: (z, 1 - y),
)


def snp_exchange(value, dim):
    flip = SNP_FLIPS[dim]
    pairs = []
    for z, y in SNPS:
        z2, y2 = flip(z, y)
        pairs.append((z * 2 + y, z2 * 2 + y2))
    return lax.ppermute(value, "snp", pairs)


def snp_bits():
    index = lax.axis_index("snp")
    z, y = index // 2, index % 2
    return (jnp.where((z == 1) | (z == 2), 1, 0), jnp.where(z >= 2, 1, 0), y)


ORDERS = ((0, 1, 2), (1, 2, 0), (2, 0, 1))


def cut(value, start, size):
    return lax.dynamic_slice_in_dim(value, start, size, 0)


def join(mine, other, bit):
    rows = mine.shape[0]
    return cut(jnp.concatenate([mine, other, mine], 0), bit * rows, 2 * rows)


PART_ROWS = (768, 640, 640)


def halves(parts, stage, bits):
    sent, kept = [], []
    for part, order in zip(parts, ORDERS):
        half = part.shape[0] // 2
        sent.append(cut(part, (1 - bits[order[stage]]) * half, half))
        kept.append(cut(part, bits[order[stage]] * half, half))
    return sent, kept


def exchange_all(values, stage):
    return [snp_exchange(v, order[stage]) for v, order in zip(values, ORDERS)]


def sum_and_factor(product, diag, pheno):
    bits = snp_bits()
    at, starts = 0, []
    for size in PART_ROWS:
        starts.append(at)
        at += size
    sent, kept = [], []
    for start, size, order in zip(starts, PART_ROWS, ORDERS):
        half = size // 2
        sent.append(product(start + (1 - bits[order[0]]) * half, half))
        kept.append(product(start + bits[order[0]] * half, half))
    for dim in range(3):
        term, sent[dim] = tie(snp_exchange(diag, dim), sent[dim])
        diag = diag + term
    diag, pheno, kept = gather_small(diag, pheno, kept)
    diag, *sent = tie(diag, *sent)
    got = exchange_all(sent, 0)
    state, *got = tie(factor_block(1, factor_block(0, diag)), *got)
    parts = [k + g for k, g in zip(kept, got)]

    sent, kept = halves(parts, 1, bits)
    got = exchange_all(sent, 1)
    state, *got = tie(factor_block(2, state), *got)
    parts = [k + g for k, g in zip(kept, got)]

    sent, kept = halves(parts, 2, bits)
    got = exchange_all(sent, 2)
    lower, inverse = factor_block(3, state)
    lower, inverse, *got = tie(lower, inverse, *got)
    parts = [dot_t(k + g, inverse, HIGHEST) for k, g in zip(kept, got)]

    for stage in (2, 1):
        got = exchange_all(parts, stage)
        parts = [join(p, g, bits[order[stage]]) for p, g, order in zip(parts, got, ORDERS)]
    got = exchange_all(parts, 0)
    pieces = []
    for start, size, order, part, other in zip(starts, PART_ROWS, ORDERS, parts, got):
        half = size // 2
        bit = bits[order[0]]
        pieces.append((start + bit * half, part))
        pieces.append((start + (1 - bit) * half, other))
    return lower, inverse, pheno, pieces


def gather_small(diag, pheno, beside):
    beside = list(beside)
    tile = lax.axis_index("tile")
    x = (tile // 2) % 4
    pheno = jnp.where(tile < 2, pheno, jnp.zeros_like(pheno))
    pheno = pheno + tile_send(pheno, lambda y, xx, c: (1 - y, xx, c))
    rows = diag.shape[0]
    for i, (bit, flip) in enumerate(
        (
            (x % 2, lambda y, xx, c: (y, xx ^ 1, c)),
            (x // 2, lambda y, xx, c: (y, 3 - xx, c)),
        )
    ):
        other = tile_send(jnp.concatenate([diag, pheno], 0), flip)
        other, beside[i] = tie(other, beside[i])
        diag = join(diag, other[:rows], bit)
        pheno = pheno + other[rows:]
        rows = 2 * rows
    other = swap_cores(jnp.concatenate([diag, pheno], 0))
    other, beside[2] = tie(other, beside[2])
    core = tile % 2
    return join(diag, other[:rows], core), join(pheno, other[rows:], core), beside


def swap_cores(value):
    return tile_send(value, lambda y, x, c: (y, x, 1 - c))


def tie(*values):
    return lax.optimization_barrier(values)


def spread_panels(head, counts):
    tile = lax.axis_index("tile")
    x = (tile // 2) % 4
    below = tile >= 8
    p = [head[i * 32 : (i + 1) * 32] for i in range(8)]
    at = lambda row, col: lambda y, xx, c: (y, xx) == (row, col)
    to = lambda row, col: lambda y, xx, c: (row, col, c)
    ahead = lambda y, xx, c: (y, (xx + 1) % 4, c)
    back = lambda y, xx, c: (y, (xx + 3) % 4, c)
    root = at(0, 0)

    def go_down(own):
        down = tile_send(own, lambda y, xx, c: (1, xx, c), lambda y, xx, c: y == 0)
        return jnp.where(below, down, own)

    far_a = tile_send(p[4], to(0, 1), root)
    far_b = tile_send(p[5], to(0, 3), root)
    near = tile_send(head[64:128], to(0, 1), root)
    behind = tile_send(head[192:256], to(0, 3), root)
    far_a, far_b, counts = tie(far_a, far_b, counts)
    far_a = tile_send(far_a, to(0, 2), at(0, 1))
    far_b = tile_send(far_b, to(0, 2), at(0, 3))
    counts = counts + swap_cores(counts)
    counts = counts + tile_send(counts, lambda y, xx, c: (1 - y, xx, c))
    near, behind, counts = tie(near, behind, counts)
    own_a = jnp.where(x == 0, p[0], jnp.where(x == 1, near[:32], jnp.where(x == 3, behind[:32], far_a)))
    own_b = jnp.where(x == 0, p[1], jnp.where(x == 1, near[32:], jnp.where(x == 3, behind[32:], far_b)))
    own_a = go_down(own_a)
    counts = counts + tile_send(counts, lambda y, xx, c: (y, xx ^ 1, c))
    counts = counts + tile_send(counts, lambda y, xx, c: (y, 3 - xx, c))
    own_b = go_down(own_b)
    own_a, counts = tie(own_a, counts)
    left_a = tile_send(own_a, ahead)
    right_a = tile_send(own_a, back)
    left_b = tile_send(own_b, ahead)
    right_b = tile_send(own_b, back)
    far_a = tile_send(left_a, ahead)
    far_b = tile_send(right_b, back)
    mine = (own_a, own_b, left_a, right_a, left_b, right_b, far_a, far_b)
    return mine, tuple(swap_cores(piece) for piece in mine), counts


PIECES = ((0, 0), (0, 32), (3, 0), (1, 0), (3, 32), (1, 32), (2, 0), (2, 32))


def split(value):
    high = value.astype(jnp.bfloat16)
    return high, (value - high.astype(F32)).astype(jnp.bfloat16)


NT = (((1,), (1,)), ((), ()))


def dot3(a, b):
    total = lax.dot_general(a[0], b[0], NT, preferred_element_type=F32)
    total = total + lax.dot_general(a[0], b[1], NT, preferred_element_type=F32)
    return total + lax.dot_general(a[1], b[0], NT, preferred_element_type=F32)


def standardize_kernel(where_ref, mean_ref, weight_ref, *refs):
    mine, other = refs[:8], refs[8:16]
    diag_ref, panels_ref, own = refs[16:]
    x = where_ref[0]
    core = where_ref[1]
    mean = mean_ref[...]
    weight = weight_ref[...]
    for i, (turn, offset) in enumerate(PIECES):
        at = ((x + turn) % 4) * 64 + offset
        centered = mine[i][...] - mean
        if turn == 0:
            own[offset : offset + 32, :] = centered
        for panel, value in ((core, centered), (1 - core, other[i][...] - mean)):
            panels_ref[pl.ds(pl.multiple_of(panel * BLK + at, 32), 32), :] = value * weight
    diag_ref[...] = dot3(split(own[...]), split(panels_ref[...]))


def standardize_panels(mine, other, mean, weight):
    n = mean.shape[0]
    tile = lax.axis_index("tile")
    where = jnp.stack([(tile // 2) % 4, tile % 2]).astype(jnp.int32)
    vmem = pl.BlockSpec(memory_space=pltpu.VMEM)
    return pl.pallas_call(
        standardize_kernel,
        out_shape=(
            jax.ShapeDtypeStruct((64, 2 * BLK), F32),
            jax.ShapeDtypeStruct((2 * BLK, n), F32),
        ),
        in_specs=[pl.BlockSpec(memory_space=pltpu.SMEM)] + [vmem] * 18,
        out_specs=(vmem, vmem),
        scratch_shapes=[pltpu.VMEM((64, n), F32)],
        compiler_params=pltpu.CompilerParams(vmem_limit_bytes=16 << 20),
        cost_estimate=pl.CostEstimate(flops=1000, bytes_accessed=1000, transcendentals=0),
        name="standardize_panels",
    )(where, mean.reshape(1, n), weight.reshape(1, n), *mine, *other)


def lane_columns(rows, j):
    return [jnp.broadcast_to(rows[:, j + k : j + k + 1], (8, 128)) for k in range(8)]


def factor_leaf(work):
    sub = lax.broadcasted_iota(jnp.int32, (8, 128), 0)
    row = lax.broadcasted_iota(jnp.int32, (128, 256), 0)

    def step(i, carry):
        current, before = carry[:2], carry[2:]
        j = pl.multiple_of(i * 8, 8)
        turn = lax.rem(128 - j, 128)
        columns = lane_columns(pltpu.roll(current[0], turn, 1), 0)
        update = lax.dot_general(
            before[0],
            jnp.concatenate(before, 1),
            (((0,), (0,)), ((), ())),
            precision=HIGHEST,
            preferred_element_type=F32,
        )
        work[0:128, :] = work[0:128, :] - jnp.where(row >= j + 8, update, 0.0)
        following = [work[pl.ds(j + 8, 8), 0:128], work[pl.ds(j + 8, 8), 128:256]]
        below = lane_columns(pltpu.roll(following[0], turn, 1), 0)
        s = {}
        for k in range(8):
            for m in range(k, 8):
                s[m, k] = jnp.broadcast_to(columns[k][m : m + 1, :], (8, 128))
        scale, low, coefs = [], {}, []
        rows = ([], [])
        for k in range(8):
            scale.append(lax.rsqrt(s[k, k]))
            for m in range(k + 1, 8):
                low[m, k] = s[m, k] * scale[k]
            for n in range(k + 1, 8):
                for m in range(n, 8):
                    s[m, n] = s[m, n] - low[m, k] * low[n, k]
            coef = below[k]
            for q in range(k):
                coef = coef - coefs[q] * low[k, q]
            coefs.append(coef * scale[k])
            for h in range(2):
                line = jnp.broadcast_to(current[h][k : k + 1, :], (8, 128))
                for q in range(k):
                    line = line - low[k, q] * rows[h][q]
                rows[h].append(line * scale[k])
                following[h] = following[h] - coefs[k] * rows[h][k]
        solved = []
        for h in range(2):
            block = rows[h][0]
            for m in range(1, 8):
                block = jnp.where(sub == m, rows[h][m], block)
            solved.append(block)
        work[pl.ds(j, 8), :] = jnp.concatenate(solved, 1)
        return (*following, *solved)

    none = jnp.zeros((8, 128), F32)
    lax.fori_loop(0, 16, step, (work[0:8, 0:128], work[0:8, 128:256], none, none))


def factor_step(b, first_ref, aug, work):
    n = aug.shape[0]
    rows = slice(b * 128, b * 128 + 128)
    if b == 0:
        eye = lax.broadcasted_iota(jnp.int32, (n, n), 0) == lax.broadcasted_iota(jnp.int32, (n, n), 1)
        eye = jnp.where(eye, 1.0, 0.0).astype(F32)
        aug[:, 0:n] = first_ref[...] + eye
        aug[:, n : 2 * n] = eye
    else:
        aug[...] = first_ref[...]
    small = lax.broadcasted_iota(jnp.int32, (128, 128), 0) == lax.broadcasted_iota(
        jnp.int32, (128, 128), 1
    )
    work[0:128, 0:128] = aug[rows, rows]
    work[0:128, 128:256] = jnp.where(small, 1.0, 0.0).astype(F32)
    work[128:136, :] = jnp.zeros((8, 256), F32)
    factor_leaf(work)
    right = slice(b * 128, n + b * 128 + 128)
    solved = lax.dot_general(
        work[0:128, 128:256],
        aug[rows, right],
        (((1,), (0,)), ((), ())),
        precision=HIGHEST,
        preferred_element_type=F32,
    )
    aug[rows, right] = solved
    aug[rows, rows] = work[0:128, 0:128]
    if b < 3:
        below = slice(b * 128 + 128, n)
        aug[below, right] = aug[below, right] - lax.dot_general(
            solved[:, 128 : n - b * 128],
            solved,
            (((0,), (0,)), ((), ())),
            precision=HIGHEST,
            preferred_element_type=F32,
        )


def last_step_kernel(in_ref, lower_ref, inverse_ref, aug, work):
    factor_step(3, in_ref, aug, work)
    n = aug.shape[0]
    row = lax.broadcasted_iota(jnp.int32, (n, n), 0)
    col = lax.broadcasted_iota(jnp.int32, (n, n), 1)
    lower_ref[...] = jnp.where(row >= col, jnp.transpose(aug[:, 0:n]), 0.0)
    inverse_ref[...] = aug[:, n : 2 * n]


def factor_block(b, value):
    n = value.shape[0]
    vmem = pl.BlockSpec(memory_space=pltpu.VMEM)
    work = pltpu.VMEM((136, 256), F32)
    square = jax.ShapeDtypeStruct((n, n), F32)
    if b == 3:
        body, shape, specs = last_step_kernel, (square, square), (vmem, vmem)
        scratch = [pltpu.VMEM((n, 2 * n), F32), work]
    else:
        body = lambda i, o, w: factor_step(b, i, o, w)
        shape, specs, scratch = jax.ShapeDtypeStruct((n, 2 * n), F32), vmem, [work]
    return pl.pallas_call(
        body,
        out_shape=shape,
        in_specs=[vmem],
        out_specs=specs,
        scratch_shapes=scratch,
        compiler_params=pltpu.CompilerParams(vmem_limit_bytes=16 << 20),
        cost_estimate=pl.CostEstimate(flops=7_000_000_000, bytes_accessed=1000, transcendentals=0),
        name="factor_%d" % b,
    )(value)


def dot_t(a, b, precision):
    return lax.dot_general(
        a, b, (((1,), (1,)), ((), ())), precision=precision, preferred_element_type=F32
    )


def output_kernel(where_ref, *refs):
    n_pieces = len(refs) - 10
    pieces = refs[:n_pieces]
    lower_ref, solved_ref, pheno_ref, factor_ref, white_ref, product, pheno, sems, head_sem, pheno_sem = refs[
        n_pieces:
    ]
    tile = where_ref[n_pieces]
    fetch = pltpu.make_async_copy(pheno_ref, pheno, pheno_sem)
    fetch.start()
    copies = []
    for i, piece in enumerate(pieces):
        rows = piece.shape[0]
        at = pl.multiple_of(where_ref[i], 64)
        copy = pltpu.make_async_copy(piece, factor_ref.at[pl.ds(at, rows), :], sems.at[i])
        copy.start()
        copies.append(copy)
    n = solved_ref.shape[1]
    solved_high, solved_low = split(solved_ref[...])
    solved = jnp.concatenate([solved_high, solved_low], 1)
    for i, piece in enumerate(pieces):
        rows = piece.shape[0]
        at = pl.multiple_of(where_ref[i], 64)
        high, low = split(piece[...])
        total = jnp.dot(high, solved, preferred_element_type=F32)
        total = total[:, :n] + total[:, n:]
        product[pl.ds(at, rows), :] = total + jnp.dot(low, solved_high, preferred_element_type=F32)
    fetch.wait()
    white_ref[...] = pheno[...] - jnp.transpose(product[...])
    for copy in copies:
        copy.wait()
    for panel in range(2):

        @pl.when(tile == panel)
        def _():
            own = slice(panel * BLK, panel * BLK + BLK)
            head = pltpu.make_async_copy(lower_ref.at[own, :], factor_ref.at[0:BLK, :], head_sem)
            head.start()
            white_ref[:, 0:BLK] = jnp.transpose(solved_ref[own, :])
            head.wait()


def write_outputs(pieces, lower, solved, pheno):
    n_pheno, rows = pheno.shape
    where = jnp.stack([at for at, _ in pieces] + [lax.axis_index("tile")]).astype(jnp.int32)
    vmem = pl.BlockSpec(memory_space=pltpu.VMEM)
    anywhere = pl.BlockSpec(memory_space=pl.ANY)
    return pl.pallas_call(
        output_kernel,
        out_shape=(
            jax.ShapeDtypeStruct((rows, 2 * BLK), F32),
            jax.ShapeDtypeStruct((n_pheno, rows), F32),
        ),
        in_specs=[pl.BlockSpec(memory_space=pltpu.SMEM)] + [vmem] * len(pieces) + [anywhere, vmem, anywhere],
        out_specs=(anywhere, vmem),
        scratch_shapes=[
            pltpu.VMEM((rows, n_pheno), F32),
            pltpu.VMEM((n_pheno, rows), F32),
            pltpu.SemaphoreType.DMA((len(pieces),)),
            pltpu.SemaphoreType.DMA,
            pltpu.SemaphoreType.DMA,
        ],
        compiler_params=pltpu.CompilerParams(vmem_limit_bytes=12 << 20),
        cost_estimate=pl.CostEstimate(flops=500_000_000, bytes_accessed=10 << 20, transcendentals=0),
        name="write_outputs",
    )(where, *[p for _, p in pieces], lower, solved, pheno)


def body(dosages, phenotypes):
    n_tile = lax.axis_size("tile")
    n_snp = lax.axis_size("snp")
    rows, snps = dosages.shape
    width = BLK
    tile_index = lax.axis_index("tile")

    counts = jnp.sum(dosages, axis=0)
    mine, other, counts = spread_panels(dosages[:width], counts.reshape(16, 128))
    flipped = phenotypes.T
    head = flipped[:, :width]
    head = jnp.concatenate([head[:32], head[32:]], 1)

    counts = counts.reshape(snps)
    allele_freq = counts / (2.0 * rows * n_tile)
    spread = jnp.maximum(2.0 * allele_freq * (1.0 - allele_freq), 0.05)
    mean = 2.0 * allele_freq
    weight = (1.0 / (snps * n_snp)) / spread
    diag, panels = standardize_panels(mine, other, mean, weight)

    def product(start, size):
        return dot_t(cut(dosages, start, size) - mean, panels, HIGH)

    lower, inverse, heads, pieces = sum_and_factor(product, diag, head)
    panel_pheno = jnp.concatenate(
        [
            jnp.concatenate([heads[:32, :width], heads[32:, :width]], 1),
            jnp.concatenate([heads[:32, width:], heads[32:, width:]], 1),
        ],
        0,
    )
    solved = dot_t(inverse, panel_pheno, HIGHEST)
    factor, whitened = write_outputs(pieces, lower, solved, flipped)
    return factor, whitened.T


def solution(mesh):
    placed = (P("tile", "snp"), P("tile", "snp"))
    return jax.shard_map(
        body,
        mesh=mesh,
        in_specs=placed,
        out_specs=(P("tile", None), P("tile", "snp")),
        check_vma=False,
    )
```

```python
import jax
import jax.numpy as jnp
from jax import lax
from jax.experimental import pallas as pl
from jax.experimental.pallas import tpu as pltpu
from jax.sharding import PartitionSpec as P

BLK = 256
HIGHEST = lax.Precision.HIGHEST
HIGH = lax.Precision.HIGH
F32 = jnp.float32

TILES = [(y, x, c) for y in range(2) for x in range(4) for c in range(2)]
SNPS = [(z, y) for z in range(4) for y in range(2)]


def tile_id(y, x, c):
    return (y * 4 + x) * 2 + c


def tile_send(value, target, only=None):
    pairs = [
        (tile_id(*a), tile_id(*target(*a))) for a in TILES if only is None or only(*a)
    ]
    return lax.ppermute(value, "tile", pairs)


SNP_FLIPS = (
    lambda z, y: (z ^ 1, y),
    lambda z, y: (3 - z, y),
    lambda z, y: (z, 1 - y),
)


def snp_exchange(value, dim):
    flip = SNP_FLIPS[dim]
    pairs = []
    for z, y in SNPS:
        z2, y2 = flip(z, y)
        pairs.append((z * 2 + y, z2 * 2 + y2))
    return lax.ppermute(value, "snp", pairs)


def snp_bits():
    index = lax.axis_index("snp")
    z, y = index // 2, index % 2
    return (jnp.where((z == 1) | (z == 2), 1, 0), jnp.where(z >= 2, 1, 0), y)


ORDERS = ((0, 1, 2), (1, 2, 0), (2, 0, 1))


def cut(value, start, size):
    return lax.dynamic_slice_in_dim(value, start, size, 0)


def join(mine, other, bit):
    rows = mine.shape[0]
    return cut(jnp.concatenate([mine, other, mine], 0), bit * rows, 2 * rows)


PART_ROWS = (768, 640, 640)


def halves(parts, stage, bits):
    sent, kept = [], []
    for part, order in zip(parts, ORDERS):
        half = part.shape[0] // 2
        sent.append(cut(part, (1 - bits[order[stage]]) * half, half))
        kept.append(cut(part, bits[order[stage]] * half, half))
    return sent, kept


def exchange_all(values, stage):
    return [snp_exchange(v, order[stage]) for v, order in zip(values, ORDERS)]


def sum_and_factor(product, diag, pheno):
    bits = snp_bits()
    at, starts = 0, []
    for size in PART_ROWS:
        starts.append(at)
        at += size
    got = []
    for start, size, order in zip(starts, PART_ROWS, ORDERS):
        half = size // 2
        term = snp_exchange(diag, order[0])
        sent = product(start + (1 - bits[order[0]]) * half, half)
        sent, term = tie(sent, term)
        diag = diag + term
        got.append(snp_exchange(sent, order[0]))
    state, pheno = gather_small(diag, pheno)
    parts = []
    for start, size, order, term in zip(starts, PART_ROWS, ORDERS, got):
        half = size // 2
        parts.append(product(start + bits[order[0]] * half, half) + term)
    for stage in (1, 2):
        sent, kept = halves(parts, stage, bits)
        got = exchange_all(sent, stage)
        state, *got = tie(factor_block(stage - 1, state), *got)
        parts = [k + g for k, g in zip(kept, got)]

    got = exchange_all(parts, 2)
    state, *got = tie(factor_block(2, state), *got)
    parts = [join(p, g, bits[order[2]]) for p, g, order in zip(parts, got, ORDERS)]
    got = exchange_all(parts, 1)
    lower, inverse, *got = tie(*factor_block(3, state), *got)
    parts = [join(p, g, bits[order[1]]) for p, g, order in zip(parts, got, ORDERS)]
    parts = [dot_t(part, inverse, HIGHEST) for part in parts]
    got = exchange_all(parts, 0)
    pieces = []
    for start, size, order, part, other in zip(starts, PART_ROWS, ORDERS, parts, got):
        half = size // 2
        bit = bits[order[0]]
        pieces.append((start + bit * half, part))
        pieces.append((start + (1 - bit) * half, other))
    return lower, inverse, pheno, pieces


def gather_small(diag, pheno):
    tile = lax.axis_index("tile")
    x = (tile // 2) % 4
    pheno = jnp.where(tile < 2, pheno, jnp.zeros_like(pheno))
    pheno = pheno + tile_send(pheno, lambda y, xx, c: (1 - y, xx, c))
    rows = diag.shape[0]
    for bit, flip in (
        (x % 2, lambda y, xx, c: (y, xx ^ 1, c)),
        (x // 2, lambda y, xx, c: (y, 3 - xx, c)),
    ):
        other = tile_send(jnp.concatenate([diag, pheno], 0), flip)
        diag = join(diag, other[:rows], bit)
        pheno = pheno + other[rows:]
        rows = 2 * rows
    other = swap_cores(jnp.concatenate([diag, pheno], 0))
    core = tile % 2
    return join(diag, other[:rows], core), join(pheno, other[rows:], core)


def swap_cores(value):
    return tile_send(value, lambda y, x, c: (y, x, 1 - c))


def tie(*values):
    return lax.optimization_barrier(values)


def spread_panels(head, counts):
    tile = lax.axis_index("tile")
    x = (tile // 2) % 4
    below = tile >= 8
    p = [head[i * 32 : (i + 1) * 32] for i in range(8)]
    at = lambda row, col: lambda y, xx, c: (y, xx) == (row, col)
    to = lambda row, col: lambda y, xx, c: (row, col, c)
    ahead = lambda y, xx, c: (y, (xx + 1) % 4, c)
    back = lambda y, xx, c: (y, (xx + 3) % 4, c)
    root = at(0, 0)

    def go_down(own):
        down = tile_send(own, lambda y, xx, c: (1, xx, c), lambda y, xx, c: y == 0)
        return jnp.where(below, down, own)

    far_a = tile_send(p[4], to(0, 1), root)
    far_b = tile_send(p[5], to(0, 3), root)
    near = tile_send(head[64:128], to(0, 1), root)
    behind = tile_send(head[192:256], to(0, 3), root)
    far_a, far_b, counts = tie(far_a, far_b, counts)
    far_a = tile_send(far_a, to(0, 2), at(0, 1))
    far_b = tile_send(far_b, to(0, 2), at(0, 3))
    counts = counts + swap_cores(counts)
    counts = counts + tile_send(counts, lambda y, xx, c: (1 - y, xx, c))
    near, behind, counts = tie(near, behind, counts)
    own_a = jnp.where(x == 0, p[0], jnp.where(x == 1, near[:32], jnp.where(x == 3, behind[:32], far_a)))
    own_b = jnp.where(x == 0, p[1], jnp.where(x == 1, near[32:], jnp.where(x == 3, behind[32:], far_b)))
    own_a = go_down(own_a)
    counts = counts + tile_send(counts, lambda y, xx, c: (y, xx ^ 1, c))
    counts = counts + tile_send(counts, lambda y, xx, c: (y, 3 - xx, c))
    own_b = go_down(own_b)
    own_a, counts = tie(own_a, counts)
    left_a = tile_send(own_a, ahead)
    right_a = tile_send(own_a, back)
    left_b = tile_send(own_b, ahead)
    right_b = tile_send(own_b, back)
    far_a = tile_send(left_a, ahead)
    far_b = tile_send(right_b, back)
    mine = (own_a, own_b, left_a, right_a, left_b, right_b, far_a, far_b)
    return mine, tuple(swap_cores(piece) for piece in mine), counts


PIECES = ((0, 0), (0, 32), (3, 0), (1, 0), (3, 32), (1, 32), (2, 0), (2, 32))


def split(value):
    high = value.astype(jnp.bfloat16)
    return high, (value - high.astype(F32)).astype(jnp.bfloat16)


NT = (((1,), (1,)), ((), ()))


def dot3(a, b):
    total = lax.dot_general(a[0], b[0], NT, preferred_element_type=F32)
    total = total + lax.dot_general(a[0], b[1], NT, preferred_element_type=F32)
    return total + lax.dot_general(a[1], b[0], NT, preferred_element_type=F32)


def standardize_kernel(where_ref, mean_ref, weight_ref, *refs):
    mine, other = refs[:8], refs[8:16]
    diag_ref, panels_ref, own = refs[16:]
    x = where_ref[0]
    core = where_ref[1]
    mean = mean_ref[...]
    weight = weight_ref[...]
    for i, (turn, offset) in enumerate(PIECES):
        at = ((x + turn) % 4) * 64 + offset
        centered = mine[i][...] - mean
        if turn == 0:
            own[offset : offset + 32, :] = centered
        for panel, value in ((core, centered), (1 - core, other[i][...] - mean)):
            panels_ref[pl.ds(pl.multiple_of(panel * BLK + at, 32), 32), :] = value * weight
    diag_ref[...] = dot3(split(own[...]), split(panels_ref[...]))


def standardize_panels(mine, other, mean, weight):
    n = mean.shape[0]
    tile = lax.axis_index("tile")
    where = jnp.stack([(tile // 2) % 4, tile % 2]).astype(jnp.int32)
    vmem = pl.BlockSpec(memory_space=pltpu.VMEM)
    return pl.pallas_call(
        standardize_kernel,
        out_shape=(
            jax.ShapeDtypeStruct((64, 2 * BLK), F32),
            jax.ShapeDtypeStruct((2 * BLK, n), F32),
        ),
        in_specs=[pl.BlockSpec(memory_space=pltpu.SMEM)] + [vmem] * 18,
        out_specs=(vmem, vmem),
        scratch_shapes=[pltpu.VMEM((64, n), F32)],
        compiler_params=pltpu.CompilerParams(vmem_limit_bytes=16 << 20),
        cost_estimate=pl.CostEstimate(flops=1000, bytes_accessed=1000, transcendentals=0),
        name="standardize_panels",
    )(where, mean.reshape(1, n), weight.reshape(1, n), *mine, *other)


def lane_columns(rows, j):
    return [jnp.broadcast_to(rows[:, j + k : j + k + 1], (8, 128)) for k in range(8)]


def factor_leaf(work):
    sub = lax.broadcasted_iota(jnp.int32, (8, 128), 0)
    current = [work[0:8, 0:128], work[0:8, 128:256]]
    for j in range(0, 128, 8):
        last = j == 120
        columns = lane_columns(current[0], j)
        s = {}
        for k in range(8):
            for m in range(k, 8):
                s[m, k] = jnp.broadcast_to(columns[k][m : m + 1, :], (8, 128))
        if not last:
            following = [work[j + 8 : j + 16, 0:128], work[j + 8 : j + 16, 128:256]]
            below = lane_columns(following[0], j)
        scale, low, coefs = [], {}, []
        rows = ([], [])
        for k in range(8):
            scale.append(lax.rsqrt(s[k, k]))
            for m in range(k + 1, 8):
                low[m, k] = s[m, k] * scale[k]
            for n in range(k + 1, 8):
                for m in range(n, 8):
                    s[m, n] = s[m, n] - low[m, k] * low[n, k]
            for h in range(2):
                row = jnp.broadcast_to(current[h][k : k + 1, :], (8, 128))
                for i in range(k):
                    row = row - low[k, i] * rows[h][i]
                rows[h].append(row * scale[k])
            if not last:
                coef = below[k]
                for i in range(k):
                    coef = coef - coefs[i] * low[k, i]
                coefs.append(coef * scale[k])
                for h in range(2):
                    following[h] = following[h] - coefs[k] * rows[h][k]
        solved = []
        for h in range(2):
            block = rows[h][0]
            for m in range(1, 8):
                block = jnp.where(sub == m, rows[h][m], block)
            solved.append(block)
        both = jnp.concatenate(solved, 1)
        work[j : j + 8, :] = both
        if j < 112:
            update = lax.dot_general(
                solved[0], both, (((0,), (0,)), ((), ())), precision=HIGHEST, preferred_element_type=F32
            )
            work[j + 16 : 128, :] = work[j + 16 : 128, :] - update[j + 16 :, :]
        if not last:
            current = following


def factor_step(b, first_ref, aug, work):
    n = aug.shape[0]
    rows = slice(b * 128, b * 128 + 128)
    if b == 0:
        eye = lax.broadcasted_iota(jnp.int32, (n, n), 0) == lax.broadcasted_iota(jnp.int32, (n, n), 1)
        eye = jnp.where(eye, 1.0, 0.0).astype(F32)
        aug[:, 0:n] = first_ref[...] + eye
        aug[:, n : 2 * n] = eye
    else:
        aug[...] = first_ref[...]
    small = lax.broadcasted_iota(jnp.int32, (128, 128), 0) == lax.broadcasted_iota(
        jnp.int32, (128, 128), 1
    )
    work[:, 0:128] = aug[rows, rows]
    work[:, 128:256] = jnp.where(small, 1.0, 0.0).astype(F32)
    factor_leaf(work)
    right = slice(b * 128, n + b * 128 + 128)
    solved = lax.dot_general(
        work[:, 128:256],
        aug[rows, right],
        (((1,), (0,)), ((), ())),
        precision=HIGHEST,
        preferred_element_type=F32,
    )
    aug[rows, right] = solved
    aug[rows, rows] = work[:, 0:128]
    if b < 3:
        below = slice(b * 128 + 128, n)
        aug[below, right] = aug[below, right] - lax.dot_general(
            solved[:, 128 : n - b * 128],
            solved,
            (((0,), (0,)), ((), ())),
            precision=HIGHEST,
            preferred_element_type=F32,
        )


def last_step_kernel(in_ref, lower_ref, inverse_ref, aug, work):
    factor_step(3, in_ref, aug, work)
    n = aug.shape[0]
    row = lax.broadcasted_iota(jnp.int32, (n, n), 0)
    col = lax.broadcasted_iota(jnp.int32, (n, n), 1)
    lower_ref[...] = jnp.where(row >= col, jnp.transpose(aug[:, 0:n]), 0.0)
    inverse_ref[...] = aug[:, n : 2 * n]


def factor_block(b, value):
    n = value.shape[0]
    vmem = pl.BlockSpec(memory_space=pltpu.VMEM)
    work = pltpu.VMEM((128, 256), F32)
    square = jax.ShapeDtypeStruct((n, n), F32)
    if b == 3:
        body, shape, specs = last_step_kernel, (square, square), (vmem, vmem)
        scratch = [pltpu.VMEM((n, 2 * n), F32), work]
    else:
        body = lambda i, o, w: factor_step(b, i, o, w)
        shape, specs, scratch = jax.ShapeDtypeStruct((n, 2 * n), F32), vmem, [work]
    return pl.pallas_call(
        body,
        out_shape=shape,
        in_specs=[vmem],
        out_specs=specs,
        scratch_shapes=scratch,
        compiler_params=pltpu.CompilerParams(vmem_limit_bytes=16 << 20),
        cost_estimate=pl.CostEstimate(flops=7_000_000_000, bytes_accessed=1000, transcendentals=0),
        name="factor_%d" % b,
    )(value)


def dot_t(a, b, precision):
    return lax.dot_general(
        a, b, (((1,), (1,)), ((), ())), precision=precision, preferred_element_type=F32
    )


def output_kernel(where_ref, *refs):
    n_pieces = len(refs) - 10
    pieces = refs[:n_pieces]
    lower_ref, solved_ref, pheno_ref, factor_ref, white_ref, product, pheno, sems, head_sem, pheno_sem = refs[
        n_pieces:
    ]
    tile = where_ref[n_pieces]
    fetch = pltpu.make_async_copy(pheno_ref, pheno, pheno_sem)
    fetch.start()
    copies = []
    for i, piece in enumerate(pieces):
        rows = piece.shape[0]
        at = pl.multiple_of(where_ref[i], 64)
        copy = pltpu.make_async_copy(piece, factor_ref.at[pl.ds(at, rows), :], sems.at[i])
        copy.start()
        copies.append(copy)
    n = solved_ref.shape[1]
    solved_high, solved_low = split(solved_ref[...])
    solved = jnp.concatenate([solved_high, solved_low], 1)
    for i, piece in enumerate(pieces):
        rows = piece.shape[0]
        at = pl.multiple_of(where_ref[i], 64)
        high, low = split(piece[...])
        total = jnp.dot(high, solved, preferred_element_type=F32)
        total = total[:, :n] + total[:, n:]
        product[pl.ds(at, rows), :] = total + jnp.dot(low, solved_high, preferred_element_type=F32)
    fetch.wait()
    white_ref[...] = pheno[...] - jnp.transpose(product[...])
    for copy in copies:
        copy.wait()
    for panel in range(2):

        @pl.when(tile == panel)
        def _():
            own = slice(panel * BLK, panel * BLK + BLK)
            head = pltpu.make_async_copy(lower_ref.at[own, :], factor_ref.at[0:BLK, :], head_sem)
            head.start()
            white_ref[:, 0:BLK] = jnp.transpose(solved_ref[own, :])
            head.wait()


def write_outputs(pieces, lower, solved, pheno):
    n_pheno, rows = pheno.shape
    where = jnp.stack([at for at, _ in pieces] + [lax.axis_index("tile")]).astype(jnp.int32)
    vmem = pl.BlockSpec(memory_space=pltpu.VMEM)
    anywhere = pl.BlockSpec(memory_space=pl.ANY)
    return pl.pallas_call(
        output_kernel,
        out_shape=(
            jax.ShapeDtypeStruct((rows, 2 * BLK), F32),
            jax.ShapeDtypeStruct((n_pheno, rows), F32),
        ),
        in_specs=[pl.BlockSpec(memory_space=pltpu.SMEM)] + [vmem] * len(pieces) + [anywhere, vmem, anywhere],
        out_specs=(anywhere, vmem),
        scratch_shapes=[
            pltpu.VMEM((rows, n_pheno), F32),
            pltpu.VMEM((n_pheno, rows), F32),
            pltpu.SemaphoreType.DMA((len(pieces),)),
            pltpu.SemaphoreType.DMA,
            pltpu.SemaphoreType.DMA,
        ],
        compiler_params=pltpu.CompilerParams(vmem_limit_bytes=12 << 20),
        cost_estimate=pl.CostEstimate(flops=500_000_000, bytes_accessed=10 << 20, transcendentals=0),
        name="write_outputs",
    )(where, *[p for _, p in pieces], lower, solved, pheno)


def body(dosages, phenotypes):
    n_tile = lax.axis_size("tile")
    n_snp = lax.axis_size("snp")
    rows, snps = dosages.shape
    width = BLK
    tile_index = lax.axis_index("tile")

    counts = jnp.sum(dosages, axis=0)
    mine, other, counts = spread_panels(dosages[:width], counts.reshape(16, 128))
    flipped = phenotypes.T
    head = flipped[:, :width]
    head = jnp.concatenate([head[:32], head[32:]], 1)

    counts = counts.reshape(snps)
    allele_freq = counts / (2.0 * rows * n_tile)
    spread = jnp.maximum(2.0 * allele_freq * (1.0 - allele_freq), 0.05)
    mean = 2.0 * allele_freq
    weight = (1.0 / (snps * n_snp)) / spread
    diag, panels = standardize_panels(mine, other, mean, weight)

    def product(start, size):
        return dot_t(cut(dosages, start, size) - mean, panels, HIGH)

    lower, inverse, heads, pieces = sum_and_factor(product, diag, head)
    panel_pheno = jnp.concatenate(
        [
            jnp.concatenate([heads[:32, :width], heads[32:, :width]], 1),
            jnp.concatenate([heads[:32, width:], heads[32:, width:]], 1),
        ],
        0,
    )
    solved = dot_t(inverse, panel_pheno, HIGHEST)
    factor, whitened = write_outputs(pieces, lower, solved, flipped)
    return factor, whitened.T


def solution(mesh):
    placed = (P("tile", "snp"), P("tile", "snp"))
    return jax.shard_map(
        body,
        mesh=mesh,
        in_specs=placed,
        out_specs=(P("tile", None), P("tile", "snp")),
        check_vma=False,
    )
```

```python
import jax
import jax.numpy as jnp
from jax import lax
from jax.experimental import pallas as pl
from jax.experimental.pallas import tpu as pltpu
from jax.sharding import PartitionSpec as P

BLK = 256
HIGHEST = lax.Precision.HIGHEST
HIGH = lax.Precision.HIGH
F32 = jnp.float32

TILES = [(y, x, c) for y in range(2) for x in range(4) for c in range(2)]
SNPS = [(z, y) for z in range(4) for y in range(2)]


def tile_id(y, x, c):
    return (y * 4 + x) * 2 + c


def tile_send(value, target, only=None):
    pairs = [
        (tile_id(*a), tile_id(*target(*a))) for a in TILES if only is None or only(*a)
    ]
    return lax.ppermute(value, "tile", pairs)


SNP_FLIPS = (
    lambda z, y: (z ^ 1, y),
    lambda z, y: (3 - z, y),
    lambda z, y: (z, 1 - y),
)


def snp_exchange(value, dim):
    flip = SNP_FLIPS[dim]
    pairs = []
    for z, y in SNPS:
        z2, y2 = flip(z, y)
        pairs.append((z * 2 + y, z2 * 2 + y2))
    return lax.ppermute(value, "snp", pairs)


def snp_bits():
    index = lax.axis_index("snp")
    z, y = index // 2, index % 2
    return (jnp.where((z == 1) | (z == 2), 1, 0), jnp.where(z >= 2, 1, 0), y)


ORDERS = ((0, 1, 2), (1, 2, 0), (2, 0, 1))


def cut(value, start, size):
    return lax.dynamic_slice_in_dim(value, start, size, 0)


def join(mine, other, bit):
    rows = mine.shape[0]
    return cut(jnp.concatenate([mine, other, mine], 0), bit * rows, 2 * rows)


PART_ROWS = (768, 640, 640)


def halves(parts, stage, bits):
    sent, kept = [], []
    for part, order in zip(parts, ORDERS):
        half = part.shape[0] // 2
        sent.append(cut(part, (1 - bits[order[stage]]) * half, half))
        kept.append(cut(part, bits[order[stage]] * half, half))
    return sent, kept


def exchange_all(values, stage):
    return [snp_exchange(v, order[stage]) for v, order in zip(values, ORDERS)]


def sum_and_factor(product, diag, pheno):
    bits = snp_bits()
    at, starts = 0, []
    for size in PART_ROWS:
        starts.append(at)
        at += size
    got = []
    for start, size, order in zip(starts, PART_ROWS, ORDERS):
        half = size // 2
        term = snp_exchange(diag, order[0])
        sent = product(start + (1 - bits[order[0]]) * half, half)
        sent, term = tie(sent, term)
        diag = diag + term
        got.append(snp_exchange(sent, order[0]))
    kept = []
    for start, size, order in zip(starts, PART_ROWS, ORDERS):
        half = size // 2
        kept.append(product(start + bits[order[0]] * half, half, diag))
    state, pheno, kept = gather_small(diag, pheno, kept)
    parts = [k + g for k, g in zip(kept, got)]
    for stage in (1, 2):
        sent, kept = halves(parts, stage, bits)
        got = exchange_all(sent, stage)
        state, *got = tie(factor_block(stage - 1, state), *got)
        parts = [k + g for k, g in zip(kept, got)]

    got = exchange_all(parts, 2)
    state, *got = tie(factor_block(2, state), *got)
    parts = [join(p, g, bits[order[2]]) for p, g, order in zip(parts, got, ORDERS)]
    got = exchange_all(parts, 1)
    lower, inverse, *got = tie(*factor_block(3, state), *got)
    parts = [join(p, g, bits[order[1]]) for p, g, order in zip(parts, got, ORDERS)]
    parts = [dot_t(part, inverse, HIGHEST) for part in parts]
    got = exchange_all(parts, 0)
    pieces = []
    for start, size, order, part, other in zip(starts, PART_ROWS, ORDERS, parts, got):
        half = size // 2
        bit = bits[order[0]]
        pieces.append((start + bit * half, part))
        pieces.append((start + (1 - bit) * half, other))
    return lower, inverse, pheno, pieces


def gather_small(diag, pheno, beside):
    beside = list(beside)
    tile = lax.axis_index("tile")
    x = (tile // 2) % 4
    pheno = jnp.where(tile < 2, pheno, jnp.zeros_like(pheno))
    pheno = pheno + tile_send(pheno, lambda y, xx, c: (1 - y, xx, c))
    rows = diag.shape[0]
    for i, (bit, flip) in enumerate(
        (
            (x % 2, lambda y, xx, c: (y, xx ^ 1, c)),
            (x // 2, lambda y, xx, c: (y, 3 - xx, c)),
        )
    ):
        other = tile_send(jnp.concatenate([diag, pheno], 0), flip)
        other, beside[i] = tie(other, beside[i])
        diag = join(diag, other[:rows], bit)
        pheno = pheno + other[rows:]
        rows = 2 * rows
    other = swap_cores(jnp.concatenate([diag, pheno], 0))
    other, beside[2] = tie(other, beside[2])
    core = tile % 2
    return join(diag, other[:rows], core), join(pheno, other[rows:], core), beside


def swap_cores(value):
    return tile_send(value, lambda y, x, c: (y, x, 1 - c))


def tie(*values):
    return lax.optimization_barrier(values)


def spread_panels(head, counts):
    tile = lax.axis_index("tile")
    x = (tile // 2) % 4
    below = tile >= 8
    p = [head[i * 32 : (i + 1) * 32] for i in range(8)]
    at = lambda row, col: lambda y, xx, c: (y, xx) == (row, col)
    to = lambda row, col: lambda y, xx, c: (row, col, c)
    ahead = lambda y, xx, c: (y, (xx + 1) % 4, c)
    back = lambda y, xx, c: (y, (xx + 3) % 4, c)
    root = at(0, 0)

    def go_down(own):
        down = tile_send(own, lambda y, xx, c: (1, xx, c), lambda y, xx, c: y == 0)
        return jnp.where(below, down, own)

    far_a = tile_send(p[4], to(0, 1), root)
    far_b = tile_send(p[5], to(0, 3), root)
    near = tile_send(head[64:128], to(0, 1), root)
    behind = tile_send(head[192:256], to(0, 3), root)
    far_a, far_b, counts = tie(far_a, far_b, counts)
    far_a = tile_send(far_a, to(0, 2), at(0, 1))
    far_b = tile_send(far_b, to(0, 2), at(0, 3))
    counts = counts + swap_cores(counts)
    counts = counts + tile_send(counts, lambda y, xx, c: (1 - y, xx, c))
    near, behind, counts = tie(near, behind, counts)
    own_a = jnp.where(x == 0, p[0], jnp.where(x == 1, near[:32], jnp.where(x == 3, behind[:32], far_a)))
    own_b = jnp.where(x == 0, p[1], jnp.where(x == 1, near[32:], jnp.where(x == 3, behind[32:], far_b)))
    own_a = go_down(own_a)
    counts = counts + tile_send(counts, lambda y, xx, c: (y, xx ^ 1, c))
    counts = counts + tile_send(counts, lambda y, xx, c: (y, 3 - xx, c))
    own_b = go_down(own_b)
    own_a, counts = tie(own_a, counts)
    left_a = tile_send(own_a, ahead)
    right_a = tile_send(own_a, back)
    left_b = tile_send(own_b, ahead)
    right_b = tile_send(own_b, back)
    far_a = tile_send(left_a, ahead)
    far_b = tile_send(right_b, back)
    mine = (own_a, own_b, left_a, right_a, left_b, right_b, far_a, far_b)
    return mine, tuple(swap_cores(piece) for piece in mine), counts


PIECES = ((0, 0), (0, 32), (3, 0), (1, 0), (3, 32), (1, 32), (2, 0), (2, 32))


def split(value):
    high = value.astype(jnp.bfloat16)
    return high, (value - high.astype(F32)).astype(jnp.bfloat16)


NT = (((1,), (1,)), ((), ()))


def dot3(a, b):
    total = lax.dot_general(a[0], b[0], NT, preferred_element_type=F32)
    total = total + lax.dot_general(a[0], b[1], NT, preferred_element_type=F32)
    return total + lax.dot_general(a[1], b[0], NT, preferred_element_type=F32)


def standardize_kernel(where_ref, mean_ref, weight_ref, *refs):
    mine, other = refs[:8], refs[8:16]
    diag_ref, panels_ref, own = refs[16:]
    x = where_ref[0]
    core = where_ref[1]
    mean = mean_ref[...]
    weight = weight_ref[...]
    for i, (turn, offset) in enumerate(PIECES):
        at = ((x + turn) % 4) * 64 + offset
        centered = mine[i][...] - mean
        if turn == 0:
            own[offset : offset + 32, :] = centered
        for panel, value in ((core, centered), (1 - core, other[i][...] - mean)):
            panels_ref[pl.ds(pl.multiple_of(panel * BLK + at, 32), 32), :] = value * weight
    diag_ref[...] = dot3(split(own[...]), split(panels_ref[...]))


def standardize_panels(mine, other, mean, weight):
    n = mean.shape[0]
    tile = lax.axis_index("tile")
    where = jnp.stack([(tile // 2) % 4, tile % 2]).astype(jnp.int32)
    vmem = pl.BlockSpec(memory_space=pltpu.VMEM)
    return pl.pallas_call(
        standardize_kernel,
        out_shape=(
            jax.ShapeDtypeStruct((64, 2 * BLK), F32),
            jax.ShapeDtypeStruct((2 * BLK, n), F32),
        ),
        in_specs=[pl.BlockSpec(memory_space=pltpu.SMEM)] + [vmem] * 18,
        out_specs=(vmem, vmem),
        scratch_shapes=[pltpu.VMEM((64, n), F32)],
        compiler_params=pltpu.CompilerParams(vmem_limit_bytes=16 << 20),
        cost_estimate=pl.CostEstimate(flops=1000, bytes_accessed=1000, transcendentals=0),
        name="standardize_panels",
    )(where, mean.reshape(1, n), weight.reshape(1, n), *mine, *other)


def lane_columns(rows, j):
    return [jnp.broadcast_to(rows[:, j + k : j + k + 1], (8, 128)) for k in range(8)]


def factor_leaf(work):
    sub = lax.broadcasted_iota(jnp.int32, (8, 128), 0)
    current = [work[0:8, 0:128], work[0:8, 128:256]]
    for j in range(0, 128, 8):
        last = j == 120
        columns = lane_columns(current[0], j)
        s = {}
        for k in range(8):
            for m in range(k, 8):
                s[m, k] = jnp.broadcast_to(columns[k][m : m + 1, :], (8, 128))
        if not last:
            following = [work[j + 8 : j + 16, 0:128], work[j + 8 : j + 16, 128:256]]
            below = lane_columns(following[0], j)
        scale, low, coefs = [], {}, []
        rows = ([], [])
        for k in range(8):
            scale.append(lax.rsqrt(s[k, k]))
            for m in range(k + 1, 8):
                low[m, k] = s[m, k] * scale[k]
            for n in range(k + 1, 8):
                for m in range(n, 8):
                    s[m, n] = s[m, n] - low[m, k] * low[n, k]
            for h in range(2):
                row = jnp.broadcast_to(current[h][k : k + 1, :], (8, 128))
                for i in range(k):
                    row = row - low[k, i] * rows[h][i]
                rows[h].append(row * scale[k])
            if not last:
                coef = below[k]
                for i in range(k):
                    coef = coef - coefs[i] * low[k, i]
                coefs.append(coef * scale[k])
                for h in range(2):
                    following[h] = following[h] - coefs[k] * rows[h][k]
        solved = []
        for h in range(2):
            block = rows[h][0]
            for m in range(1, 8):
                block = jnp.where(sub == m, rows[h][m], block)
            solved.append(block)
        both = jnp.concatenate(solved, 1)
        work[j : j + 8, :] = both
        if j < 112:
            update = lax.dot_general(
                solved[0], both, (((0,), (0,)), ((), ())), precision=HIGHEST, preferred_element_type=F32
            )
            work[j + 16 : 128, :] = work[j + 16 : 128, :] - update[j + 16 :, :]
        if not last:
            current = following


def factor_step(b, first_ref, aug, work):
    n = aug.shape[0]
    rows = slice(b * 128, b * 128 + 128)
    if b == 0:
        eye = lax.broadcasted_iota(jnp.int32, (n, n), 0) == lax.broadcasted_iota(jnp.int32, (n, n), 1)
        eye = jnp.where(eye, 1.0, 0.0).astype(F32)
        aug[:, 0:n] = first_ref[...] + eye
        aug[:, n : 2 * n] = eye
    else:
        aug[...] = first_ref[...]
    small = lax.broadcasted_iota(jnp.int32, (128, 128), 0) == lax.broadcasted_iota(
        jnp.int32, (128, 128), 1
    )
    work[:, 0:128] = aug[rows, rows]
    work[:, 128:256] = jnp.where(small, 1.0, 0.0).astype(F32)
    factor_leaf(work)
    right = slice(b * 128, n + b * 128 + 128)
    solved = lax.dot_general(
        work[:, 128:256],
        aug[rows, right],
        (((1,), (0,)), ((), ())),
        precision=HIGHEST,
        preferred_element_type=F32,
    )
    aug[rows, right] = solved
    aug[rows, rows] = work[:, 0:128]
    if b < 3:
        below = slice(b * 128 + 128, n)
        aug[below, right] = aug[below, right] - lax.dot_general(
            solved[:, 128 : n - b * 128],
            solved,
            (((0,), (0,)), ((), ())),
            precision=HIGHEST,
            preferred_element_type=F32,
        )


def last_step_kernel(in_ref, lower_ref, inverse_ref, aug, work):
    factor_step(3, in_ref, aug, work)
    n = aug.shape[0]
    row = lax.broadcasted_iota(jnp.int32, (n, n), 0)
    col = lax.broadcasted_iota(jnp.int32, (n, n), 1)
    lower_ref[...] = jnp.where(row >= col, jnp.transpose(aug[:, 0:n]), 0.0)
    inverse_ref[...] = aug[:, n : 2 * n]


def factor_block(b, value):
    n = value.shape[0]
    vmem = pl.BlockSpec(memory_space=pltpu.VMEM)
    work = pltpu.VMEM((128, 256), F32)
    square = jax.ShapeDtypeStruct((n, n), F32)
    if b == 3:
        body, shape, specs = last_step_kernel, (square, square), (vmem, vmem)
        scratch = [pltpu.VMEM((n, 2 * n), F32), work]
    else:
        body = lambda i, o, w: factor_step(b, i, o, w)
        shape, specs, scratch = jax.ShapeDtypeStruct((n, 2 * n), F32), vmem, [work]
    return pl.pallas_call(
        body,
        out_shape=shape,
        in_specs=[vmem],
        out_specs=specs,
        scratch_shapes=scratch,
        compiler_params=pltpu.CompilerParams(vmem_limit_bytes=16 << 20),
        cost_estimate=pl.CostEstimate(flops=7_000_000_000, bytes_accessed=1000, transcendentals=0),
        name="factor_%d" % b,
    )(value)


def dot_t(a, b, precision):
    return lax.dot_general(
        a, b, (((1,), (1,)), ((), ())), precision=precision, preferred_element_type=F32
    )


def output_kernel(where_ref, *refs):
    n_pieces = len(refs) - 10
    pieces = refs[:n_pieces]
    lower_ref, solved_ref, pheno_ref, factor_ref, white_ref, product, pheno, sems, head_sem, pheno_sem = refs[
        n_pieces:
    ]
    tile = where_ref[n_pieces]
    fetch = pltpu.make_async_copy(pheno_ref, pheno, pheno_sem)
    fetch.start()
    copies = []
    for i, piece in enumerate(pieces):
        rows = piece.shape[0]
        at = pl.multiple_of(where_ref[i], 64)
        copy = pltpu.make_async_copy(piece, factor_ref.at[pl.ds(at, rows), :], sems.at[i])
        copy.start()
        copies.append(copy)
    n = solved_ref.shape[1]
    solved_high, solved_low = split(solved_ref[...])
    solved = jnp.concatenate([solved_high, solved_low], 1)
    for i, piece in enumerate(pieces):
        rows = piece.shape[0]
        at = pl.multiple_of(where_ref[i], 64)
        high, low = split(piece[...])
        total = jnp.dot(high, solved, preferred_element_type=F32)
        total = total[:, :n] + total[:, n:]
        product[pl.ds(at, rows), :] = total + jnp.dot(low, solved_high, preferred_element_type=F32)
    fetch.wait()
    white_ref[...] = pheno[...] - jnp.transpose(product[...])
    for copy in copies:
        copy.wait()
    for panel in range(2):

        @pl.when(tile == panel)
        def _():
            own = slice(panel * BLK, panel * BLK + BLK)
            head = pltpu.make_async_copy(lower_ref.at[own, :], factor_ref.at[0:BLK, :], head_sem)
            head.start()
            white_ref[:, 0:BLK] = jnp.transpose(solved_ref[own, :])
            head.wait()


def write_outputs(pieces, lower, solved, pheno):
    n_pheno, rows = pheno.shape
    where = jnp.stack([at for at, _ in pieces] + [lax.axis_index("tile")]).astype(jnp.int32)
    vmem = pl.BlockSpec(memory_space=pltpu.VMEM)
    anywhere = pl.BlockSpec(memory_space=pl.ANY)
    return pl.pallas_call(
        output_kernel,
        out_shape=(
            jax.ShapeDtypeStruct((rows, 2 * BLK), F32),
            jax.ShapeDtypeStruct((n_pheno, rows), F32),
        ),
        in_specs=[pl.BlockSpec(memory_space=pltpu.SMEM)] + [vmem] * len(pieces) + [anywhere, vmem, anywhere],
        out_specs=(anywhere, vmem),
        scratch_shapes=[
            pltpu.VMEM((rows, n_pheno), F32),
            pltpu.VMEM((n_pheno, rows), F32),
            pltpu.SemaphoreType.DMA((len(pieces),)),
            pltpu.SemaphoreType.DMA,
            pltpu.SemaphoreType.DMA,
        ],
        compiler_params=pltpu.CompilerParams(vmem_limit_bytes=12 << 20),
        cost_estimate=pl.CostEstimate(flops=500_000_000, bytes_accessed=10 << 20, transcendentals=0),
        name="write_outputs",
    )(where, *[p for _, p in pieces], lower, solved, pheno)


def body(dosages, phenotypes):
    n_tile = lax.axis_size("tile")
    n_snp = lax.axis_size("snp")
    rows, snps = dosages.shape
    width = BLK
    tile_index = lax.axis_index("tile")

    counts = jnp.sum(dosages, axis=0)
    mine, other, counts = spread_panels(dosages[:width], counts.reshape(16, 128))
    flipped = phenotypes.T
    head = flipped[:, :width]
    head = jnp.concatenate([head[:32], head[32:]], 1)

    counts = counts.reshape(snps)
    allele_freq = counts / (2.0 * rows * n_tile)
    spread = jnp.maximum(2.0 * allele_freq * (1.0 - allele_freq), 0.05)
    mean = 2.0 * allele_freq
    weight = (1.0 / (snps * n_snp)) / spread
    diag, panels = standardize_panels(mine, other, mean, weight)

    def product(start, size, later=None):
        right = panels if later is None else tie(panels, later)[0]
        return dot_t(cut(dosages, start, size) - mean, right, HIGH)

    diag, head = tie(diag, head)
    lower, inverse, heads, pieces = sum_and_factor(product, diag, head)
    panel_pheno = jnp.concatenate(
        [
            jnp.concatenate([heads[:32, :width], heads[32:, :width]], 1),
            jnp.concatenate([heads[:32, width:], heads[32:, width:]], 1),
        ],
        0,
    )
    solved = dot_t(inverse, panel_pheno, HIGHEST)
    factor, whitened = write_outputs(pieces, lower, solved, flipped)
    return factor, whitened.T


def solution(mesh):
    placed = (P("tile", "snp"), P("tile", "snp"))
    return jax.shard_map(
        body,
        mesh=mesh,
        in_specs=placed,
        out_specs=(P("tile", None), P("tile", "snp")),
        check_vma=False,
    )
```

```python
import jax
import jax.numpy as jnp
from jax import lax
from jax.experimental import pallas as pl
from jax.experimental.pallas import tpu as pltpu
from jax.sharding import PartitionSpec as P

BLK = 256
HIGHEST = lax.Precision.HIGHEST
HIGH = lax.Precision.HIGH
F32 = jnp.float32

TILES = [(y, x, c) for y in range(2) for x in range(4) for c in range(2)]
SNPS = [(z, y) for z in range(4) for y in range(2)]


def tile_id(y, x, c):
    return (y * 4 + x) * 2 + c


def tile_send(value, target, only=None):
    pairs = [
        (tile_id(*a), tile_id(*target(*a))) for a in TILES if only is None or only(*a)
    ]
    return lax.ppermute(value, "tile", pairs)


SNP_FLIPS = (
    lambda z, y: (z ^ 1, y),
    lambda z, y: (3 - z, y),
    lambda z, y: (z, 1 - y),
)


def snp_exchange(value, dim):
    flip = SNP_FLIPS[dim]
    pairs = []
    for z, y in SNPS:
        z2, y2 = flip(z, y)
        pairs.append((z * 2 + y, z2 * 2 + y2))
    return lax.ppermute(value, "snp", pairs)


def snp_bits():
    index = lax.axis_index("snp")
    z, y = index // 2, index % 2
    return (jnp.where((z == 1) | (z == 2), 1, 0), jnp.where(z >= 2, 1, 0), y)


ORDERS = ((0, 1, 2), (1, 2, 0), (2, 0, 1))


def cut(value, start, size):
    return lax.dynamic_slice_in_dim(value, start, size, 0)


def join(mine, other, bit):
    rows = mine.shape[0]
    return cut(jnp.concatenate([mine, other, mine], 0), bit * rows, 2 * rows)


PART_ROWS = (768, 640, 640)


def halves(parts, stage, bits):
    sent, kept = [], []
    for part, order in zip(parts, ORDERS):
        half = part.shape[0] // 2
        sent.append(cut(part, (1 - bits[order[stage]]) * half, half))
        kept.append(cut(part, bits[order[stage]] * half, half))
    return sent, kept


def exchange_all(values, stage):
    return [snp_exchange(v, order[stage]) for v, order in zip(values, ORDERS)]


def sum_and_factor(product, diag, pheno):
    bits = snp_bits()
    at, starts = 0, []
    for size in PART_ROWS:
        starts.append(at)
        at += size
    got = []
    for start, size, order in zip(starts, PART_ROWS, ORDERS):
        half = size // 2
        term = snp_exchange(diag, order[0])
        sent = product(start + (1 - bits[order[0]]) * half, half)
        sent, term = tie(sent, term)
        diag = diag + term
        if not got:
            diag, pheno = tie(diag, pheno)
        got.append(snp_exchange(sent, order[0]))
    kept = []
    for start, size, order in zip(starts, PART_ROWS, ORDERS):
        half = size // 2
        kept.append(product(start + bits[order[0]] * half, half, diag))
    state, pheno, kept = gather_small(diag, pheno, kept)
    parts = [k + g for k, g in zip(kept, got)]
    for stage in (1, 2):
        sent, kept = halves(parts, stage, bits)
        got = exchange_all(sent, stage)
        state, *got = tie(factor_block(stage - 1, state), *got)
        parts = [k + g for k, g in zip(kept, got)]

    got = exchange_all(parts, 2)
    state, *got = tie(factor_block(2, state), *got)
    parts = [join(p, g, bits[order[2]]) for p, g, order in zip(parts, got, ORDERS)]
    got = exchange_all(parts, 1)
    lower, inverse, *got = tie(*factor_block(3, state), *got)
    parts = [join(p, g, bits[order[1]]) for p, g, order in zip(parts, got, ORDERS)]
    parts = [dot_t(part, inverse, HIGHEST) for part in parts]
    got = exchange_all(parts, 0)
    pieces = []
    for start, size, order, part, other in zip(starts, PART_ROWS, ORDERS, parts, got):
        half = size // 2
        bit = bits[order[0]]
        pieces.append((start + bit * half, part))
        pieces.append((start + (1 - bit) * half, other))
    return lower, inverse, pheno, pieces


def gather_small(diag, pheno, beside):
    beside = list(beside)
    tile = lax.axis_index("tile")
    x = (tile // 2) % 4
    pheno = jnp.where(tile < 2, pheno, jnp.zeros_like(pheno))
    pheno = pheno + tile_send(pheno, lambda y, xx, c: (1 - y, xx, c))
    rows = diag.shape[0]
    for i, (bit, flip) in enumerate(
        (
            (x % 2, lambda y, xx, c: (y, xx ^ 1, c)),
            (x // 2, lambda y, xx, c: (y, 3 - xx, c)),
        )
    ):
        other = tile_send(jnp.concatenate([diag, pheno], 0), flip)
        other, beside[i] = tie(other, beside[i])
        diag = join(diag, other[:rows], bit)
        pheno = pheno + other[rows:]
        rows = 2 * rows
    other = swap_cores(jnp.concatenate([diag, pheno], 0))
    other, beside[2] = tie(other, beside[2])
    core = tile % 2
    return join(diag, other[:rows], core), join(pheno, other[rows:], core), beside


def swap_cores(value):
    return tile_send(value, lambda y, x, c: (y, x, 1 - c))


def tie(*values):
    return lax.optimization_barrier(values)


def spread_panels(head, counts):
    tile = lax.axis_index("tile")
    x = (tile // 2) % 4
    below = tile >= 8
    p = [head[i * 32 : (i + 1) * 32] for i in range(8)]
    at = lambda row, col: lambda y, xx, c: (y, xx) == (row, col)
    to = lambda row, col: lambda y, xx, c: (row, col, c)
    ahead = lambda y, xx, c: (y, (xx + 1) % 4, c)
    back = lambda y, xx, c: (y, (xx + 3) % 4, c)
    root = at(0, 0)

    def go_down(own):
        down = tile_send(own, lambda y, xx, c: (1, xx, c), lambda y, xx, c: y == 0)
        return jnp.where(below, down, own)

    far_a = tile_send(p[4], to(0, 1), root)
    far_b = tile_send(p[5], to(0, 3), root)
    near = tile_send(head[64:128], to(0, 1), root)
    behind = tile_send(head[192:256], to(0, 3), root)
    far_a, far_b, counts = tie(far_a, far_b, counts)
    far_a = tile_send(far_a, to(0, 2), at(0, 1))
    far_b = tile_send(far_b, to(0, 2), at(0, 3))
    counts = counts + swap_cores(counts)
    counts = counts + tile_send(counts, lambda y, xx, c: (1 - y, xx, c))
    near, behind, counts = tie(near, behind, counts)
    own_a = jnp.where(x == 0, p[0], jnp.where(x == 1, near[:32], jnp.where(x == 3, behind[:32], far_a)))
    own_b = jnp.where(x == 0, p[1], jnp.where(x == 1, near[32:], jnp.where(x == 3, behind[32:], far_b)))
    own_a = go_down(own_a)
    counts = counts + tile_send(counts, lambda y, xx, c: (y, xx ^ 1, c))
    counts = counts + tile_send(counts, lambda y, xx, c: (y, 3 - xx, c))
    own_b = go_down(own_b)
    own_a, counts = tie(own_a, counts)
    left_a = tile_send(own_a, ahead)
    right_a = tile_send(own_a, back)
    left_b = tile_send(own_b, ahead)
    right_b = tile_send(own_b, back)
    far_a = tile_send(left_a, ahead)
    far_b = tile_send(right_b, back)
    mine = (own_a, own_b, left_a, right_a, left_b, right_b, far_a, far_b)
    return mine, tuple(swap_cores(piece) for piece in mine), counts


PIECES = ((0, 0), (0, 32), (3, 0), (1, 0), (3, 32), (1, 32), (2, 0), (2, 32))


def split(value):
    high = value.astype(jnp.bfloat16)
    return high, (value - high.astype(F32)).astype(jnp.bfloat16)


NT = (((1,), (1,)), ((), ()))


def dot3(a, b):
    total = lax.dot_general(a[0], b[0], NT, preferred_element_type=F32)
    total = total + lax.dot_general(a[0], b[1], NT, preferred_element_type=F32)
    return total + lax.dot_general(a[1], b[0], NT, preferred_element_type=F32)


def standardize_kernel(where_ref, mean_ref, weight_ref, *refs):
    mine, other = refs[:8], refs[8:16]
    diag_ref, panels_ref, own = refs[16:]
    x = where_ref[0]
    core = where_ref[1]
    mean = mean_ref[...]
    weight = weight_ref[...]
    for i, (turn, offset) in enumerate(PIECES):
        at = ((x + turn) % 4) * 64 + offset
        centered = mine[i][...] - mean
        if turn == 0:
            own[offset : offset + 32, :] = centered
        for panel, value in ((core, centered), (1 - core, other[i][...] - mean)):
            panels_ref[pl.ds(pl.multiple_of(panel * BLK + at, 32), 32), :] = value * weight
    diag_ref[...] = dot3(split(own[...]), split(panels_ref[...]))


def standardize_panels(mine, other, mean, weight):
    n = mean.shape[0]
    tile = lax.axis_index("tile")
    where = jnp.stack([(tile // 2) % 4, tile % 2]).astype(jnp.int32)
    vmem = pl.BlockSpec(memory_space=pltpu.VMEM)
    return pl.pallas_call(
        standardize_kernel,
        out_shape=(
            jax.ShapeDtypeStruct((64, 2 * BLK), F32),
            jax.ShapeDtypeStruct((2 * BLK, n), F32),
        ),
        in_specs=[pl.BlockSpec(memory_space=pltpu.SMEM)] + [vmem] * 18,
        out_specs=(vmem, vmem),
        scratch_shapes=[pltpu.VMEM((64, n), F32)],
        compiler_params=pltpu.CompilerParams(vmem_limit_bytes=16 << 20),
        cost_estimate=pl.CostEstimate(flops=1000, bytes_accessed=1000, transcendentals=0),
        name="standardize_panels",
    )(where, mean.reshape(1, n), weight.reshape(1, n), *mine, *other)


def lane_columns(rows, j):
    return [jnp.broadcast_to(rows[:, j + k : j + k + 1], (8, 128)) for k in range(8)]


def factor_leaf(work):
    sub = lax.broadcasted_iota(jnp.int32, (8, 128), 0)
    current = [work[0:8, 0:128], work[0:8, 128:256]]
    for j in range(0, 128, 8):
        last = j == 120
        columns = lane_columns(current[0], j)
        s = {}
        for k in range(8):
            for m in range(k, 8):
                s[m, k] = jnp.broadcast_to(columns[k][m : m + 1, :], (8, 128))
        if not last:
            following = [work[j + 8 : j + 16, 0:128], work[j + 8 : j + 16, 128:256]]
            below = lane_columns(following[0], j)
        scale, low, coefs = [], {}, []
        rows = ([], [])
        for k in range(8):
            scale.append(lax.rsqrt(s[k, k]))
            for m in range(k + 1, 8):
                low[m, k] = s[m, k] * scale[k]
            for n in range(k + 1, 8):
                for m in range(n, 8):
                    s[m, n] = s[m, n] - low[m, k] * low[n, k]
            for h in range(2):
                row = jnp.broadcast_to(current[h][k : k + 1, :], (8, 128))
                for i in range(k):
                    row = row - low[k, i] * rows[h][i]
                rows[h].append(row * scale[k])
            if not last:
                coef = below[k]
                for i in range(k):
                    coef = coef - coefs[i] * low[k, i]
                coefs.append(coef * scale[k])
                for h in range(2):
                    following[h] = following[h] - coefs[k] * rows[h][k]
        solved = []
        for h in range(2):
            block = rows[h][0]
            for m in range(1, 8):
                block = jnp.where(sub == m, rows[h][m], block)
            solved.append(block)
        both = jnp.concatenate(solved, 1)
        work[j : j + 8, :] = both
        if j < 112:
            update = lax.dot_general(
                solved[0], both, (((0,), (0,)), ((), ())), precision=HIGHEST, preferred_element_type=F32
            )
            work[j + 16 : 128, :] = work[j + 16 : 128, :] - update[j + 16 :, :]
        if not last:
            current = following


def factor_step(b, first_ref, aug, work):
    n = aug.shape[0]
    rows = slice(b * 128, b * 128 + 128)
    if b == 0:
        eye = lax.broadcasted_iota(jnp.int32, (n, n), 0) == lax.broadcasted_iota(jnp.int32, (n, n), 1)
        eye = jnp.where(eye, 1.0, 0.0).astype(F32)
        aug[:, 0:n] = first_ref[...] + eye
        aug[:, n : 2 * n] = eye
    else:
        aug[...] = first_ref[...]
    small = lax.broadcasted_iota(jnp.int32, (128, 128), 0) == lax.broadcasted_iota(
        jnp.int32, (128, 128), 1
    )
    work[:, 0:128] = aug[rows, rows]
    work[:, 128:256] = jnp.where(small, 1.0, 0.0).astype(F32)
    factor_leaf(work)
    right = slice(b * 128, n + b * 128 + 128)
    solved = lax.dot_general(
        work[:, 128:256],
        aug[rows, right],
        (((1,), (0,)), ((), ())),
        precision=HIGHEST,
        preferred_element_type=F32,
    )
    aug[rows, right] = solved
    aug[rows, rows] = work[:, 0:128]
    if b < 3:
        below = slice(b * 128 + 128, n)
        aug[below, right] = aug[below, right] - lax.dot_general(
            solved[:, 128 : n - b * 128],
            solved,
            (((0,), (0,)), ((), ())),
            precision=HIGHEST,
            preferred_element_type=F32,
        )


def last_step_kernel(in_ref, lower_ref, inverse_ref, aug, work):
    factor_step(3, in_ref, aug, work)
    n = aug.shape[0]
    row = lax.broadcasted_iota(jnp.int32, (n, n), 0)
    col = lax.broadcasted_iota(jnp.int32, (n, n), 1)
    lower_ref[...] = jnp.where(row >= col, jnp.transpose(aug[:, 0:n]), 0.0)
    inverse_ref[...] = aug[:, n : 2 * n]


def factor_block(b, value):
    n = value.shape[0]
    vmem = pl.BlockSpec(memory_space=pltpu.VMEM)
    work = pltpu.VMEM((128, 256), F32)
    square = jax.ShapeDtypeStruct((n, n), F32)
    if b == 3:
        body, shape, specs = last_step_kernel, (square, square), (vmem, vmem)
        scratch = [pltpu.VMEM((n, 2 * n), F32), work]
    else:
        body = lambda i, o, w: factor_step(b, i, o, w)
        shape, specs, scratch = jax.ShapeDtypeStruct((n, 2 * n), F32), vmem, [work]
    return pl.pallas_call(
        body,
        out_shape=shape,
        in_specs=[vmem],
        out_specs=specs,
        scratch_shapes=scratch,
        compiler_params=pltpu.CompilerParams(vmem_limit_bytes=16 << 20),
        cost_estimate=pl.CostEstimate(flops=7_000_000_000, bytes_accessed=1000, transcendentals=0),
        name="factor_%d" % b,
    )(value)


def dot_t(a, b, precision):
    return lax.dot_general(
        a, b, (((1,), (1,)), ((), ())), precision=precision, preferred_element_type=F32
    )


def write_pieces(where_ref, pieces, solved_ref, factor_ref, product_ref, sems):
    copies = []
    for i, piece in enumerate(pieces):
        rows = piece.shape[0]
        at = pl.multiple_of(where_ref[i], 64)
        copy = pltpu.make_async_copy(piece, factor_ref.at[pl.ds(at, rows), :], sems.at[i])
        copy.start()
        copies.append(copy)
    n = solved_ref.shape[1]
    high, low = split(solved_ref[...])
    solved = jnp.concatenate([high, low], 1)
    for i, piece in enumerate(pieces):
        rows = piece.shape[0]
        at = pl.multiple_of(where_ref[i], 64)
        piece_high, piece_low = split(piece[...])
        total = jnp.dot(piece_high, solved, preferred_element_type=F32)
        total = total[:, :n] + total[:, n:]
        product_ref[pl.ds(at, rows), :] = total + jnp.dot(piece_low, high, preferred_element_type=F32)
    return copies


def own_output_kernel(where_ref, *refs):
    pieces, (solved_ref, factor_ref, product_ref, sems) = refs[:-4], refs[-4:]
    for copy in write_pieces(where_ref, pieces, solved_ref, factor_ref, product_ref, sems):
        copy.wait()


def output_kernel(where_ref, *refs):
    n_pieces = len(refs) - 11
    pieces = refs[:n_pieces]
    lower_ref, solved_ref, pheno_ref, _, _, factor_ref, product_ref, white_ref = refs[n_pieces : n_pieces + 8]
    pheno, sems, one_sem = refs[n_pieces + 8 :]
    tile = where_ref[n_pieces]
    fetch = pltpu.make_async_copy(pheno_ref, pheno, one_sem)
    fetch.start()
    copies = write_pieces(where_ref, pieces, solved_ref, factor_ref, product_ref, sems)
    fetch.wait()
    white_ref[...] = pheno[...] - jnp.transpose(product_ref[...])
    for copy in copies:
        copy.wait()
    for panel in range(2):

        @pl.when(tile == panel)
        def _():
            own = slice(panel * BLK, panel * BLK + BLK)
            head = pltpu.make_async_copy(lower_ref.at[own, :], factor_ref.at[0:BLK, :], one_sem)
            head.start()
            white_ref[:, 0:BLK] = jnp.transpose(solved_ref[own, :])
            head.wait()


def write_outputs(pieces, lower, solved, pheno):
    n_pheno, rows = pheno.shape
    own, others = pieces[::2], pieces[1::2]
    smem = pl.BlockSpec(memory_space=pltpu.SMEM)
    vmem = pl.BlockSpec(memory_space=pltpu.VMEM)
    anywhere = pl.BlockSpec(memory_space=pl.ANY)
    full = jax.ShapeDtypeStruct((rows, 2 * BLK), F32)
    tall = jax.ShapeDtypeStruct((rows, n_pheno), F32)
    params = pltpu.CompilerParams(vmem_limit_bytes=12 << 20)
    cost = pl.CostEstimate(flops=250_000_000, bytes_accessed=5 << 20, transcendentals=0)
    factor, product = pl.pallas_call(
        own_output_kernel,
        out_shape=(full, tall),
        in_specs=[smem] + [vmem] * (len(own) + 1),
        out_specs=(anywhere, vmem),
        scratch_shapes=[pltpu.SemaphoreType.DMA((len(own),))],
        compiler_params=params,
        cost_estimate=cost,
        name="write_own",
    )(jnp.stack([at for at, _ in own]).astype(jnp.int32), *[p for _, p in own], solved)
    where = jnp.stack([at for at, _ in others] + [lax.axis_index("tile")]).astype(jnp.int32)
    first = 1 + len(others) + 3
    factor, _, white = pl.pallas_call(
        output_kernel,
        out_shape=(full, tall, jax.ShapeDtypeStruct((n_pheno, rows), F32)),
        in_specs=[smem] + [vmem] * len(others) + [anywhere, vmem, anywhere, anywhere, vmem],
        out_specs=(anywhere, vmem, vmem),
        scratch_shapes=[
            pltpu.VMEM((n_pheno, rows), F32),
            pltpu.SemaphoreType.DMA((len(others),)),
            pltpu.SemaphoreType.DMA,
        ],
        input_output_aliases={first: 0, first + 1: 1},
        compiler_params=params,
        cost_estimate=cost,
        name="write_others",
    )(where, *[p for _, p in others], lower, solved, pheno, factor, product)
    return factor, white


def body(dosages, phenotypes):
    n_tile = lax.axis_size("tile")
    n_snp = lax.axis_size("snp")
    rows, snps = dosages.shape
    width = BLK
    tile_index = lax.axis_index("tile")

    counts = jnp.sum(dosages, axis=0)
    mine, other, counts = spread_panels(dosages[:width], counts.reshape(16, 128))
    flipped = phenotypes.T
    head = flipped[:, :width]
    head = jnp.concatenate([head[:32], head[32:]], 1)

    counts = counts.reshape(snps)
    allele_freq = counts / (2.0 * rows * n_tile)
    spread = jnp.maximum(2.0 * allele_freq * (1.0 - allele_freq), 0.05)
    mean = 2.0 * allele_freq
    weight = (1.0 / (snps * n_snp)) / spread
    diag, panels = standardize_panels(mine, other, mean, weight)

    def product(start, size, later=None):
        right = panels if later is None else tie(panels, later)[0]
        return dot_t(cut(dosages, start, size) - mean, right, HIGH)

    lower, inverse, heads, pieces = sum_and_factor(product, diag, head)
    panel_pheno = jnp.concatenate(
        [
            jnp.concatenate([heads[:32, :width], heads[32:, :width]], 1),
            jnp.concatenate([heads[:32, width:], heads[32:, width:]], 1),
        ],
        0,
    )
    solved = dot_t(inverse, panel_pheno, HIGHEST)
    factor, whitened = write_outputs(pieces, lower, solved, flipped)
    return factor, whitened.T


def solution(mesh):
    placed = (P("tile", "snp"), P("tile", "snp"))
    return jax.shard_map(
        body,
        mesh=mesh,
        in_specs=placed,
        out_specs=(P("tile", None), P("tile", "snp")),
        check_vma=False,
    )
```

```python
import jax
import jax.numpy as jnp
from jax import lax
from jax.experimental import pallas as pl
from jax.experimental.pallas import tpu as pltpu
from jax.sharding import PartitionSpec as P

BLK = 256
HIGHEST = lax.Precision.HIGHEST
HIGH = lax.Precision.HIGH
F32 = jnp.float32

TILES = [(y, x, c) for y in range(2) for x in range(4) for c in range(2)]
SNPS = [(z, y) for z in range(4) for y in range(2)]


def tile_id(y, x, c):
    return (y * 4 + x) * 2 + c


def tile_send(value, target, only=None):
    pairs = [
        (tile_id(*a), tile_id(*target(*a))) for a in TILES if only is None or only(*a)
    ]
    return lax.ppermute(value, "tile", pairs)


SNP_FLIPS = (
    lambda z, y: (z ^ 1, y),
    lambda z, y: (3 - z, y),
    lambda z, y: (z, 1 - y),
)


def snp_exchange(value, dim):
    flip = SNP_FLIPS[dim]
    pairs = []
    for z, y in SNPS:
        z2, y2 = flip(z, y)
        pairs.append((z * 2 + y, z2 * 2 + y2))
    return lax.ppermute(value, "snp", pairs)


def snp_bits():
    index = lax.axis_index("snp")
    z, y = index // 2, index % 2
    return (jnp.where((z == 1) | (z == 2), 1, 0), jnp.where(z >= 2, 1, 0), y)


ORDERS = ((0, 1, 2), (1, 2, 0), (2, 0, 1))


def cut(value, start, size):
    return lax.dynamic_slice_in_dim(value, start, size, 0)


def join(mine, other, bit):
    rows = mine.shape[0]
    return cut(jnp.concatenate([mine, other, mine], 0), bit * rows, 2 * rows)


PART_ROWS = (704, 704, 640)


def halves(parts, stage, bits):
    sent, kept = [], []
    for part, order in zip(parts, ORDERS):
        half = part.shape[0] // 2
        sent.append(cut(part, (1 - bits[order[stage]]) * half, half))
        kept.append(cut(part, bits[order[stage]] * half, half))
    return sent, kept


def exchange_all(values, stage):
    return [snp_exchange(v, order[stage]) for v, order in zip(values, ORDERS)]


def sum_and_factor(product, diag, pheno):
    bits = snp_bits()
    at, starts = 0, []
    for size in PART_ROWS:
        starts.append(at)
        at += size
    got = []
    for start, size, order in zip(starts, PART_ROWS, ORDERS):
        half = size // 2
        term = snp_exchange(diag, order[0])
        sent = product(start + (1 - bits[order[0]]) * half, half)
        sent, term = tie(sent, term)
        diag = diag + term
        if not got:
            diag, pheno = tie(diag, pheno)
        got.append(snp_exchange(sent, order[0]))
    kept = []
    for start, size, order in zip(starts, PART_ROWS, ORDERS):
        half = size // 2
        kept.append(product(start + bits[order[0]] * half, half, diag))
    state, pheno, kept = gather_small(diag, pheno, kept)
    parts = [k + g for k, g in zip(kept, got)]
    for stage in (1, 2):
        sent, kept = halves(parts, stage, bits)
        got = exchange_all(sent, stage)
        state, *got = tie(factor_block(stage - 1, state), *got)
        parts = [k + g for k, g in zip(kept, got)]

    got = exchange_all(parts, 2)
    state, *got = tie(factor_block(2, state), *got)
    parts = [join(p, g, bits[order[2]]) for p, g, order in zip(parts, got, ORDERS)]
    got = exchange_all(parts, 1)
    lower, inverse, *got = tie(*factor_block(3, state), *got)
    parts = [join(p, g, bits[order[1]]) for p, g, order in zip(parts, got, ORDERS)]
    parts = [dot_t(part, inverse, HIGHEST) for part in parts]
    got = exchange_all(parts, 0)
    pieces = []
    for start, size, order, part, other in zip(starts, PART_ROWS, ORDERS, parts, got):
        half = size // 2
        bit = bits[order[0]]
        pieces.append((start + bit * half, part))
        pieces.append((start + (1 - bit) * half, other))
    return lower, inverse, pheno, pieces


def gather_small(diag, pheno, beside):
    beside = list(beside)
    tile = lax.axis_index("tile")
    x = (tile // 2) % 4
    pheno = jnp.where(tile < 2, pheno, jnp.zeros_like(pheno))
    pheno = pheno + tile_send(pheno, lambda y, xx, c: (1 - y, xx, c))
    rows = diag.shape[0]
    for i, (bit, flip) in enumerate(
        (
            (x % 2, lambda y, xx, c: (y, xx ^ 1, c)),
            (x // 2, lambda y, xx, c: (y, 3 - xx, c)),
        )
    ):
        other = tile_send(jnp.concatenate([diag, pheno], 0), flip)
        other, beside[i] = tie(other, beside[i])
        diag = join(diag, other[:rows], bit)
        pheno = pheno + other[rows:]
        rows = 2 * rows
    other = swap_cores(jnp.concatenate([diag, pheno], 0))
    other, beside[2] = tie(other, beside[2])
    core = tile % 2
    return join(diag, other[:rows], core), join(pheno, other[rows:], core), beside


def swap_cores(value):
    return tile_send(value, lambda y, x, c: (y, x, 1 - c))


def tie(*values):
    return lax.optimization_barrier(values)


def spread_panels(head, counts):
    tile = lax.axis_index("tile")
    x = (tile // 2) % 4
    below = tile >= 8
    p = [head[i * 32 : (i + 1) * 32] for i in range(8)]
    at = lambda row, col: lambda y, xx, c: (y, xx) == (row, col)
    to = lambda row, col: lambda y, xx, c: (row, col, c)
    ahead = lambda y, xx, c: (y, (xx + 1) % 4, c)
    back = lambda y, xx, c: (y, (xx + 3) % 4, c)
    root = at(0, 0)

    def go_down(own):
        down = tile_send(own, lambda y, xx, c: (1, xx, c), lambda y, xx, c: y == 0)
        return jnp.where(below, down, own)

    far_a = tile_send(p[4], to(0, 1), root)
    far_b = tile_send(p[5], to(0, 3), root)
    near = tile_send(head[64:128], to(0, 1), root)
    behind = tile_send(head[192:256], to(0, 3), root)
    far_a, far_b, counts = tie(far_a, far_b, counts)
    far_a = tile_send(far_a, to(0, 2), at(0, 1))
    far_b = tile_send(far_b, to(0, 2), at(0, 3))
    counts = counts + swap_cores(counts)
    counts = counts + tile_send(counts, lambda y, xx, c: (1 - y, xx, c))
    near, behind, counts = tie(near, behind, counts)
    own_a = jnp.where(x == 0, p[0], jnp.where(x == 1, near[:32], jnp.where(x == 3, behind[:32], far_a)))
    own_b = jnp.where(x == 0, p[1], jnp.where(x == 1, near[32:], jnp.where(x == 3, behind[32:], far_b)))
    own_a = go_down(own_a)
    counts = counts + tile_send(counts, lambda y, xx, c: (y, xx ^ 1, c))
    counts = counts + tile_send(counts, lambda y, xx, c: (y, 3 - xx, c))
    own_b = go_down(own_b)
    own_a, counts = tie(own_a, counts)
    left_a = tile_send(own_a, ahead)
    right_a = tile_send(own_a, back)
    left_b = tile_send(own_b, ahead)
    right_b = tile_send(own_b, back)
    far_a = tile_send(left_a, ahead)
    far_b = tile_send(right_b, back)
    mine = (own_a, own_b, left_a, right_a, left_b, right_b, far_a, far_b)
    return mine, tuple(swap_cores(piece) for piece in mine), counts


PIECES = ((0, 0), (0, 32), (3, 0), (1, 0), (3, 32), (1, 32), (2, 0), (2, 32))


def split(value):
    high = value.astype(jnp.bfloat16)
    return high, (value - high.astype(F32)).astype(jnp.bfloat16)


NT = (((1,), (1,)), ((), ()))


def dot3(a, b):
    total = lax.dot_general(a[0], b[0], NT, preferred_element_type=F32)
    total = total + lax.dot_general(a[0], b[1], NT, preferred_element_type=F32)
    return total + lax.dot_general(a[1], b[0], NT, preferred_element_type=F32)


def standardize_kernel(where_ref, mean_ref, weight_ref, *refs):
    mine, other = refs[:8], refs[8:16]
    diag_ref, panels_ref, own = refs[16:]
    x = where_ref[0]
    core = where_ref[1]
    mean = mean_ref[...]
    weight = weight_ref[...]
    for i, (turn, offset) in enumerate(PIECES):
        at = ((x + turn) % 4) * 64 + offset
        centered = mine[i][...] - mean
        if turn == 0:
            own[offset : offset + 32, :] = centered
        for panel, value in ((core, centered), (1 - core, other[i][...] - mean)):
            panels_ref[pl.ds(pl.multiple_of(panel * BLK + at, 32), 32), :] = value * weight
    diag_ref[...] = dot3(split(own[...]), split(panels_ref[...]))


def standardize_panels(mine, other, mean, weight):
    n = mean.shape[0]
    tile = lax.axis_index("tile")
    where = jnp.stack([(tile // 2) % 4, tile % 2]).astype(jnp.int32)
    vmem = pl.BlockSpec(memory_space=pltpu.VMEM)
    return pl.pallas_call(
        standardize_kernel,
        out_shape=(
            jax.ShapeDtypeStruct((64, 2 * BLK), F32),
            jax.ShapeDtypeStruct((2 * BLK, n), F32),
        ),
        in_specs=[pl.BlockSpec(memory_space=pltpu.SMEM)] + [vmem] * 18,
        out_specs=(vmem, vmem),
        scratch_shapes=[pltpu.VMEM((64, n), F32)],
        compiler_params=pltpu.CompilerParams(vmem_limit_bytes=16 << 20),
        cost_estimate=pl.CostEstimate(flops=1000, bytes_accessed=1000, transcendentals=0),
        name="standardize_panels",
    )(where, mean.reshape(1, n), weight.reshape(1, n), *mine, *other)


def lane_columns(rows, j):
    return [jnp.broadcast_to(rows[:, j + k : j + k + 1], (8, 128)) for k in range(8)]


def factor_leaf(work):
    sub = lax.broadcasted_iota(jnp.int32, (8, 128), 0)
    current = [work[0:8, 0:128], work[0:8, 128:256]]
    for j in range(0, 128, 8):
        last = j == 120
        columns = lane_columns(current[0], j)
        s = {}
        for k in range(8):
            for m in range(k, 8):
                s[m, k] = jnp.broadcast_to(columns[k][m : m + 1, :], (8, 128))
        if not last:
            following = [work[j + 8 : j + 16, 0:128], work[j + 8 : j + 16, 128:256]]
            below = lane_columns(following[0], j)
        scale, low, coefs = [], {}, []
        rows = ([], [])
        for k in range(8):
            scale.append(lax.rsqrt(s[k, k]))
            for m in range(k + 1, 8):
                low[m, k] = s[m, k] * scale[k]
            for n in range(k + 1, 8):
                for m in range(n, 8):
                    s[m, n] = s[m, n] - low[m, k] * low[n, k]
            for h in range(2):
                row = jnp.broadcast_to(current[h][k : k + 1, :], (8, 128))
                for i in range(k):
                    row = row - low[k, i] * rows[h][i]
                rows[h].append(row * scale[k])
            if not last:
                coef = below[k]
                for i in range(k):
                    coef = coef - coefs[i] * low[k, i]
                coefs.append(coef * scale[k])
                for h in range(2):
                    following[h] = following[h] - coefs[k] * rows[h][k]
        solved = []
        for h in range(2):
            block = rows[h][0]
            for m in range(1, 8):
                block = jnp.where(sub == m, rows[h][m], block)
            solved.append(block)
        both = jnp.concatenate(solved, 1)
        work[j : j + 8, :] = both
        if j < 112:
            update = lax.dot_general(
                solved[0], both, (((0,), (0,)), ((), ())), precision=HIGHEST, preferred_element_type=F32
            )
            work[j + 16 : 128, :] = work[j + 16 : 128, :] - update[j + 16 :, :]
        if not last:
            current = following


def factor_step(b, first_ref, aug, work):
    n = aug.shape[0]
    rows = slice(b * 128, b * 128 + 128)
    if b == 0:
        eye = lax.broadcasted_iota(jnp.int32, (n, n), 0) == lax.broadcasted_iota(jnp.int32, (n, n), 1)
        eye = jnp.where(eye, 1.0, 0.0).astype(F32)
        aug[:, 0:n] = first_ref[...] + eye
        aug[:, n : 2 * n] = eye
    else:
        aug[...] = first_ref[...]
    small = lax.broadcasted_iota(jnp.int32, (128, 128), 0) == lax.broadcasted_iota(
        jnp.int32, (128, 128), 1
    )
    work[:, 0:128] = aug[rows, rows]
    work[:, 128:256] = jnp.where(small, 1.0, 0.0).astype(F32)
    factor_leaf(work)
    right = slice(b * 128, n + b * 128 + 128)
    solved = lax.dot_general(
        work[:, 128:256],
        aug[rows, right],
        (((1,), (0,)), ((), ())),
        precision=HIGHEST,
        preferred_element_type=F32,
    )
    aug[rows, right] = solved
    aug[rows, rows] = work[:, 0:128]
    if b < 3:
        below = slice(b * 128 + 128, n)
        aug[below, right] = aug[below, right] - lax.dot_general(
            solved[:, 128 : n - b * 128],
            solved,
            (((0,), (0,)), ((), ())),
            precision=HIGHEST,
            preferred_element_type=F32,
        )


def last_step_kernel(in_ref, lower_ref, inverse_ref, aug, work):
    factor_step(3, in_ref, aug, work)
    n = aug.shape[0]
    row = lax.broadcasted_iota(jnp.int32, (n, n), 0)
    col = lax.broadcasted_iota(jnp.int32, (n, n), 1)
    lower_ref[...] = jnp.where(row >= col, jnp.transpose(aug[:, 0:n]), 0.0)
    inverse_ref[...] = aug[:, n : 2 * n]


def factor_block(b, value):
    n = value.shape[0]
    vmem = pl.BlockSpec(memory_space=pltpu.VMEM)
    work = pltpu.VMEM((128, 256), F32)
    square = jax.ShapeDtypeStruct((n, n), F32)
    if b == 3:
        body, shape, specs = last_step_kernel, (square, square), (vmem, vmem)
        scratch = [pltpu.VMEM((n, 2 * n), F32), work]
    else:
        body = lambda i, o, w: factor_step(b, i, o, w)
        shape, specs, scratch = jax.ShapeDtypeStruct((n, 2 * n), F32), vmem, [work]
    return pl.pallas_call(
        body,
        out_shape=shape,
        in_specs=[vmem],
        out_specs=specs,
        scratch_shapes=scratch,
        compiler_params=pltpu.CompilerParams(vmem_limit_bytes=16 << 20),
        cost_estimate=pl.CostEstimate(flops=7_000_000_000, bytes_accessed=1000, transcendentals=0),
        name="factor_%d" % b,
    )(value)


def dot_t(a, b, precision):
    return lax.dot_general(
        a, b, (((1,), (1,)), ((), ())), precision=precision, preferred_element_type=F32
    )


def write_pieces(where_ref, pieces, solved_ref, factor_ref, product_ref, sems):
    copies = []
    for i, piece in enumerate(pieces):
        rows = piece.shape[0]
        at = pl.multiple_of(where_ref[i], 32)
        copy = pltpu.make_async_copy(piece, factor_ref.at[pl.ds(at, rows), :], sems.at[i])
        copy.start()
        copies.append(copy)
    n = solved_ref.shape[1]
    high, low = split(solved_ref[...])
    solved = jnp.concatenate([high, low], 1)
    for i, piece in enumerate(pieces):
        rows = piece.shape[0]
        at = pl.multiple_of(where_ref[i], 32)
        piece_high, piece_low = split(piece[...])
        total = jnp.dot(piece_high, solved, preferred_element_type=F32)
        total = total[:, :n] + total[:, n:]
        product_ref[pl.ds(at, rows), :] = total + jnp.dot(piece_low, high, preferred_element_type=F32)
    return copies


def own_output_kernel(where_ref, *refs):
    pieces, (solved_ref, factor_ref, product_ref, sems) = refs[:-4], refs[-4:]
    for copy in write_pieces(where_ref, pieces, solved_ref, factor_ref, product_ref, sems):
        copy.wait()


def output_kernel(where_ref, *refs):
    n_pieces = len(refs) - 11
    pieces = refs[:n_pieces]
    lower_ref, solved_ref, pheno_ref, _, _, factor_ref, product_ref, white_ref = refs[n_pieces : n_pieces + 8]
    pheno, sems, one_sem = refs[n_pieces + 8 :]
    tile = where_ref[n_pieces]
    fetch = pltpu.make_async_copy(pheno_ref, pheno, one_sem)
    fetch.start()
    copies = write_pieces(where_ref, pieces, solved_ref, factor_ref, product_ref, sems)
    fetch.wait()
    white_ref[...] = pheno[...] - jnp.transpose(product_ref[...])
    for copy in copies:
        copy.wait()
    for panel in range(2):

        @pl.when(tile == panel)
        def _():
            own = slice(panel * BLK, panel * BLK + BLK)
            head = pltpu.make_async_copy(lower_ref.at[own, :], factor_ref.at[0:BLK, :], one_sem)
            head.start()
            white_ref[:, 0:BLK] = jnp.transpose(solved_ref[own, :])
            head.wait()


def write_outputs(pieces, lower, solved, pheno):
    n_pheno, rows = pheno.shape
    own, others = pieces[::2], pieces[1::2]
    smem = pl.BlockSpec(memory_space=pltpu.SMEM)
    vmem = pl.BlockSpec(memory_space=pltpu.VMEM)
    anywhere = pl.BlockSpec(memory_space=pl.ANY)
    full = jax.ShapeDtypeStruct((rows, 2 * BLK), F32)
    tall = jax.ShapeDtypeStruct((rows, n_pheno), F32)
    params = pltpu.CompilerParams(vmem_limit_bytes=12 << 20)
    cost = pl.CostEstimate(flops=250_000_000, bytes_accessed=5 << 20, transcendentals=0)
    factor, product = pl.pallas_call(
        own_output_kernel,
        out_shape=(full, tall),
        in_specs=[smem] + [vmem] * (len(own) + 1),
        out_specs=(anywhere, vmem),
        scratch_shapes=[pltpu.SemaphoreType.DMA((len(own),))],
        compiler_params=params,
        cost_estimate=cost,
        name="write_own",
    )(jnp.stack([at for at, _ in own]).astype(jnp.int32), *[p for _, p in own], solved)
    where = jnp.stack([at for at, _ in others] + [lax.axis_index("tile")]).astype(jnp.int32)
    first = 1 + len(others) + 3
    factor, _, white = pl.pallas_call(
        output_kernel,
        out_shape=(full, tall, jax.ShapeDtypeStruct((n_pheno, rows), F32)),
        in_specs=[smem] + [vmem] * len(others) + [anywhere, vmem, anywhere, anywhere, vmem],
        out_specs=(anywhere, vmem, vmem),
        scratch_shapes=[
            pltpu.VMEM((n_pheno, rows), F32),
            pltpu.SemaphoreType.DMA((len(others),)),
            pltpu.SemaphoreType.DMA,
        ],
        input_output_aliases={first: 0, first + 1: 1},
        compiler_params=params,
        cost_estimate=cost,
        name="write_others",
    )(where, *[p for _, p in others], lower, solved, pheno, factor, product)
    return factor, white


def body(dosages, phenotypes):
    n_tile = lax.axis_size("tile")
    n_snp = lax.axis_size("snp")
    rows, snps = dosages.shape
    width = BLK
    tile_index = lax.axis_index("tile")

    counts = jnp.sum(dosages, axis=0)
    mine, other, counts = spread_panels(dosages[:width], counts.reshape(16, 128))
    flipped = phenotypes.T
    head = flipped[:, :width]
    head = jnp.concatenate([head[:32], head[32:]], 1)

    counts = counts.reshape(snps)
    allele_freq = counts / (2.0 * rows * n_tile)
    spread = jnp.maximum(2.0 * allele_freq * (1.0 - allele_freq), 0.05)
    mean = 2.0 * allele_freq
    weight = (1.0 / (snps * n_snp)) / spread
    diag, panels = standardize_panels(mine, other, mean, weight)

    def product(start, size, later=None):
        right = panels if later is None else tie(panels, later)[0]
        return dot_t(cut(dosages, start, size) - mean, right, HIGH)

    lower, inverse, heads, pieces = sum_and_factor(product, diag, head)
    panel_pheno = jnp.concatenate(
        [
            jnp.concatenate([heads[:32, :width], heads[32:, :width]], 1),
            jnp.concatenate([heads[:32, width:], heads[32:, width:]], 1),
        ],
        0,
    )
    solved = dot_t(inverse, panel_pheno, HIGHEST)
    factor, whitened = write_outputs(pieces, lower, solved, flipped)
    return factor, whitened.T


def solution(mesh):
    placed = (P("tile", "snp"), P("tile", "snp"))
    return jax.shard_map(
        body,
        mesh=mesh,
        in_specs=placed,
        out_specs=(P("tile", None), P("tile", "snp")),
        check_vma=False,
    )
```
